32 devices in a mesh: seq: 8 (over y, x, core), dp: 4 (over z).
Axes of the slice: x: 2, y: 2, z: 4, core: 2. Of those that a mesh axis runs over, the one named last changes fastest.
Arguments:
- tokens: bfloat16 [4, 1024, 2048], P('dp', 'seq'), may hold values from -6 to 6
- valid_mask: int32 [4, 1024], P('dp', 'seq'), may hold values from 0 to 1, as said below
- teacher: bfloat16 [4, 1024, 2048], P('dp', 'seq'), may hold values from -6 to 6
- norm_one: bfloat16 [2048], P(('seq', 'dp')), may hold values from 0.5 to 1.5
- proj_gelu: bfloat16 [2048, 2560], P(('seq', 'dp')), may hold values from -0.125 to 0.125
- proj_rec: bfloat16 [2048, 2560], P(('seq', 'dp')), may hold values from -0.125 to 0.125
- conv_taps: bfloat16 [4, 2560], P(None, ('seq', 'dp')), may hold values from -3 to 3
- conv_bias: bfloat16 [2560], P(('seq', 'dp')), may hold values from -3 to 3
- gate_rec_w: bfloat16 [2560, 256], P(('seq', 'dp')), may hold values from -0.375 to 0.375
- gate_rec_b: bfloat16 [2560], P(('seq', 'dp')), may hold values from -4 to 4
- gate_inp_w: bfloat16 [2560, 256], P(('seq', 'dp')), may hold values from -0.375 to 0.375
- gate_inp_b: bfloat16 [2560], P(('seq', 'dp')), may hold values from -4 to 4
- rec_param: bfloat16 [2560], P(('seq', 'dp')), may hold values from 4 to 16
- proj_out: bfloat16 [2560, 2048], P(None, ('seq', 'dp')), may hold values from -0.25 to 0.25
- norm_two: bfloat16 [2048], P(('seq', 'dp')), may hold values from 0.5 to 1.5
- mlp_gate: bfloat16 [2048, 6144], P(('seq', 'dp')), may hold values from -0.125 to 0.125
- mlp_up: bfloat16 [2048, 6144], P(('seq', 'dp')), may hold values from -0.125 to 0.125
- mlp_down: bfloat16 [6144, 2048], P(None, ('seq', 'dp')), may hold values from -0.15625 to 0.15625
Outputs:
- output: bfloat16 [4, 1024, 2048], P('dp', 'seq')
- mean_loss: float32 [], replicated
- grad_tokens: bfloat16 [4, 1024, 2048], P('dp', 'seq')
- grad_norm_one: float32 [2048], P(('seq', 'dp'))
- grad_proj_gelu: float32 [2048, 2560], P(('seq', 'dp'))
- grad_proj_rec: float32 [2048, 2560], P(('seq', 'dp'))
- grad_conv_taps: float32 [4, 2560], P(None, ('seq', 'dp'))
- grad_conv_bias: float32 [2560], P(('seq', 'dp'))
- grad_gate_rec_w: float32 [2560, 256], P(('seq', 'dp'))
- grad_gate_rec_b: float32 [2560], P(('seq', 'dp'))
- grad_gate_inp_w: float32 [2560, 256], P(('seq', 'dp'))
- grad_gate_inp_b: float32 [2560], P(('seq', 'dp'))
- grad_rec_param: float32 [2560], P(('seq', 'dp'))
- grad_proj_out: float32 [2560, 2048], P(None, ('seq', 'dp'))
- grad_norm_two: float32 [2048], P(('seq', 'dp'))
- grad_mlp_gate: float32 [2048, 6144], P(('seq', 'dp'))
- grad_mlp_up: float32 [2048, 6144], P(('seq', 'dp'))
- grad_mlp_down: float32 [6144, 2048], P(None, ('seq', 'dp'))
The draws below stay inside these ranges and needn't reach their ends.
Inputs may be any that keep to these rules, and one draw needn't show every extreme that they name: `valid_mask`: the last token of every sequence has 1.
All inputs are finite; a program needn't handle non-finite values.
Results may differ from the reference program's by a relative error of at most 0.0075.
Values may be sent and summed in bfloat16 or wider, within the bound.
A program may use at most 384 MiB of HBM per device.

```python
import jax
import jax.numpy as jnp
from jax import lax

D = 2048
NB = 10
BW = 256
FF = 6144
CONV = 4
R = 2560
SEQS = 4
LENGTH = 1024


def draw_valid_mask(key, part):
    position = jnp.arange(LENGTH, dtype=jnp.int32)[None, :]
    ticket = jax.random.randint(key, (SEQS, LENGTH), 0, 4 * LENGTH)
    counted = (ticket < LENGTH + 2 * position) | (position == LENGTH - 1)
    return counted.astype(jnp.int32)


def draw_rec_param(key, part):
    upper_rate = 0.01
    lower_rate = 0.1 / LENGTH
    uniform_draw = jax.random.uniform(key, (NB * BW,), jnp.float32)
    decay_rate = lower_rate * jnp.exp(uniform_draw * jnp.log(upper_rate / lower_rate))
    return (-jnp.log(jnp.expm1(decay_rate))).astype(jnp.bfloat16)


def shard_levels(rng, shape, split, low, largest):
    factor_of, own = 1.0, jax.random.fold_in(rng, 6)
    for dim, shards_of in split:
        steps = jnp.exp(jax.random.uniform(jax.random.fold_in(own, dim), (shards_of,), jnp.float32, low / len(split), largest / len(split)))
        factor_of = factor_of * jnp.repeat(steps, shape[dim] // shards_of).reshape([-1 if axis == dim else 1 for axis in range(len(shape))])
    return factor_of


def gaussian(rng, extent, scale, bound, cuts=(), held_as=jnp.bfloat16):
    array = scale * jax.random.normal(rng, extent, jnp.float32)
    if cuts:
        array = array * shard_levels(rng, extent, cuts, -0.22, 0.18)
    return jnp.clip(array, -bound, bound).astype(held_as)


def setup_inputs(seed: int = 0) -> dict:
    key_of = jax.random.split(jax.random.key(seed), 19)
    return {
        "tokens": gaussian(key_of[0], (SEQS, LENGTH, D), 1.0, 6.0, ((0, 4), (1, 8))),
        "valid_mask": draw_valid_mask(jax.random.fold_in(key_of[18], 71), 0),
        "teacher": gaussian(key_of[2], (SEQS, LENGTH, D), 1.0, 6.0, ((0, 4), (1, 8))),
        "norm_one": jnp.clip(1.0 + 0.1 * jax.random.normal(key_of[3], (D,), jnp.float32), 0.5, 1.5).astype(jnp.bfloat16),
        "proj_gelu": gaussian(key_of[4], (D, R), D ** -0.5, 0.125, ((0, 32),)),
        "proj_rec": gaussian(key_of[5], (D, R), D ** -0.5, 0.125, ((0, 32),)),
        "conv_taps": gaussian(key_of[6], (CONV, R), 0.5, 3.0, ((1, 32),)),
        "conv_bias": gaussian(key_of[7], (R,), 0.5, 3.0, ((0, 32),)),
        "gate_rec_w": gaussian(key_of[8], (R, BW), BW ** -0.5, 0.375, ((0, 32),)),
        "gate_rec_b": gaussian(key_of[9], (R,), 1.0, 4.0, ((0, 32),)),
        "gate_inp_w": gaussian(key_of[10], (R, BW), BW ** -0.5, 0.375, ((0, 32),)),
        "gate_inp_b": gaussian(key_of[11], (R,), 1.0, 4.0, ((0, 32),)),
        "rec_param": draw_rec_param(jax.random.fold_in(key_of[18], 71), 0),
        "proj_out": gaussian(key_of[13], (R, D), (R // 4) ** -0.5, 0.25, ((1, 32),)),
        "norm_two": jnp.clip(1.0 + 0.1 * jax.random.normal(key_of[14], (D,), jnp.float32), 0.5, 1.5).astype(jnp.bfloat16),
        "mlp_gate": gaussian(key_of[15], (D, FF), D ** -0.5, 0.125, ((0, 32),)),
        "mlp_up": gaussian(key_of[16], (D, FF), D ** -0.5, 0.125, ((0, 32),)),
        "mlp_down": gaussian(key_of[17], (FF, D), (FF // 4) ** -0.5, 0.15625, ((1, 32),)),
    }


@jax.custom_vjp
def low(v):
    return lax.optimization_barrier(v.astype(jnp.bfloat16)).astype(jnp.float32)

@jax.custom_vjp
def low_back(v):
    return v

def low_keep(v):
    return (low(v), None)

def low_pass(kept, grad):
    return (grad,)

def back_keep(v):
    return (v, None)

def back_low(kept, grad):
    return (low(grad),)
low.defvjp(low_keep, low_pass)
low_back.defvjp(back_keep, back_low)
norm_eps = 1e-06
gate_power = 8.0
floor_square = 0.0001
highest = lax.Precision.HIGHEST

def rms_norm(values, gain_vec):
    return values * lax.rsqrt(lax.optimization_barrier(jnp.mean(values * values, axis=-1, keepdims=True)) + norm_eps) * gain_vec

def gate_terms(gate_rec, gate_inp, conv_val, rec_vals):
    recur_gate = jax.nn.sigmoid(gate_rec)
    admit_gate = jax.nn.sigmoid(gate_inp)
    log_decay = -gate_power * recur_gate * jax.nn.softplus(-rec_vals)
    decays = jnp.exp(log_decay)
    scaler = jnp.sqrt(jnp.maximum(-jnp.expm1(2.0 * log_decay), floor_square))
    return (decays, scaler * admit_gate * conv_val)

def block_mix(values, weight):
    blocks = values.reshape(values.shape[0], NB, BW)
    mixed_blocks = jnp.einsum('tki,kij->tkj', blocks, weight.reshape(NB, BW, BW), precision=highest)
    return mixed_blocks.reshape(values.shape)

def wide_dot(left, right):
    return jnp.dot(left, right, precision=highest, preferred_element_type=jnp.float32)

def layer_forward(inputs, params):
    norm_one, proj_gelu, proj_rec, conv_taps, conv_bias, gate_rec_w, gate_rec_b, gate_inp_w, gate_inp_b, rec_param, proj_out, norm_two, mlp_gate, mlp_up, mlp_down = params
    normed = low(rms_norm(inputs, norm_one))
    gelu_pre = low_back(wide_dot(normed, proj_gelu))
    rec_pre = low_back(wide_dot(normed, proj_rec))
    padded = jnp.concatenate([jnp.zeros((CONV - 1, NB * BW), jnp.float32), rec_pre], axis=0)
    conv_sum = conv_bias + jnp.zeros_like(rec_pre)
    for offset in range(CONV):
        conv_sum = conv_sum + conv_taps[offset] * padded[CONV - 1 - offset:CONV - 1 - offset + LENGTH]
    conv_out = low(conv_sum)
    gate_rec = low_back(block_mix(conv_out, gate_rec_w) + gate_rec_b)
    gate_inp = low_back(block_mix(conv_out, gate_inp_w) + gate_inp_b)
    decays, drives = gate_terms(gate_rec, gate_inp, conv_out, rec_param)

    def advance(carried, step_pair):
        carried = step_pair[0] * carried + step_pair[1]
        return (carried, carried)
    _, states = lax.scan(jax.checkpoint(advance), jnp.zeros((NB * BW,), jnp.float32), (decays, drives))
    mixed = low(jax.nn.gelu(gelu_pre, approximate=True) * states)
    middle = inputs + low_back(wide_dot(mixed, proj_out))
    normed_two = low(rms_norm(middle, norm_two))
    gate_pre = low_back(wide_dot(normed_two, mlp_gate))
    up_pre = low_back(wide_dot(normed_two, mlp_up))
    hidden = low(jax.nn.gelu(gate_pre, approximate=True) * up_pre)
    return middle + low_back(wide_dot(hidden, mlp_down))

def reference(tokens, valid_mask, teacher, norm_one, proj_gelu, proj_rec, conv_taps, conv_bias, gate_rec_w, gate_rec_b, gate_inp_w, gate_inp_b, rec_param, proj_out, norm_two, mlp_gate, mlp_up, mlp_down):
    params = tuple((param_arr.astype(jnp.float32) for param_arr in (norm_one, proj_gelu, proj_rec, conv_taps, conv_bias, gate_rec_w, gate_rec_b, gate_inp_w, gate_inp_b, rec_param, proj_out, norm_two, mlp_gate, mlp_up, mlp_down)))
    valid_count = jnp.sum(valid_mask).astype(jnp.float32)
    tok_weight = valid_mask.astype(jnp.float32) * (SEQS * LENGTH) / valid_count

    def one_sequence(carried, seq_item):
        grad_sums, loss_sum = carried
        seq_in, seq_weight, seq_target = seq_item

        def objective(seq_x, seq_params):
            result = layer_forward(seq_x, seq_params)
            differ = result - seq_target
            return (result, 0.5 * jnp.sum(seq_weight[:, None] * differ * differ))
        (result, partial_loss), pull_back = jax.vjp(objective, seq_in, params)
        grad_in, grad_params = pull_back((jnp.zeros_like(result), jnp.ones((), jnp.float32)))
        grad_sums = jax.tree.map(jnp.add, grad_sums, grad_params)
        return ((grad_sums, loss_sum + partial_loss), (result.astype(jnp.bfloat16), grad_in.astype(jnp.bfloat16)))
    initial = (tuple((jnp.zeros(param_arr.shape, jnp.float32) for param_arr in params)), jnp.zeros((), jnp.float32))
    (grad_sums, loss_sum), (output, grad_tokens) = lax.scan(one_sequence, initial, (tokens.astype(jnp.float32), tok_weight, teacher.astype(jnp.float32)))
    mean_loss = loss_sum / (SEQS * LENGTH * D)
    return (output, mean_loss, grad_tokens, grad_sums[0], grad_sums[1], grad_sums[2], grad_sums[3], grad_sums[4], grad_sums[5], grad_sums[6], grad_sums[7], grad_sums[8], grad_sums[9], grad_sums[10], grad_sums[11], grad_sums[12], grad_sums[13], grad_sums[14])
```

```python
import functools
import itertools

import jax
import jax.numpy as jnp
from jax import lax
from jax.experimental import pallas as pl
from jax.experimental.pallas import tpu as pltpu
from jax.sharding import PartitionSpec as P

NB = 10
BW = 256
CONV = 4
LANES = 128

norm_eps = 1e-06
gate_power = 8.0
floor_square = 0.0001

fp32 = jnp.float32
half = jnp.bfloat16


def flip(index, mask):
    return index + mask - 2 * mask * ((index // mask) % 2)


def bit_values(bits):
    return [(lax.axis_index(axis) // mask) % 2 for axis, mask, _ in bits]


def slot_number(bits, vals, flipped):
    total = 0
    for place, (_, _, weight) in enumerate(bits):
        total = total + weight * (1 - vals[place] if place in flipped else vals[place])
    return total


def partner(bit):
    axis, mask, _ = bit
    return {axis: flip(lax.axis_index(axis), mask)}


def greet(bits):
    barrier = pltpu.get_barrier_semaphore()
    for bit in bits:
        pl.semaphore_signal(
            barrier, inc=1, device_id=partner(bit), device_id_type=pl.DeviceIdType.MESH
        )
    pl.semaphore_wait(barrier, len(bits))


def masks_of(size):
    return [2**place for place in reversed(range(size.bit_length() - 1))]


def plane_bits():
    return tuple(("seq", mask, mask) for mask in masks_of(lax.axis_size("seq")))


def pair_count():
    return 2 if lax.axis_size("dp") > 1 and 2 * lax.axis_size("seq") <= 16 else 1


def cube_bits():
    pair = (("dp", 1, lax.axis_size("seq")),) if pair_count() == 2 else ()
    return (*pair, *plane_bits())


def world_bits():
    dps = lax.axis_size("dp")
    return tuple(("dp", mask, mask) for mask in masks_of(dps)) + tuple(
        ("seq", mask, mask * dps) for mask in masks_of(lax.axis_size("seq"))
    )


def subsets(items):
    for size in range(len(items) + 1):
        yield from itertools.combinations(items, size)


def splits(width, count):
    tiles = width // LANES
    if tiles * LANES != width or tiles < count:
        return [(0, width)]
    cuts = [tiles * i // count * LANES for i in range(count + 1)]
    return [(cuts[i], cuts[i + 1] - cuts[i]) for i in range(count)]


def rotations(bits, width):
    slow, last = list(range(len(bits) - 1)), [len(bits) - 1]
    pieces = splits(width, len(slow))
    return [
        (first, size, tuple(slow[turn:] + slow[:turn] + last))
        for turn, (first, size) in enumerate(pieces)
    ]


class Gathering:
    def __init__(self, bits, width, x_ref, o_ref, sems):
        self.bits, self.x_ref, self.o_ref = bits, x_ref, o_ref
        self.send_sems, self.recv_sems, self.local_sem = sems
        self.vals = bit_values(bits)
        self.parts = rotations(bits, width)
        self.numbers = {}
        for which in range(len(self.parts)):
            for stage in range(len(bits)):
                for held in subsets(range(stage)):
                    self.numbers[which, stage, held] = len(self.numbers)

    @staticmethod
    def semaphores(bits, width):
        copies = len(rotations(bits, width)) * (2 ** len(bits) - 1)
        return [
            pltpu.SemaphoreType.DMA((copies,)),
            pltpu.SemaphoreType.DMA((copies,)),
            pltpu.SemaphoreType.DMA,
        ]

    def own(self):
        slot = slot_number(self.bits, self.vals, ())
        return pltpu.make_async_copy(self.x_ref, self.o_ref.at[slot], self.local_sem)

    def transfer(self, which, stage, held):
        first, width, order = self.parts[which]
        cols = pl.ds(first, width)
        slot = slot_number(self.bits, self.vals, [order[place] for place in held])
        dst = self.o_ref.at[slot, :, cols]
        number = self.numbers[which, stage, held]
        return pltpu.make_async_remote_copy(
            src_ref=dst if held else self.x_ref.at[:, cols],
            dst_ref=dst,
            send_sem=self.send_sems.at[number],
            recv_sem=self.recv_sems.at[number],
            device_id=partner(self.bits[order[stage]]),
            device_id_type=pl.DeviceIdType.MESH,
        )

    def begin(self):
        self.own().start()
        for stage in range(len(self.bits)):
            for which in range(len(self.parts)):
                self.transfer(which, stage, ()).start()

    def level(self, size):
        depth = len(self.bits)
        for held in itertools.combinations(range(depth), size):
            for which in range(len(self.parts)):
                self.transfer(which, held[-1], held[:-1]).wait_recv()
                for stage in range(held[-1] + 1, depth):
                    self.transfer(which, stage, held).start()

    def finish(self):
        for key in self.numbers:
            self.transfer(*key).wait_send()
        self.own().wait()


class Scattering:
    def __init__(self, bits, x_ref, o_ref, scratch):
        self.bits, self.x_ref, self.o_ref = bits, x_ref, o_ref
        self.held, self.outgoing, self.incoming, self.load, self.send, self.recv = scratch
        self.rows, width = o_ref.shape
        self.chunk = 32 if self.rows % 32 == 0 else 16
        self.parts = [(at, size, order[::-1]) for at, size, order in rotations(bits, width)]
        self.vals = bit_values(bits)
        self.depth = len(bits)
        first_bit = self.parts[0][2][0]
        self.blocks = sorted(subsets(range(self.depth)), key=lambda s: (first_bit not in s, -len(s)))
        self.slots, self.numbers = {}, {}
        for stage in range(self.depth):
            for rest in subsets(range(stage + 1, self.depth)):
                self.slots[stage, rest] = len(self.slots)
        for which in range(len(self.parts)):
            for key in self.slots:
                self.numbers[(which, *key)] = len(self.numbers)
        self.loaded = set()

    @staticmethod
    def scratch(bits, value, wire):
        count, rows, width = value.shape
        copies = len(rotations(bits, width)) * (count - 1)
        return [
            pltpu.VMEM((count, rows, width), value.dtype),
            pltpu.VMEM((count - 1, rows, width), wire),
            pltpu.VMEM((count - 1, rows, width), wire),
            pltpu.SemaphoreType.DMA((count,)),
            pltpu.SemaphoreType.DMA((copies,)),
            pltpu.SemaphoreType.DMA((copies,)),
        ]

    def loading(self, members):
        key = sum(2**place for place in members)
        slot = slot_number(self.bits, self.vals, members)
        return pltpu.make_async_copy(self.x_ref.at[slot], self.held.at[key], self.load.at[key])

    def begin(self):
        for members in self.blocks:
            self.loading(members).start()

    def ready(self, members):
        key = sum(2**place for place in members)
        if key not in self.loaded:
            self.loaded.add(key)
            self.loading(members).wait()
        return key

    def transfer(self, which, stage, rest):
        first, width, order = self.parts[which]
        place = self.slots[stage, rest]
        number = self.numbers[which, stage, rest]
        return pltpu.make_async_remote_copy(
            src_ref=self.outgoing.at[place, :, pl.ds(first, width)],
            dst_ref=self.incoming.at[place, :, pl.ds(first, width)],
            send_sem=self.send.at[number],
            recv_sem=self.recv.at[number],
            device_id=partner(self.bits[order[stage]]),
            device_id_type=pl.DeviceIdType.MESH,
        )

    def add_up(self, which, key, arrived, store):
        first, width, _ = self.parts[which]
        cols = pl.ds(first, width)

        def body(step, carry):
            lines = pl.ds(pl.multiple_of(step * self.chunk, self.chunk), self.chunk)
            total = self.held[key, lines, cols].astype(fp32)
            for place in arrived:
                total = total + self.incoming[place, lines, cols].astype(fp32)
            store(lines, cols, total)
            return carry

        lax.fori_loop(0, self.rows // self.chunk, body, 0)

    def stage(self, stage):
        for rest in sorted(subsets(range(stage + 1, self.depth)), key=lambda s: (-len(s), s)):
            for which, (_, _, order) in enumerate(self.parts):
                going = (stage, *rest)
                key = self.ready([order[place] for place in going])
                for earlier in range(stage):
                    self.transfer(which, earlier, going).wait_recv()
                place = self.slots[stage, rest]

                def keep(lines, cols, total, place=place):
                    self.outgoing[place, lines, cols] = total.astype(self.outgoing.dtype)

                arrived = [self.slots[earlier, going] for earlier in range(stage)]
                self.add_up(which, key, arrived, keep)
                self.transfer(which, stage, rest).start()

    def finish(self):
        def keep(lines, cols, total):
            self.o_ref[lines, cols] = total

        key = self.ready(())
        for which in range(len(self.parts)):
            for stage in range(self.depth):
                self.transfer(which, stage, ()).wait_recv()
            self.add_up(which, key, [self.slots[stage, ()] for stage in range(self.depth)], keep)

    def close(self):
        for members in self.blocks:
            self.ready(members)
        for key in self.numbers:
            self.transfer(*key).wait_send()


def gather(value, bits, number):
    rows, width = value.shape

    def kernel(x_ref, o_ref, *sems):
        work = Gathering(bits, width, x_ref, o_ref, sems)
        greet(bits)
        work.begin()
        for size in range(1, len(bits) + 1):
            work.level(size)
        work.finish()

    return pl.pallas_call(
        kernel,
        out_shape=jax.ShapeDtypeStruct((2 ** len(bits), rows, width), value.dtype),
        in_specs=[pl.BlockSpec(memory_space=pltpu.VMEM)],
        out_specs=pl.BlockSpec(memory_space=pl.ANY),
        scratch_shapes=Gathering.semaphores(bits, width),
        compiler_params=pltpu.CompilerParams(collective_id=number, has_side_effects=True),
        name=f"gather_{number}",
    )(value)


def scatter_sum(value, bits, number, wire=half):
    _, rows, width = value.shape

    def kernel(x_ref, o_ref, *scratch):
        work = Scattering(bits, x_ref, o_ref, scratch)
        work.begin()
        greet(bits)
        for stage in range(len(bits)):
            work.stage(stage)
        work.finish()
        work.close()

    return pl.pallas_call(
        kernel,
        out_shape=jax.ShapeDtypeStruct((rows, width), fp32),
        in_specs=[pl.BlockSpec(memory_space=pl.ANY)],
        out_specs=pl.BlockSpec(memory_space=pltpu.VMEM),
        scratch_shapes=Scattering.scratch(bits, value, wire),
        compiler_params=pltpu.CompilerParams(
            collective_id=number, has_side_effects=True, vmem_limit_bytes=60 * 2**20
        ),
        name=f"scatter_{number}",
    )(value)


def greet_all(axes):
    barrier = pltpu.get_barrier_semaphore()
    total = 0
    for axis in axes:
        count = lax.axis_size(axis)
        for step in range(1, count):
            pl.semaphore_signal(
                barrier,
                inc=1,
                device_id={axis: lax.rem(lax.axis_index(axis) + step, count)},
                device_id_type=pl.DeviceIdType.MESH,
            )
        total += count - 1
    pl.semaphore_wait(barrier, total)


def remote(src, dst, send_sem, recv_sem, device):
    return pltpu.make_async_remote_copy(
        src_ref=src,
        dst_ref=dst,
        send_sem=send_sem,
        recv_sem=recv_sem,
        device_id=device,
        device_id_type=pl.DeviceIdType.MESH,
    )


class Exchange:
    def __init__(self, pay, place, sems):
        self.pay, self.place = pay, place
        self.send, self.recv, self.local = sems
        self.me, self.count = lax.axis_index("seq"), lax.axis_size("seq")

    @staticmethod
    def semaphores(count):
        return [
            pltpu.SemaphoreType.DMA((count,)),
            pltpu.SemaphoreType.DMA((count,)),
            pltpu.SemaphoreType.DMA,
        ]

    def own(self):
        return pltpu.make_async_copy(self.pay.at[self.me], self.place(self.me), self.local)

    def going(self, step):
        to = lax.rem(self.me + step, self.count)
        return remote(
            self.pay.at[to],
            self.place(self.me),
            self.send.at[step],
            self.recv.at[step],
            {"seq": to},
        )

    def source(self, step):
        return lax.rem(self.me - step + self.count, self.count)

    def arriving(self, step):
        block = self.place(self.source(step))
        return remote(block, block, self.send.at[step], self.recv.at[step], {"seq": self.me})


def opening(pay_in, pay_out, pay_mlp, package, tokens, number):
    seqs, dps = lax.axis_size("seq"), lax.axis_size("dp")
    plane, world = plane_bits(), world_bits()
    pays = [pay_in, pay_out]
    rows = pay_in.shape[1]
    relays = 2 * len(pays)
    x_sems = len(Exchange.semaphores(seqs))

    def kernel(*refs):
        pay_refs, refs = refs[:2], refs[2:]
        mlp_ref, package_ref, tokens_ref, refs = refs[0], refs[1], refs[2], refs[3:]
        full_refs, refs = refs[:2], refs[2:]
        mlp_all, shared_all, tokens_all, refs = refs[0], refs[1], refs[2], refs[3:]
        exchange_sems = [refs[x_sems * i : x_sems * (i + 1)] for i in range(3)]
        refs = refs[3 * x_sems :]
        line_send, line_recv, refs = refs[0], refs[1], refs[2:]
        me_d = lax.axis_index("dp")

        def slot(full):
            return lambda source: full.at[source, me_d]

        moves = [Exchange(pay, slot(full), sems) for pay, full, sems in zip(pay_refs, full_refs, exchange_sems)]
        mlp_move = Exchange(mlp_ref, lambda source: mlp_all.at[source], exchange_sems[2])
        shared = Gathering(world, package.shape[1], package_ref, shared_all, refs[:3])
        toks = Gathering(plane, tokens.shape[1], tokens_ref, tokens_all, refs[3:6])

        greet_all(("seq", "dp"))
        for move in moves:
            move.own().start()
        for step in range(1, seqs):
            for move in moves:
                move.going(step).start()
        shared.begin()
        toks.begin()
        mlp_move.own().start()
        for step in range(1, seqs):
            mlp_move.going(step).start()

        def line_copy(way, which, hop, step):
            sign = 1 if way == 0 else -1
            origin = jnp.clip(me_d - sign * hop, 0, dps - 1)
            block = full_refs[which].at[moves[which].source(step), origin]
            return remote(
                block,
                block,
                line_send.at[2 * which + way, hop, step],
                line_recv.at[2 * which + way, hop, step],
                {"dp": jnp.clip(me_d + sign, 0, dps - 1)},
            )

        def has_next(way):
            return me_d < dps - 1 if way == 0 else me_d > 0

        def has_origin(way, hop):
            return me_d >= hop if way == 0 else me_d < dps - hop

        def pass_on(hop, step):
            for which in range(2):
                for way in range(2):

                    @pl.when(has_next(way) & has_origin(way, hop))
                    def _():
                        line_copy(way, which, hop, step).start()

        def incoming_line(way, which, hop, step):
            sign = 1 if way == 0 else -1
            origin = jnp.clip(me_d - sign * hop, 0, dps - 1)
            block = full_refs[which].at[moves[which].source(step), origin]
            return remote(
                block,
                block,
                line_send.at[2 * which + way, hop - 1, step],
                line_recv.at[2 * which + way, hop - 1, step],
                {"dp": jnp.clip(me_d + sign, 0, dps - 1)},
            )

        for which in range(2):
            moves[which].own().wait()
        pass_on(0, 0)

        def first_round(step, carry):
            for move in moves:
                move.arriving(step).wait_recv()
            pass_on(0, step)
            return carry

        lax.fori_loop(1, seqs, first_round, 0)
        world_levels, plane_levels = len(world), len(plane)
        for size in range(1, world_levels + 1):
            shared.level(size)
        for hop in range(1, dps):

            def round_of(step, carry, hop=hop):
                for which in range(2):
                    for way in range(2):

                        @pl.when(has_origin(way, hop))
                        def _():
                            incoming_line(way, which, hop, step).wait_recv()

                if hop < dps - 1:
                    pass_on(hop, step)
                return carry

            lax.fori_loop(0, seqs, round_of, 0)
            if hop == 1:
                for size in range(1, plane_levels + 1):
                    toks.level(size)

        def last_round(step, carry):
            for move in [*moves, mlp_move]:
                move.going(step).wait_send()
            mlp_move.arriving(step).wait_recv()
            return carry

        lax.fori_loop(1, seqs, last_round, 0)
        mlp_move.own().wait()

        def close_round(step, carry):
            for hop in range(dps - 1):
                for which in range(2):
                    for way in range(2):

                        @pl.when(has_next(way) & has_origin(way, hop))
                        def _():
                            line_copy(way, which, hop, step).wait_send()

            return carry

        lax.fori_loop(0, seqs, close_round, 0)
        shared.finish()
        toks.finish()

    vmem, anywhere = pl.BlockSpec(memory_space=pltpu.VMEM), pl.BlockSpec(memory_space=pl.ANY)
    return pl.pallas_call(
        kernel,
        out_shape=[
            *(jax.ShapeDtypeStruct((seqs, dps, rows, pay.shape[2]), half) for pay in pays),
            jax.ShapeDtypeStruct(pay_mlp.shape, half),
            jax.ShapeDtypeStruct((seqs * dps, *package.shape), half),
            jax.ShapeDtypeStruct((seqs, *tokens.shape), half),
        ],
        in_specs=[vmem] * 5,
        out_specs=[anywhere] * 5,
        scratch_shapes=[
            *(Exchange.semaphores(seqs) * 3),
            pltpu.SemaphoreType.DMA((relays, max(dps - 1, 1), seqs)),
            pltpu.SemaphoreType.DMA((relays, max(dps - 1, 1), seqs)),
            *Gathering.semaphores(world, package.shape[1]),
            *Gathering.semaphores(plane, tokens.shape[1]),
        ],
        compiler_params=pltpu.CompilerParams(
            collective_id=number, has_side_effects=True, vmem_limit_bytes=40 * 2**20
        ),
        name="opening",
    )(pay_in, pay_out, pay_mlp, package, tokens)


def closing(in_part, grad_in, grad_out, mlp, mats, small, number):
    seqs, dps = lax.axis_size("seq"), lax.axis_size("dp")
    plane, world = plane_bits(), world_bits()
    grads = [grad_in, grad_out]
    rows = grad_in.shape[2]
    widths = [grad.shape[3] for grad in grads]
    links = max(dps - 1, 1)
    x_sems = len(Exchange.semaphores(seqs))
    jobs = [(plane, in_part, half), (world, small, fp32), (world, mats, half)]
    s_count = len(Scattering.scratch(plane, in_part, half))

    def kernel(*refs):
        part_ref, grad_refs, mlp_ref, mats_ref, small_ref = refs[0], refs[1:3], refs[3], refs[4], refs[5]
        part_out, back_refs, mlp_out, mats_out, small_out = refs[6], refs[7:9], refs[9], refs[10], refs[11]
        refs = refs[12:]
        works = []
        for (bits, _, _), x_ref, o_ref in zip(
            jobs, (part_ref, small_ref, mats_ref), (part_out, small_out, mats_out)
        ):
            works.append(Scattering(bits, x_ref, o_ref, refs[:s_count]))
            refs = refs[s_count:]
        held, refs = refs[:2], refs[2:]
        outgoing, incoming, totals, refs = refs[:2], refs[2:4], refs[4:6], refs[6:]
        load, line_send, line_recv, refs = refs[0], refs[1], refs[2], refs[3:]
        exchange_sems = [refs[x_sems * i : x_sems * (i + 1)] for i in range(3)]
        me_s, me_d = lax.axis_index("seq"), lax.axis_index("dp")
        moves = [
            Exchange(total, lambda source, back=back: back.at[source], sems)
            for total, back, sems in zip(totals, back_refs, exchange_sems)
        ]
        mlp_move = Exchange(mlp_ref, lambda source: mlp_out.at[source], exchange_sems[2])

        def loading(which, chunk):
            return pltpu.make_async_copy(
                grad_refs[which].at[chunk], held[which].at[chunk], load.at[which, chunk]
            )

        def chunk_of(step):
            return lax.rem(me_s + step, seqs)

        for step in range(seqs):
            for which in range(2):
                loading(which, chunk_of(step)).start()
        for work in works:
            work.begin()
        greet_all(("seq", "dp"))

        def ahead(way):
            return me_d < dps - 1 if way == 0 else me_d > 0

        def behind(way):
            return me_d > 0 if way == 0 else me_d < dps - 1

        def target(way, hop):
            sign = 1 if way == 0 else -1
            return jnp.clip(me_d + sign * hop, 0, dps - 1)

        def has_target(way, hop):
            return me_d < dps - hop if way == 0 else me_d >= hop

        def line_copy(way, which, hop, chunk):
            return remote(
                outgoing[which].at[way, hop % 2, chunk],
                incoming[which].at[way, hop - 1, chunk],
                line_send.at[2 * which + way, hop - 1, chunk],
                line_recv.at[2 * which + way, hop - 1, chunk],
                {"dp": target(way, 1)},
            )

        def combine(store, terms):
            def body(step, carry):
                lines = pl.ds(pl.multiple_of(step * 16, 16), 16)
                total = terms[0](lines)
                for term in terms[1:]:
                    total = total + term(lines)
                store(lines, total)
                return carry

            lax.fori_loop(0, rows // 16, body, 0)

        def own_term(which, chunk, block):
            return lambda lines: held[which][chunk, block, lines, :]

        def far_term(which, way, hop, chunk):
            return lambda lines: incoming[which][way, hop - 1, chunk, lines, :].astype(fp32)

        def line_round(hop, first):
            def body(step, carry):
                chunk = chunk_of(step)
                for which in range(2):
                    if first:
                        loading(which, chunk).wait()
                    for way in range(2):
                        if hop + 2 < dps:

                            @pl.when(has_target(way, hop + 2))
                            def _():
                                line_copy(way, which, hop + 2, chunk).wait_send()

                        def send(far, which=which, way=way):
                            def keep(lines, total):
                                outgoing[which][way, hop % 2, chunk, lines, :] = total.astype(half)

                            terms = [own_term(which, chunk, target(way, hop))]
                            if far:
                                line_copy(way, which, hop + 1, chunk).wait_recv()
                                terms.append(far_term(which, way, hop + 1, chunk))
                            combine(keep, terms)
                            line_copy(way, which, hop, chunk).start()

                        if hop == dps - 1:

                            @pl.when(has_target(way, hop))
                            def _():
                                send(False)

                        else:

                            @pl.when(has_target(way, hop) & behind(way))
                            def _():
                                send(True)

                            @pl.when(has_target(way, hop) & jnp.logical_not(behind(way)))
                            def _():
                                send(False)

                return carry

            lax.fori_loop(0, seqs, body, 0)

        def line_total(step, carry):
            chunk = chunk_of(step)
            for which in range(2):
                if dps == 1:
                    loading(which, chunk).wait()

                def keep(lines, total, which=which):
                    totals[which][chunk, lines, :] = total.astype(half)

                mine = own_term(which, chunk, me_d)
                for low, high in ((True, True), (True, False), (False, True), (False, False)):
                    test_low = behind(0) if low else jnp.logical_not(behind(0))
                    test_high = behind(1) if high else jnp.logical_not(behind(1))

                    @pl.when(test_low & test_high)
                    def _():
                        terms = [mine]
                        for way in [way for way, far in ((0, low), (1, high)) if far and dps > 1]:
                            line_copy(way, which, 1, chunk).wait_recv()
                            terms.append(far_term(which, way, 1, chunk))
                        combine(keep, terms)

                @pl.when(step > 0)
                def _():
                    moves[which].going(step).start()

                @pl.when(step == 0)
                def _():
                    moves[which].own().start()

            return carry

        depth = max(len(world), dps - 1)
        for turn in range(depth):
            if turn < dps - 1:
                line_round(dps - 1 - turn, turn == 0)
            if turn == 0:
                mlp_move.own().start()
                for step in range(1, seqs):
                    mlp_move.going(step).start()
            if turn == max(dps - 2, 0):
                lax.fori_loop(0, seqs, line_total, 0)
            for work in works:
                if turn < work.depth:
                    work.stage(turn)
        for work in works:
            work.finish()

        def last_round(step, carry):
            for move in [*moves, mlp_move]:
                move.arriving(step).wait_recv()
                move.going(step).wait_send()
            return carry

        lax.fori_loop(1, seqs, last_round, 0)
        for move in [*moves, mlp_move]:
            move.own().wait()

        def close_round(step, carry):
            for hop in range(1, min(dps, 3)):
                for which in range(2):
                    for way in range(2):

                        @pl.when(has_target(way, hop))
                        def _():
                            line_copy(way, which, hop, step).wait_send()

            return carry

        lax.fori_loop(0, seqs, close_round, 0)
        for work in works:
            work.close()

    vmem, anywhere = pl.BlockSpec(memory_space=pltpu.VMEM), pl.BlockSpec(memory_space=pl.ANY)
    shape = jax.ShapeDtypeStruct
    return pl.pallas_call(
        kernel,
        out_shape=[
            shape(in_part.shape[1:], fp32),
            *(shape((seqs, rows, width), half) for width in widths),
            shape(mlp.shape, half),
            shape(mats.shape[1:], fp32),
            shape(small.shape[1:], fp32),
        ],
        in_specs=[anywhere, anywhere, anywhere, vmem, anywhere, anywhere],
        out_specs=[vmem, anywhere, anywhere, anywhere, vmem, vmem],
        scratch_shapes=[
            *itertools.chain.from_iterable(
                Scattering.scratch(bits, value, wire) for bits, value, wire in jobs
            ),
            *(pltpu.VMEM((seqs, dps, rows, width), fp32) for width in widths),
            *(pltpu.VMEM((2, 2, seqs, rows, width), half) for width in widths),
            *(pltpu.VMEM((2, links, seqs, rows, width), half) for width in widths),
            *(pltpu.VMEM((seqs, rows, width), half) for width in widths),
            pltpu.SemaphoreType.DMA((2, seqs)),
            pltpu.SemaphoreType.DMA((4, links, seqs)),
            pltpu.SemaphoreType.DMA((4, links, seqs)),
            *(Exchange.semaphores(seqs) * 3),
        ],
        compiler_params=pltpu.CompilerParams(
            collective_id=number, has_side_effects=True, vmem_limit_bytes=63 * 2**20
        ),
        name="closing",
    )(in_part, grad_in, grad_out, mlp, mats, small)


STRETCHES = 8


def forward_scan_kernel(decay_ref, drive_ref, state_ref):
    steps, width = decay_ref.shape
    span = steps // STRETCHES

    def lines(step):
        return pl.ds(step, STRETCHES, stride=span)

    def measure(step, carry):
        state, product = carry
        decay = decay_ref[lines(step), :]
        return decay * state + drive_ref[lines(step), :], product * decay

    zero = jnp.zeros((STRETCHES, width), fp32)
    state, product = lax.fori_loop(0, span, measure, (zero, zero + 1.0), unroll=4)
    row = jnp.zeros((1, width), fp32)
    rows = []
    for place in range(STRETCHES):
        rows.append(row)
        row = product[place : place + 1] * row + state[place : place + 1]
    enter = jnp.concatenate(rows, axis=0)

    def run(step, carry):
        carry = decay_ref[lines(step), :] * carry + drive_ref[lines(step), :]
        state_ref[lines(step), :] = carry
        return carry

    lax.fori_loop(0, span, run, enter, unroll=4)


def backward_scan_kernel(decay_ref, grad_ref, adjoint_ref):
    steps, width = decay_ref.shape
    span = steps // STRETCHES

    def lines(step):
        return pl.ds(span - 1 - step, STRETCHES, stride=span)

    def measure(step, carry):
        flow, product = carry
        decay = decay_ref[lines(step), :]
        return decay * (grad_ref[lines(step), :] + flow), product * decay

    zero = jnp.zeros((STRETCHES, width), fp32)
    flow, product = lax.fori_loop(0, span, measure, (zero, zero + 1.0), unroll=4)
    row = jnp.zeros((1, width), fp32)
    rows = []
    for place in reversed(range(STRETCHES)):
        rows.append(row)
        row = product[place : place + 1] * row + flow[place : place + 1]
    enter = jnp.concatenate(rows[::-1], axis=0)

    def run(step, carry):
        adjoint = grad_ref[lines(step), :] + carry
        adjoint_ref[lines(step), :] = adjoint
        return decay_ref[lines(step), :] * adjoint

    lax.fori_loop(0, span, run, enter, unroll=4)


def time_scan(kernel, decays, other):
    steps, width = decays.shape
    padded = -(-width // LANES) * LANES
    wide = ((0, 0), (0, padded - width))
    block = pl.BlockSpec((steps, LANES), lambda place: (0, place))
    out = pl.pallas_call(
        kernel,
        grid=(padded // LANES,),
        out_shape=jax.ShapeDtypeStruct((steps, padded), fp32),
        in_specs=[block, block],
        out_specs=block,
        name=kernel.__name__,
    )(jnp.pad(decays, wide), jnp.pad(other, wide))
    return out[:, :width]


def across(value, axis, mask):
    return lax.ppermute(value, axis, [(i, i ^ mask) for i in range(lax.axis_size(axis))])


def far_masks(axis):
    mask, masks = pair_count(), []
    while mask < lax.axis_size(axis):
        masks.append(mask)
        mask *= 2
    return masks


def place_at(axis, at):
    where, mask = lax.axis_index(axis), 1
    while mask <= at:
        where = flip(where, mask) if at & mask else where
        mask *= 2
    return where


def cube_gather(value, axis):
    low = lax.axis_index(axis) % pair_count()
    mine = lax.dynamic_index_in_dim(value, low, axis=1, keepdims=False)
    pieces = [(0, mine)]
    if pair_count() == 2:
        other = lax.dynamic_index_in_dim(value, 1 - low, axis=1, keepdims=False)
        pieces.append((1, across(other, axis, 1)))
    for mask in far_masks(axis):
        pieces += [(at ^ mask, across(piece, axis, mask)) for at, piece in pieces]
    sources, rows, width = mine.shape
    out = jnp.zeros((sources, lax.axis_size(axis), rows, width), value.dtype)
    for at, piece in pieces:
        out = lax.dynamic_update_slice(out, piece[:, None], (0, place_at(axis, at), 0, 0))
    return out


def cube_scatter(values, axis):
    def block(at):
        where = place_at(axis, at)
        return jnp.concatenate(
            [lax.dynamic_index_in_dim(v, where, axis=1, keepdims=False) for v in values], axis=-1
        )

    held = {at: block(at) for at in range(lax.axis_size(axis))}
    for mask in reversed(far_masks(axis)):
        kept, before = sorted((at for at in held if not at & mask), reverse=True), None
        sums = {}
        for at in kept:
            going = held[at ^ mask].astype(half)
            if before is not None:
                going, before = lax.optimization_barrier((going, before))
                sums[at_before] = (held[at_before], before)
            before, at_before = across(going, axis, mask), at
        sums[at_before] = (held[at_before], before)
        held = {at: own + far.astype(fp32) for at, (own, far) in sums.items()}
    mine = held[0].astype(half)
    if pair_count() == 1:
        return mine[:, None]
    other = across(held[1].astype(half), axis, 1)
    low = lax.axis_index(axis) % 2
    return jnp.stack([jnp.where(low == 0, mine, other), jnp.where(low == 0, other, mine)], axis=1)


def rms_norm(values, gain_vec):
    return (
        values * lax.rsqrt(jnp.mean(values * values, axis=-1, keepdims=True) + norm_eps) * gain_vec
    )


def gate_terms(gate_rec, gate_inp, conv_val, rec_vals):
    recur_gate = jax.nn.sigmoid(gate_rec)
    admit_gate = jax.nn.sigmoid(gate_inp)
    log_decay = -gate_power * recur_gate * jax.nn.softplus(-rec_vals)
    decays = jnp.exp(log_decay)
    scaler = jnp.sqrt(jnp.maximum(-jnp.expm1(2.0 * log_decay), floor_square))
    return (decays, scaler * admit_gate * conv_val)


def contract_rows(left, right):
    return lax.dot_general(left, right, (((0,), (0,)), ((), ())), preferred_element_type=fp32)


def times_trans(left, right):
    return lax.dot_general(left, right, (((1,), (1,)), ((), ())), preferred_element_type=fp32)


def part_of_sum(left, right):
    return times_trans(left, right).astype(half)


def times(left, right):
    return jnp.dot(left, right, preferred_element_type=fp32)


def gelu_product(first, second):
    return jax.nn.gelu(first, approximate=True) * second


def turned(value, shift, axis):
    size = value.shape[axis]
    return lax.dynamic_slice_in_dim(
        jnp.concatenate([value, value], axis=axis), shift, size, axis=axis
    )


def on_device(
    tokens,
    valid_mask,
    teacher,
    norm_one,
    proj_gelu,
    proj_rec,
    conv_taps,
    conv_bias,
    gate_rec_w,
    gate_rec_b,
    gate_inp_w,
    gate_inp_b,
    rec_param,
    proj_out,
    norm_two,
    mlp_gate,
    mlp_up,
    mlp_down,
):
    seqs, dps = lax.axis_size("seq"), lax.axis_size("dp")
    everyone = seqs * dps
    me_seq = lax.axis_index("seq")
    local_len, model = tokens.shape[-2:]
    rec_width = proj_rec.shape[1]
    hidden_width = mlp_gate.shape[1]
    rows_w = proj_rec.shape[0]
    rows_c = gate_rec_w.shape[0]
    steps = seqs * local_len

    plane, cube, pairs = plane_bits(), cube_bits(), pair_count()

    width_r = rec_width // seqs
    span_blocks = max((i * width_r + width_r - 1) // BW - i * width_r // BW for i in range(seqs)) + 1
    span = span_blocks * BW

    def first_block(place):
        return jnp.minimum(place * width_r // BW, NB - span_blocks)

    first = [min(i * width_r // BW, NB - span_blocks) * BW for i in range(seqs)]
    base = first_block(me_seq) * BW
    shift = me_seq * width_r - base

    def rec_columns(place):
        begin, end = first[place], first[place] + span
        own = place * width_r
        return [proj_rec[:, own:end], proj_rec[:, begin:own]]

    pay_in = jnp.stack(
        [
            jnp.concatenate(
                [*rec_columns(i), proj_gelu[:, i * width_r : (i + 1) * width_r]], axis=1
            )
            for i in range(seqs)
        ]
    )
    out_trans = proj_out.T.reshape(rows_w, seqs, width_r).transpose(1, 0, 2)

    def by_slice(value):
        return value.reshape(rows_w, seqs, pairs, -1).transpose(1, 0, 2, 3)

    pay_mlp = jnp.concatenate([by_slice(mlp_gate), by_slice(mlp_up), by_slice(mlp_down.T)], axis=3)
    pay_mlp = pay_mlp.transpose(0, 2, 1, 3)
    cols = hidden_width // (pairs * seqs)

    mask_val = valid_mask.reshape(local_len).astype(fp32)
    own_count = jnp.sum(mask_val)
    count_high = jnp.floor(own_count / 128.0)
    count_pair = jnp.stack([count_high, own_count - 128.0 * count_high]).astype(half)

    def row_of(value):
        return jnp.pad(value, ((0, 0), (0, 2 * BW - value.shape[1])))

    block_rows = -(-rows_c // 16) * 16
    package = jnp.concatenate(
        [
            jnp.pad(
                jnp.concatenate([gate_rec_w, gate_inp_w], axis=1),
                ((0, block_rows - rows_c), (0, 0)),
            ),
            row_of(conv_taps),
            row_of(jnp.stack([conv_bias, gate_rec_b, gate_inp_b, rec_param])),
            row_of(jnp.stack([norm_one, norm_two])),
            row_of(count_pair[None, :]),
            jnp.zeros((5, 2 * BW), half),
        ],
        axis=0,
    )
    w_in, w_out, mlp_own, shared, tokens_all = opening(
        pay_in, out_trans, pay_mlp, package, tokens.reshape(local_len, model), 1
    )
    w_in = w_in.reshape(model, span + width_r)
    w_out = w_out.reshape(model, width_r)
    w_mlp = cube_gather(mlp_own, "dp").reshape(model, 3 * cols)
    w_two, w_down = w_mlp[:, : 2 * cols], w_mlp[:, 2 * cols :]
    blocks_all = shared[:, :rows_c].reshape(rec_width, 2 * BW)
    vectors = shared[:, block_rows:].astype(fp32)
    channel_vecs = vectors[:, : CONV + 4, :rows_c].transpose(1, 0, 2).reshape(CONV + 4, rec_width)
    gains = vectors[:, CONV + 4 : CONV + 6, :rows_w].transpose(1, 0, 2).reshape(2, model)
    counts = jnp.sum(vectors[:, CONV + 6, :2], axis=0)
    valid_total = 128.0 * counts[0] + counts[1]

    span_vecs = turned(
        lax.dynamic_slice(channel_vecs, (0, base), (CONV + 4, span)), shift, axis=1
    )
    tap_vals, bias_vals = span_vecs[:CONV], span_vecs[CONV]
    rec_bias, inp_bias, rec_vals = (span_vecs[CONV + 1 + i, :width_r] for i in range(3))
    span_mats = lax.dynamic_slice(blocks_all, (base, 0), (span, 2 * BW))

    def block_diagonal(value):
        rows = []
        for place in range(span_blocks):
            block = value[place * BW : (place + 1) * BW]
            rows.append(jnp.pad(block, ((0, 0), (place * BW, (span_blocks - 1 - place) * BW))))
        whole = turned(jnp.concatenate(rows, axis=0), shift, axis=0)
        return lax.dynamic_slice(whole, (0, shift), (span, width_r))

    w_gates = jnp.concatenate(
        [block_diagonal(span_mats[:, :BW]), block_diagonal(span_mats[:, BW:])], axis=1
    )
    gain_one, gain_two = gains[0], gains[1]

    flat_in = tokens.reshape(local_len, model).astype(fp32)
    tokens_all = tokens_all.reshape(steps, model).astype(fp32)
    normed_all = rms_norm(tokens_all, gain_one).astype(half)
    pre = times(normed_all, w_in)
    rec_pre, gelu_pre = pre[:, :span], pre[:, span:]
    padded = jnp.concatenate([jnp.zeros((CONV - 1, span), fp32), rec_pre], axis=0)
    conv_sum = bias_vals + jnp.zeros_like(rec_pre)
    for offset in range(CONV):
        conv_sum = conv_sum + tap_vals[offset] * padded[CONV - 1 - offset : CONV - 1 - offset + steps]
    conv_low = conv_sum.astype(half)
    conv_val = conv_low[:, :width_r].astype(fp32)
    gates = times(conv_low, w_gates)
    gate_rec = gates[:, :width_r] + rec_bias
    gate_inp = gates[:, width_r:] + inp_bias
    decays, drives = gate_terms(gate_rec, gate_inp, conv_val, rec_vals)
    states = time_scan(forward_scan_kernel, decays, drives)
    mixed_low = gelu_product(gelu_pre, states).astype(half)
    mixed_part = part_of_sum(mixed_low, w_out).reshape(seqs, local_len, model)
    middle = flat_in + scatter_sum(mixed_part, plane, 3)

    normed_two_low = rms_norm(middle, gain_two).astype(half)
    group = pairs * seqs
    tall = group * local_len
    normed_two_all = gather(normed_two_low, cube, 4).reshape(tall, model)
    pre_two = times(normed_two_all, w_two)
    gate_pre, up_pre = pre_two[:, :cols], pre_two[:, cols:]
    hidden_low = gelu_product(gate_pre, up_pre).astype(half)
    down_part = part_of_sum(hidden_low, w_down).reshape(group, local_len, model)
    result = middle + scatter_sum(down_part, cube, 5)
    differ = result - teacher.reshape(local_len, model).astype(fp32)
    own_loss = 0.5 * jnp.sum(mask_val[:, None] * differ * differ)
    token_total = local_len * everyone
    grad_result = mask_val[:, None] * (token_total / valid_total) * differ
    output = result.reshape(tokens.shape).astype(half)

    down_all = gather(grad_result.astype(half), cube, 6).reshape(tall, model)
    grad_down = contract_rows(down_all, hidden_low)
    grad_hidden = times(down_all, w_down)
    _, pull_mlp = jax.vjp(gelu_product, gate_pre, up_pre)
    two_low = jnp.concatenate(pull_mlp(grad_hidden), axis=1).astype(half)
    grad_two = contract_rows(normed_two_all, two_low)
    two_part = part_of_sum(two_low, w_two).reshape(group, local_len, model)
    grad_normed_two = scatter_sum(two_part, cube, 7)

    grad_normed_two, grad_two, grad_down = lax.optimization_barrier(
        (grad_normed_two, grad_two, grad_down)
    )
    sent_mlp = cube_scatter(
        [
            grad_two.reshape(seqs, dps, rows_w, 2 * cols),
            grad_down.reshape(seqs, dps, rows_w, cols),
        ],
        "dp",
    )
    _, pull_norm_two = jax.vjp(rms_norm, middle, gain_two)
    grad_middle_norm, grad_norm_two = pull_norm_two(grad_normed_two)
    grad_middle = grad_result + grad_middle_norm

    middle_low = gather(grad_middle.astype(half), plane, 8).reshape(steps, model)
    grad_out = contract_rows(middle_low, mixed_low)
    grad_mixed = times(middle_low, w_out)
    _, pull_mix = jax.vjp(gelu_product, gelu_pre, states)
    grad_gelu_pre, grad_states = pull_mix(grad_mixed)
    adjoint = time_scan(backward_scan_kernel, decays, grad_states)
    prior_state = jnp.concatenate([jnp.zeros_like(states[:1]), states[:-1]], axis=0)
    _, pull_gates = jax.vjp(gate_terms, gate_rec, gate_inp, conv_val, rec_vals)
    grad_rec_gate, grad_inp_gate, grad_conv_direct, grad_rec_param = pull_gates(
        (adjoint * prior_state, adjoint)
    )
    gates_low = jnp.concatenate([grad_rec_gate, grad_inp_gate], axis=1).astype(half)
    grad_gate_bias = jnp.sum(gates_low.astype(fp32), axis=0)
    grad_gates = contract_rows(conv_low, gates_low)
    grad_conv = times_trans(gates_low, w_gates) + jnp.pad(
        grad_conv_direct, ((0, 0), (0, span - width_r))
    )
    grad_conv_bias = jnp.sum(grad_conv, axis=0)
    ahead = jnp.concatenate([grad_conv, jnp.zeros((CONV - 1, span), fp32)], axis=0)
    tap_grads = []
    rec_back = jnp.zeros_like(grad_conv)
    for offset in range(CONV):
        window = padded[CONV - 1 - offset : CONV - 1 - offset + steps]
        tap_grads.append(jnp.sum(grad_conv * window, axis=0))
        rec_back = rec_back + tap_vals[offset] * ahead[offset : offset + steps]
    in_low = jnp.concatenate([rec_back.astype(half), grad_gelu_pre.astype(half)], axis=1)
    grad_in = contract_rows(normed_all, in_low)
    in_part = part_of_sum(in_low, w_in).reshape(seqs, local_len, model)
    unit_all = tokens_all * lax.rsqrt(
        jnp.mean(tokens_all * tokens_all, axis=-1, keepdims=True) + norm_eps
    )
    grad_norm_one = jnp.sum(in_part.reshape(steps, model).astype(fp32) * unit_all, axis=0)

    def spread(value):
        return lax.dynamic_update_slice(
            jnp.zeros((value.shape[0], rec_width), fp32), value, (0, base)
        )

    def unturned(value, axis):
        return turned(value, span - shift, axis)

    def diagonal_blocks(value):
        wide = unturned(unturned(jnp.pad(value, ((0, 0), (0, span - width_r))), 1), 0)
        block = lax.broadcasted_iota(jnp.int32, (span, BW), 0) // BW
        picked = wide[:, :BW]
        for i in range(1, span_blocks):
            picked = jnp.where(block == i, wide[:, i * BW : (i + 1) * BW], picked)
        return picked

    mats = jnp.concatenate(
        [diagonal_blocks(grad_gates[:, :width_r]), diagonal_blocks(grad_gates[:, width_r:])], axis=1
    )
    mats = lax.dynamic_update_slice(jnp.zeros((rec_width, 2 * BW), fp32), mats, (base, 0))
    mats = jnp.pad(
        mats.reshape(everyone, rows_c, 2 * BW), ((0, 0), (0, block_rows - rows_c), (0, 0))
    )

    def widen(value):
        return jnp.pad(value[None, :], ((0, 0), (0, span - width_r)))

    lines = jnp.concatenate(
        [
            jnp.stack(tap_grads),
            grad_conv_bias[None, :],
            widen(grad_gate_bias[:width_r]),
            widen(grad_gate_bias[width_r:]),
            widen(grad_rec_param),
        ],
        axis=0,
    )
    lines = spread(unturned(lines, 1)).reshape(CONV + 4, everyone, rows_c).transpose(1, 0, 2)
    gain_lines = jnp.stack([grad_norm_one, grad_norm_two]).reshape(2, everyone, rows_w)
    gain_lines = gain_lines.transpose(1, 0, 2)

    def lane_pad(value):
        return jnp.pad(value, ((0, 0), (0, 0), (0, LANES - value.shape[2])))

    small = jnp.concatenate(
        [
            lane_pad(lines),
            lane_pad(gain_lines),
            jnp.full((everyone, 1, LANES), own_loss),
            jnp.zeros((everyone, 5, LANES), fp32),
        ],
        axis=1,
    )
    grad_normed, back_in, back_out, back_mlp, mats, small = closing(
        in_part,
        grad_in.reshape(seqs, dps, rows_w, span + width_r),
        grad_out.reshape(seqs, dps, rows_w, width_r),
        sent_mlp,
        mats.astype(half),
        small,
        2,
    )
    mean_loss = small[CONV + 6, 0] / (valid_total * model)

    _, pull_norm_one = jax.vjp(lambda values: rms_norm(values, gain_one), flat_in)
    grad_tokens = (grad_middle + pull_norm_one(grad_normed)[0]).reshape(tokens.shape).astype(half)

    def rejoin(value):
        return value.transpose(2, 0, 1, 3).reshape(rows_w, hidden_width)

    out_gate, out_up, out_down = (rejoin(back_mlp[..., i * cols : (i + 1) * cols]) for i in range(3))
    out_gate, out_up = out_gate.astype(fp32), out_up.astype(fp32)
    out_down = out_down.T.astype(fp32)
    back_in = back_in.astype(fp32)
    out_proj_out = back_out.transpose(1, 0, 2).reshape(rows_w, rec_width).T.astype(fp32)
    out_proj_gelu = back_in[:, :, span:].transpose(1, 0, 2).reshape(rows_w, rec_width)
    out_proj_rec = jnp.zeros((rows_w, rec_width), fp32)
    for place in range(seqs):
        begin, end, own = first[place], first[place] + span, place * width_r
        piece = back_in[place]
        piece = jnp.concatenate([piece[:, end - own : span], piece[:, : end - own]], axis=1)
        out_proj_rec = out_proj_rec + jnp.pad(piece, ((0, 0), (begin, rec_width - end)))

    return (
        output,
        mean_loss,
        grad_tokens,
        small[CONV + 4, :rows_w],
        out_proj_gelu,
        out_proj_rec,
        small[:CONV, :rows_c],
        small[CONV, :rows_c],
        mats[:rows_c, :BW],
        small[CONV + 1, :rows_c],
        mats[:rows_c, BW:],
        small[CONV + 2, :rows_c],
        small[CONV + 3, :rows_c],
        out_proj_out,
        small[CONV + 5, :rows_w],
        out_gate,
        out_up,
        out_down,
    )


def solution(mesh):
    both = ("seq", "dp")
    rows, cols, flat = P(both, None), P(None, both), P(both)
    acts = P("dp", "seq", None)
    in_specs = (
        acts,
        P("dp", "seq"),
        acts,
        flat,
        rows,
        rows,
        cols,
        flat,
        rows,
        flat,
        rows,
        flat,
        flat,
        cols,
        flat,
        rows,
        rows,
        cols,
    )
    out_specs = (
        acts,
        P(),
        acts,
        flat,
        rows,
        rows,
        cols,
        flat,
        rows,
        flat,
        rows,
        flat,
        flat,
        cols,
        flat,
        rows,
        rows,
        cols,
    )
    return jax.shard_map(
        on_device, mesh=mesh, in_specs=in_specs, out_specs=out_specs, check_vma=False
    )
```

```python
import functools
import itertools

import jax
import jax.numpy as jnp
from jax import lax
from jax.experimental import pallas as pl
from jax.experimental.pallas import tpu as pltpu
from jax.sharding import PartitionSpec as P

NB = 10
BW = 256
CONV = 4
LANES = 128
MLPS = 3

norm_eps = 1e-06
gate_power = 8.0
floor_square = 0.0001

fp32 = jnp.float32
half = jnp.bfloat16


def flip(index, mask):
    return index + mask - 2 * mask * ((index // mask) % 2)


def bit_values(bits):
    return [(lax.axis_index(axis) // mask) % 2 for axis, mask, _ in bits]


def slot_number(bits, vals, flipped):
    total = 0
    for place, (_, _, weight) in enumerate(bits):
        total = total + weight * (1 - vals[place] if place in flipped else vals[place])
    return total


def partner(bit):
    axis, mask, _ = bit
    return {axis: flip(lax.axis_index(axis), mask)}


def greet(bits):
    barrier = pltpu.get_barrier_semaphore()
    for bit in bits:
        pl.semaphore_signal(
            barrier, inc=1, device_id=partner(bit), device_id_type=pl.DeviceIdType.MESH
        )
    pl.semaphore_wait(barrier, len(bits))


def masks_of(size):
    return [2**place for place in reversed(range(size.bit_length() - 1))]


def plane_bits():
    return tuple(("seq", mask, mask) for mask in masks_of(lax.axis_size("seq")))


def pair_count():
    return 2 if lax.axis_size("dp") > 1 and 2 * lax.axis_size("seq") <= 16 else 1


def cube_bits():
    pair = (("dp", 1, lax.axis_size("seq")),) if pair_count() == 2 else ()
    return (*pair, *plane_bits())


def world_bits():
    dps = lax.axis_size("dp")
    return tuple(("dp", mask, mask) for mask in masks_of(dps)) + tuple(
        ("seq", mask, mask * dps) for mask in masks_of(lax.axis_size("seq"))
    )


def subsets(items):
    for size in range(len(items) + 1):
        yield from itertools.combinations(items, size)


def splits(width, count):
    tiles = width // LANES
    if tiles * LANES != width or tiles < count:
        return [(0, width)]
    cuts = [tiles * i // count * LANES for i in range(count + 1)]
    return [(cuts[i], cuts[i + 1] - cuts[i]) for i in range(count)]


def rotations(bits, width, fixed=0):
    begin, slow, last = list(range(fixed)), list(range(fixed, len(bits) - 1)), [len(bits) - 1]
    pieces = splits(width, len(slow))
    return [
        (first, size, tuple(begin + slow[turn:] + slow[:turn] + last))
        for turn, (first, size) in enumerate(pieces)
    ]


class Gathering:
    def __init__(self, bits, width, x_ref, o_ref, sems, fixed=0):
        self.bits, self.x_ref, self.o_ref = bits, x_ref, o_ref
        self.send_sems, self.recv_sems, self.local_sem = sems
        self.vals = bit_values(bits)
        self.parts = rotations(bits, width, fixed)
        self.numbers = {}
        for which in range(len(self.parts)):
            for stage in range(len(bits)):
                for held in subsets(range(stage)):
                    self.numbers[which, stage, held] = len(self.numbers)

    @staticmethod
    def semaphores(bits, width, fixed=0):
        copies = len(rotations(bits, width, fixed)) * (2 ** len(bits) - 1)
        return [
            pltpu.SemaphoreType.DMA((copies,)),
            pltpu.SemaphoreType.DMA((copies,)),
            pltpu.SemaphoreType.DMA,
        ]

    def own(self):
        slot = slot_number(self.bits, self.vals, ())
        return pltpu.make_async_copy(self.x_ref, self.o_ref.at[slot], self.local_sem)

    def transfer(self, which, stage, held):
        first, width, order = self.parts[which]
        cols = pl.ds(first, width)
        slot = slot_number(self.bits, self.vals, [order[place] for place in held])
        dst = self.o_ref.at[slot, :, cols]
        number = self.numbers[which, stage, held]
        in_place = held or self.x_ref is None
        return pltpu.make_async_remote_copy(
            src_ref=dst if in_place else self.x_ref.at[:, cols],
            dst_ref=dst,
            send_sem=self.send_sems.at[number],
            recv_sem=self.recv_sems.at[number],
            device_id=partner(self.bits[order[stage]]),
            device_id_type=pl.DeviceIdType.MESH,
        )

    def begin(self):
        if self.x_ref is not None:
            self.own().start()
        for stage in range(len(self.bits)):
            for which in range(len(self.parts)):
                self.transfer(which, stage, ()).start()

    def level(self, size):
        depth = len(self.bits)
        for held in itertools.combinations(range(depth), size):
            for which in range(len(self.parts)):
                self.transfer(which, held[-1], held[:-1]).wait_recv()
                for stage in range(held[-1] + 1, depth):
                    self.transfer(which, stage, held).start()

    def finish(self):
        for key in self.numbers:
            self.transfer(*key).wait_send()
        if self.x_ref is not None:
            self.own().wait()


class Fan:
    def __init__(self, source, target, sems):
        self.source, self.target = source, target
        self.send, self.recv = sems
        self.me, self.count = lax.axis_index("dp"), lax.axis_size("dp")

    @staticmethod
    def semaphores(count):
        return [pltpu.SemaphoreType.DMA((count,)), pltpu.SemaphoreType.DMA((count,))]

    def going(self, step):
        to = lax.rem(self.me + step, self.count)
        return remote(
            self.source(to), self.target(self.me), self.send.at[step], self.recv.at[step], {"dp": to}
        )

    def arriving(self, step):
        block = self.target(lax.rem(self.me - step + self.count, self.count))
        return remote(block, block, self.send.at[step], self.recv.at[step], {"dp": self.me})


class Scattering:
    def __init__(self, bits, x_ref, o_ref, scratch, fixed=0):
        self.bits, self.x_ref, self.o_ref = bits, x_ref, o_ref
        self.held, self.outgoing, self.incoming, self.load, self.send, self.recv = scratch
        self.rows, width = o_ref.shape
        self.chunk = 32 if self.rows % 32 == 0 else 16
        self.parts = [(at, size, order[::-1]) for at, size, order in rotations(bits, width, fixed)]
        self.vals = bit_values(bits)
        self.depth = len(bits)
        first_bit = self.parts[0][2][0]
        self.blocks = sorted(subsets(range(self.depth)), key=lambda s: (first_bit not in s, -len(s)))
        self.slots, self.numbers = {}, {}
        for stage in range(self.depth):
            for rest in subsets(range(stage + 1, self.depth)):
                self.slots[stage, rest] = len(self.slots)
        for which in range(len(self.parts)):
            for key in self.slots:
                self.numbers[(which, *key)] = len(self.numbers)
        self.loaded = set()

    @staticmethod
    def scratch(bits, value, wire, fixed=0):
        count, rows, width = value.shape
        copies = len(rotations(bits, width, fixed)) * (count - 1)
        return [
            pltpu.VMEM((count, rows, width), value.dtype),
            pltpu.VMEM((count - 1, rows, width), wire),
            pltpu.VMEM((count - 1, rows, width), wire),
            pltpu.SemaphoreType.DMA((count,)),
            pltpu.SemaphoreType.DMA((copies,)),
            pltpu.SemaphoreType.DMA((copies,)),
        ]

    def loading(self, members):
        key = sum(2**place for place in members)
        slot = slot_number(self.bits, self.vals, members)
        return pltpu.make_async_copy(self.x_ref.at[slot], self.held.at[key], self.load.at[key])

    def begin(self):
        for members in self.blocks:
            self.loading(members).start()

    def ready(self, members):
        key = sum(2**place for place in members)
        if key not in self.loaded:
            self.loaded.add(key)
            self.loading(members).wait()
        return key

    def transfer(self, which, stage, rest):
        first, width, order = self.parts[which]
        place = self.slots[stage, rest]
        number = self.numbers[which, stage, rest]
        return pltpu.make_async_remote_copy(
            src_ref=self.outgoing.at[place, :, pl.ds(first, width)],
            dst_ref=self.incoming.at[place, :, pl.ds(first, width)],
            send_sem=self.send.at[number],
            recv_sem=self.recv.at[number],
            device_id=partner(self.bits[order[stage]]),
            device_id_type=pl.DeviceIdType.MESH,
        )

    def add_up(self, which, key, arrived, store):
        first, width, _ = self.parts[which]
        cols = pl.ds(first, width)

        def body(step, carry):
            lines = pl.ds(pl.multiple_of(step * self.chunk, self.chunk), self.chunk)
            total = self.held[key, lines, cols].astype(fp32)
            for place in arrived:
                total = total + self.incoming[place, lines, cols].astype(fp32)
            store(lines, cols, total)
            return carry

        lax.fori_loop(0, self.rows // self.chunk, body, 0)

    def stage(self, stage):
        for rest in sorted(subsets(range(stage + 1, self.depth)), key=lambda s: (-len(s), s)):
            for which, (_, _, order) in enumerate(self.parts):
                going = (stage, *rest)
                key = self.ready([order[place] for place in going])
                for earlier in range(stage):
                    self.transfer(which, earlier, going).wait_recv()
                place = self.slots[stage, rest]

                def keep(lines, cols, total, place=place):
                    self.outgoing[place, lines, cols] = total.astype(self.outgoing.dtype)

                arrived = [self.slots[earlier, going] for earlier in range(stage)]
                self.add_up(which, key, arrived, keep)
                self.transfer(which, stage, rest).start()

    def finish(self):
        def keep(lines, cols, total):
            self.o_ref[lines, cols] = total

        key = self.ready(())
        for which in range(len(self.parts)):
            for stage in range(self.depth):
                self.transfer(which, stage, ()).wait_recv()
            self.add_up(which, key, [self.slots[stage, ()] for stage in range(self.depth)], keep)

    def close(self):
        for members in self.blocks:
            self.ready(members)
        for key in self.numbers:
            self.transfer(*key).wait_send()


def gather(value, bits, number, fixed=0):
    rows, width = value.shape

    def kernel(x_ref, o_ref, *sems):
        work = Gathering(bits, width, x_ref, o_ref, sems, fixed)
        greet(bits)
        work.begin()
        for size in range(1, len(bits) + 1):
            work.level(size)
        work.finish()

    return pl.pallas_call(
        kernel,
        out_shape=jax.ShapeDtypeStruct((2 ** len(bits), rows, width), value.dtype),
        in_specs=[pl.BlockSpec(memory_space=pltpu.VMEM)],
        out_specs=pl.BlockSpec(memory_space=pl.ANY),
        scratch_shapes=Gathering.semaphores(bits, width, fixed),
        compiler_params=pltpu.CompilerParams(collective_id=number, has_side_effects=True),
        name=f"gather_{number}",
    )(value)


def scatter_sum(value, bits, number, fixed=0):
    _, rows, width = value.shape

    def kernel(x_ref, o_ref, *scratch):
        work = Scattering(bits, x_ref, o_ref, scratch, fixed)
        work.begin()
        greet(bits)
        for stage in range(len(bits)):
            work.stage(stage)
        work.finish()
        work.close()

    return pl.pallas_call(
        kernel,
        out_shape=jax.ShapeDtypeStruct((rows, width), fp32),
        in_specs=[pl.BlockSpec(memory_space=pl.ANY)],
        out_specs=pl.BlockSpec(memory_space=pltpu.VMEM),
        scratch_shapes=Scattering.scratch(bits, value, half, fixed),
        compiler_params=pltpu.CompilerParams(
            collective_id=number, has_side_effects=True, vmem_limit_bytes=60 * 2**20
        ),
        name=f"scatter_{number}",
    )(value)


def remote(src, dst, send_sem, recv_sem, device):
    return pltpu.make_async_remote_copy(
        src_ref=src,
        dst_ref=dst,
        send_sem=send_sem,
        recv_sem=recv_sem,
        device_id=device,
        device_id_type=pl.DeviceIdType.MESH,
    )


class Exchange:
    def __init__(self, pieces, sems, across=False):
        self.pieces = [(*piece, None, None)[:4] for piece in pieces]
        self.send, self.recv, self.local = sems
        self.me, self.count = lax.axis_index("seq"), lax.axis_size("seq")
        self.other = {"dp": flip(lax.axis_index("dp"), 1)} if across else {}
        self.across = across

    @staticmethod
    def semaphores(pieces, count):
        return [
            pltpu.SemaphoreType.DMA((pieces, count)),
            pltpu.SemaphoreType.DMA((pieces, count)),
            pltpu.SemaphoreType.DMA((pieces,)),
        ]

    @staticmethod
    def where(needed, place, action):
        if needed is None:
            action()
        else:
            pl.when(needed(place))(action)

    def own(self, which):
        source, target = self.pieces[which][:2]
        return pltpu.make_async_copy(source(self.me), target(self.me), self.local.at[which])

    def each_own(self, action):
        for which, piece in enumerate(self.pieces):
            self.where(piece[3], self.me, lambda which=which: action(self.own(which)))

    def start_own(self):
        self.each_own(lambda copy: copy.start())

    def wait_own(self):
        self.each_own(lambda copy: copy.wait())

    def going(self, which, step):
        to = lax.rem(self.me + step, self.count)
        source, target = self.pieces[which][:2]
        return remote(
            source(to),
            target(self.me),
            self.send.at[which, step],
            self.recv.at[which, step],
            {"seq": to, **self.other},
        )

    def origin(self, step):
        return lax.rem(self.me - step + self.count, self.count)

    def each_going(self, step, action):
        to = lax.rem(self.me + step, self.count)
        for which, piece in enumerate(self.pieces):
            self.where(piece[3], to, lambda which=which: action(self.going(which, step)))

    def start(self, step):
        self.each_going(step, lambda copy: copy.start())

    def wait_sent(self, step):
        self.each_going(step, lambda copy: copy.wait_send())

    def wait_arrived(self, step):
        for which, (_, target, arrival, needed) in enumerate(self.pieces):
            block = (arrival or target)(self.origin(step))

            def wait(which=which, block=block):
                remote(
                    block,
                    block,
                    self.send.at[which, step],
                    self.recv.at[which, step],
                    {"seq": self.me},
                ).wait_recv()

            self.where(needed, self.me, wait)


class Channels:
    def __init__(self, width, places):
        tiles = width // LANES
        if places == 8 and tiles == 20:
            half_starts, half_counts = [0, 4, 2, 7], [2, 3, 2, 3]
            self.starts = half_starts + [start + 10 for start in half_starts]
            self.counts = half_counts * 2
        else:
            cuts = [tiles * i // places for i in range(places + 1)]
            self.starts = cuts[:places]
            self.counts = [cuts[i + 1] - cuts[i] for i in range(places)]
        self.places, self.total = places, width
        self.tiles = max(self.counts)
        self.width = self.tiles * LANES
        self.least = self.width - LANES
        per_block = BW // LANES
        lasts = [start + count - 1 for start, count in zip(self.starts, self.counts)]
        reach = [last // per_block - start // per_block + 1 for start, last in zip(self.starts, lasts)]
        self.blocks = max(reach)
        self.span = self.blocks * BW
        firsts = [min(start // per_block, NB - self.blocks) for start in self.starts]
        self.bases = [first * BW for first in firsts]
        self.full = [
            count == self.tiles or last // per_block > first
            for count, last, first in zip(self.counts, lasts, firsts)
        ]
        assert self.full == [count == self.tiles for count in self.counts]
        self.layer, taken = {}, []
        for part in range(2):
            for i in range(places):
                if part and not self.full[i]:
                    self.layer[i, part] = 0
                    continue
                held = {firsts[i]} if part == 0 else set(range(firsts[i] + 1, firsts[i] + self.blocks))
                free = [at for at, blocks in enumerate(taken) if not blocks & held]
                if not free:
                    free = [len(taken)]
                    taken.append(set())
                self.layer[i, part] = free[0]
                taken[free[0]] |= held
        self.taken = taken
        self.shifts = [start * LANES - base for start, base in zip(self.starts, self.bases)]
        assert all(shift + self.width <= self.span for shift in self.shifts)
        self.common = self.least + BW + self.least
        self.lanes = 2 * self.width + self.span

    def pick(self, table, place):
        out = table[0]
        for i in range(1, self.places):
            out = jnp.where(place == i, int(table[i]), out)
        return out

    def begin(self, place):
        return self.pick([start * LANES for start in self.starts], place)

    def base(self, place):
        return self.pick(self.bases, place)

    def layer_of(self, part, place):
        return self.pick([self.layer[i, part] for i in range(self.places)], place)

    def is_full(self, place):
        return self.pick([int(full) for full in self.full], place) == 1

    def owned(self, value, place):
        choices = sorted(set(self.shifts))
        shift = self.pick(self.shifts, place)
        out = value[..., choices[0] : choices[0] + self.width]
        for at in choices[1:]:
            out = jnp.where(shift == at, value[..., at : at + self.width], out)
        return out

    def widened(self, value, place):
        lead = [(0, 0)] * (value.ndim - 1)
        choices = sorted(set(self.shifts))
        shift = self.pick(self.shifts, place)
        out = jnp.pad(value, (*lead, (choices[0], self.span - self.width - choices[0])))
        for at in choices[1:]:
            padded = jnp.pad(value, (*lead, (at, self.span - self.width - at)))
            out = jnp.where(shift == at, padded, out)
        return out

    def mine(self, place):
        count = self.pick(self.counts, place)
        return lax.broadcasted_iota(jnp.int32, (1, self.width), 1) < count * LANES

    def place_in(self, at):
        if at < self.least:
            return "out", at
        if at >= self.lanes - LANES:
            return "out", at - (self.lanes - LANES) + self.least
        return "in", at - self.least

    def line_parts(self):
        common, inputs = self.common - self.least, self.span + self.width
        return [
            ("in", pl.ds(0, common), False),
            ("out", pl.ds(0, self.least), False),
            ("in", pl.ds(common, inputs - common), True),
            ("out", pl.ds(self.least, LANES), True),
        ]

    def rec_of(self, value):
        rec = jnp.concatenate([value[..., :BW], value[..., BW + self.width :]], axis=-1)
        return rec, value[..., BW : BW + self.width]

    def routes(self):
        least, common = self.least, self.common
        return [
            ("out", 0, least, 0, False),
            ("rec", 0, BW, least, False),
            ("gelu", 0, least, least + BW, False),
            ("gelu", least, LANES, common, True),
            ("rec", BW, self.span - BW, common + LANES, True),
            ("out", least, LANES, self.lanes - LANES, True),
        ]


def lanes(start, width):
    return pl.ds(pl.multiple_of(start, LANES) if width % LANES == 0 else start, width)


def opening(chans, arrays, mlps, package, tokens, number):
    seqs, dps, pairs = lax.axis_size("seq"), lax.axis_size("dp"), pair_count()
    plane = plane_bits()
    names = sorted(arrays)
    rows, lines = arrays["rec"].shape[0], package.shape[0]
    cols = mlps[0].shape[1] // (pairs * seqs)
    routes = chans.routes()
    parts = chans.line_parts()
    piece_counts = [len(routes), len(mlps), len(mlps)]
    x_sems = len(Exchange.semaphores(1, seqs))

    def kernel(*refs):
        array_refs, refs = dict(zip(names, refs)), refs[len(names) :]
        mlp_refs, refs = refs[: len(mlps)], refs[len(mlps) :]
        package_ref, tokens_ref, refs = refs[0], refs[1], refs[2:]
        fulls, refs = dict(zip(("in", "out"), refs)), refs[2:]
        mlp_all, shared_all, tokens_all, refs = *refs[:3], refs[3:]
        exchange_sems = [refs[x_sems * i : x_sems * (i + 1)] for i in range(3)]
        refs = refs[3 * x_sems :]
        line_send, line_recv, zeros, zero_sem, refs = *refs[:4], refs[4:]
        me_s, me_d = lax.axis_index("seq"), lax.axis_index("dp")
        is_full = chans.is_full(me_s)

        def route(name, skip, width, at, optional):
            def source(to):
                begin = chans.base(to) if name == "rec" else chans.begin(to)
                return array_refs[name].at[:, lanes(begin + skip, width)]

            which, inside = chans.place_in(at)
            target = lambda origin: fulls[which].at[origin, me_d, :, pl.ds(inside, width)]
            return source, target, target, chans.is_full if optional else None

        move = Exchange([route(*entry) for entry in routes], exchange_sems[0])
        low = lax.rem(me_d, pairs)

        def mlp_piece(which, target_low, here, there):
            return (
                lambda to: mlp_refs[which].at[:, lanes((to * pairs + target_low) * cols, cols)],
                lambda origin: mlp_all.at[origin, here, :, pl.ds(which * cols, cols)],
                lambda origin: mlp_all.at[origin, there, :, pl.ds(which * cols, cols)],
            )

        mlp_moves = [
            Exchange([mlp_piece(which, low, low, low) for which in range(len(mlps))], exchange_sems[1])
        ]
        if pairs == 2:
            mlp_moves.append(
                Exchange(
                    [mlp_piece(which, 1 - low, low, 1 - low) for which in range(len(mlps))],
                    exchange_sems[2],
                    across=True,
                )
            )
        shared = Gathering(plane, package.shape[1], None, shared_all, refs[:3])
        toks = Gathering(plane, tokens.shape[1], tokens_ref, tokens_all, refs[3:6])

        def package_slot(origin):
            return shared_all.at[me_s, pl.ds(pl.multiple_of(origin * lines, 16), lines), :]

        fan = Fan(lambda to: package_ref, package_slot, refs[6:8])
        package_own = pltpu.make_async_copy(package_ref, package_slot(me_d), refs[8])

        def greeted():
            barrier = pltpu.get_barrier_semaphore()
            targets = [{"seq": lax.rem(me_s + step, seqs)} for step in range(1, seqs)]
            targets += [{"dp": lax.rem(me_d + step, dps)} for step in range(1, dps)]
            if pairs == 2:
                targets += [
                    {"seq": lax.rem(me_s + step, seqs), "dp": flip(me_d, 1)}
                    for step in range(1, seqs)
                ]
            for target in targets:
                pl.semaphore_signal(
                    barrier, inc=1, device_id=target, device_id_type=pl.DeviceIdType.MESH
                )
            pl.semaphore_wait(barrier, len(targets))

        greeted()
        package_own.start()
        for step in range(1, dps):
            fan.going(step).start()
        move.start_own()
        for step in range(1, seqs):
            move.start(step)
        optional_parts = [(which, cut) for which, cut, optional in parts if optional]
        blanks = [
            pltpu.make_async_copy(
                zeros.at[:, :, :, pl.ds(0, cut.size)], fulls[which].at[:, :, :, cut], zero_sem.at[i]
            )
            for i, (which, cut) in enumerate(optional_parts)
        ]

        @pl.when(jnp.logical_not(is_full))
        def _():
            zeros[...] = jnp.zeros_like(zeros)
            for blank in blanks:
                blank.start()

        def line_copy(way, part, hop, step, number):
            sign = 1 if way == 0 else -1
            origin = jnp.clip(me_d - sign * hop, 0, dps - 1)
            which, cut, _ = parts[part]
            block = fulls[which].at[move.origin(step), origin, :, cut]
            return remote(
                block,
                block,
                line_send.at[2 * part + way, number, step],
                line_recv.at[2 * part + way, number, step],
                {"dp": jnp.clip(me_d + sign, 0, dps - 1)},
            )

        def has_next(way):
            return me_d < dps - 1 if way == 0 else me_d > 0

        def has_origin(way, hop):
            return me_d >= hop if way == 0 else me_d < dps - hop

        def each_line(test, action):
            for part, (_, _, optional) in enumerate(parts):
                for way in range(2):
                    condition = test(way)
                    if optional:
                        condition = condition & is_full
                    pl.when(condition)(lambda way=way, part=part: action(way, part))

        def pass_on(hop, step):
            each_line(
                lambda way: has_next(way) & has_origin(way, hop),
                lambda way, part: line_copy(way, part, hop, step, hop).start(),
            )

        move.wait_own()
        pass_on(0, 0)

        def first_round(step, carry):
            move.wait_arrived(step)
            pass_on(0, step)
            return carry

        lax.fori_loop(1, seqs, first_round, 0)
        package_own.wait()
        for step in range(1, dps):
            fan.arriving(step).wait_recv()
        shared.begin()
        levels = range(1, len(plane) + 1)
        for size in levels:
            shared.level(size)
        mlp_moves[0].start_own()
        for mlp_move in mlp_moves:
            for step in range(0 if mlp_move.across else 1, seqs):
                mlp_move.start(step)
        toks.begin()
        for hop in range(1, dps):

            def round_of(step, carry, hop=hop):
                each_line(
                    lambda way: has_origin(way, hop),
                    lambda way, part: line_copy(way, part, hop, step, hop - 1).wait_recv(),
                )
                if hop < dps - 1:
                    pass_on(hop, step)
                return carry

            lax.fori_loop(0, seqs, round_of, 0)
            if hop == min(2, dps - 1):
                for size in levels:
                    toks.level(size)

        def last_round(step, carry):
            move.wait_sent(step)
            for mlp_move in mlp_moves:
                mlp_move.wait_sent(step)
                mlp_move.wait_arrived(step)
            return carry

        lax.fori_loop(1, seqs, last_round, 0)
        mlp_moves[0].wait_own()
        if pairs == 2:
            mlp_moves[1].wait_sent(0)
            mlp_moves[1].wait_arrived(0)

        def close_round(step, carry):
            for hop in range(dps - 1):
                each_line(
                    lambda way: has_next(way) & has_origin(way, hop),
                    lambda way, part: line_copy(way, part, hop, step, hop).wait_send(),
                )
            return carry

        lax.fori_loop(0, seqs, close_round, 0)
        for step in range(1, dps):
            fan.going(step).wait_send()

        @pl.when(jnp.logical_not(is_full))
        def _():
            for blank in blanks:
                blank.wait()

        shared.finish()
        toks.finish()

    vmem, anywhere = pl.BlockSpec(memory_space=pltpu.VMEM), pl.BlockSpec(memory_space=pl.ANY)
    return pl.pallas_call(
        kernel,
        out_shape=[
            jax.ShapeDtypeStruct((seqs, dps, rows, chans.span + chans.width), half),
            jax.ShapeDtypeStruct((seqs, dps, rows, chans.width), half),
            jax.ShapeDtypeStruct((seqs, pairs, rows, len(mlps) * cols), half),
            jax.ShapeDtypeStruct((seqs, dps * lines, package.shape[1]), half),
            jax.ShapeDtypeStruct((seqs, *tokens.shape), half),
        ],
        in_specs=[anywhere] * (len(names) + len(mlps)) + [vmem] * 2,
        out_specs=[anywhere] * 5,
        scratch_shapes=[
            *itertools.chain.from_iterable(
                Exchange.semaphores(pieces, seqs) for pieces in piece_counts
            ),
            pltpu.SemaphoreType.DMA((2 * len(parts), max(dps - 1, 1), seqs)),
            pltpu.SemaphoreType.DMA((2 * len(parts), max(dps - 1, 1), seqs)),
            pltpu.VMEM((seqs, dps, rows, chans.span + LANES - BW), half),
            pltpu.SemaphoreType.DMA((len(parts),)),
            *Gathering.semaphores(plane, package.shape[1]),
            *Gathering.semaphores(plane, tokens.shape[1]),
            *Fan.semaphores(dps),
            pltpu.SemaphoreType.DMA,
        ],
        compiler_params=pltpu.CompilerParams(
            collective_id=number, has_side_effects=True, vmem_limit_bytes=63 * 2**20
        ),
        name="opening",
    )(*(arrays[name] for name in names), *mlps, package, tokens)


def closing(chans, in_part, grad_in, grad_out, mlp, mats, small, number):
    seqs, dps, pairs = lax.axis_size("seq"), lax.axis_size("dp"), pair_count()
    plane = plane_bits()
    rows = grad_in.shape[2]
    links = max(dps - 1, 1)
    cols = mlp.shape[3] // MLPS
    routes = chans.routes()
    names = sorted({route[0] for route in routes})
    wide = chans.total
    backs = {"rec": (len(chans.taken), rows, wide), "gelu": (rows, wide), "out": (rows, wide)}
    halves = [pl.ds(0, chans.common), pl.ds(chans.common, chans.lanes - chans.common)]
    piece_counts = [len(routes), MLPS, MLPS]
    x_sems = len(Exchange.semaphores(1, seqs))
    shape = jax.ShapeDtypeStruct
    shared = [(small, fp32), (mats, half)]
    jobs = [(plane, in_part, half), *((plane, value, wire) for value, wire in shared)]
    tall = [value.shape[1] // dps for value, _ in shared]
    s_count = len(Scattering.scratch(plane, in_part, half))

    def kernel(*refs):
        part_ref, in_ref, out_ref, mlp_ref, mats_ref, small_ref, refs = *refs[:6], refs[6:]
        part_out, refs = refs[0], refs[1:]
        back_refs, refs = dict(zip(names, refs)), refs[len(names) :]
        mlp_outs, refs = refs[:MLPS], refs[MLPS:]
        mats_out, small_out, refs = refs[0], refs[1], refs[2:]
        sums, outs, fans_out, fans_in = refs[:2], [small_out, mats_out], refs[2:4], refs[4:6]
        fan_sems, refs = [refs[6:8], refs[8:10]], refs[10:]
        works = []
        for (bits, _, _), x_ref, o_ref in zip(
            jobs, (part_ref, small_ref, mats_ref), (part_out, *sums)
        ):
            works.append(Scattering(bits, x_ref, o_ref, refs[:s_count]))
            refs = refs[s_count:]
        held, outgoing, incoming, totals, load, line_send, line_recv, refs = *refs[:7], refs[7:]
        exchange_sems = [refs[x_sems * i : x_sems * (i + 1)] for i in range(3)]
        me_s, me_d = lax.axis_index("seq"), lax.axis_index("dp")
        is_full = chans.is_full(me_s)

        def route(name, skip, width, at, optional):
            def target(origin):
                if name == "rec":
                    layer = chans.layer_of(int(skip > 0), origin)
                    return back_refs[name].at[layer, :, lanes(chans.base(origin) + skip, width)]
                return back_refs[name].at[:, lanes(chans.begin(origin) + skip, width)]

            return lambda to: totals.at[to, :, pl.ds(at, width)], target, None, optional

        low = lax.rem(me_d, pairs)

        class Owners(Exchange):
            def each_own(self, action):
                for which, piece in enumerate(self.pieces):
                    test = is_full if piece[3] else None
                    self.where(test, None, lambda which=which: action(self.own(which)))

            @staticmethod
            def where(test, place, action):
                if test is None:
                    action()
                else:
                    pl.when(test)(action)

            def each_going(self, step, action):
                for which, piece in enumerate(self.pieces):
                    test = is_full if piece[3] else None
                    self.where(test, None, lambda which=which: action(self.going(which, step)))

            def wait_arrived(self, step):
                origin = self.origin(step)
                for which, (_, target, _, optional) in enumerate(self.pieces):
                    block = target(origin)

                    def wait(which=which, block=block):
                        remote(
                            block,
                            block,
                            self.send.at[which, step],
                            self.recv.at[which, step],
                            {"seq": self.me},
                        ).wait_recv()

                    self.where(chans.is_full(origin) if optional else None, None, wait)

        move = Owners([route(*entry) for entry in routes], exchange_sems[0])

        def mlp_piece(which, source_low, here, there):
            def columns(origin, part):
                return mlp_outs[which].at[:, lanes((origin * pairs + part) * cols, cols)]

            return (
                lambda to: mlp_ref.at[to, source_low, :, pl.ds(which * cols, cols)],
                lambda origin: columns(origin, here),
                lambda origin: columns(origin, there),
            )

        mlp_moves = [
            Exchange([mlp_piece(which, low, low, low) for which in range(MLPS)], exchange_sems[1])
        ]
        if pairs == 2:
            mlp_moves.append(
                Exchange(
                    [mlp_piece(which, 1 - low, low, 1 - low) for which in range(MLPS)],
                    exchange_sems[2],
                    across=True,
                )
            )

        input_lanes = pl.ds(chans.least, chans.lanes - LANES - chans.least)
        out_lanes = [
            (pl.ds(0, chans.least), pl.ds(0, chans.least)),
            (pl.ds(chans.least, LANES), pl.ds(chans.lanes - LANES, LANES)),
        ]

        def loading(chunk):
            copies = [(in_ref.at[chunk], held.at[chunk, :, :, input_lanes])]
            copies += [
                (out_ref.at[chunk, :, :, source], held.at[chunk, :, :, target])
                for source, target in out_lanes
            ]
            return [
                pltpu.make_async_copy(source, target, load.at[which, chunk])
                for which, (source, target) in enumerate(copies)
            ]

        fans = [
            Fan(
                lambda to, ref=fans_out[i]: ref.at[to],
                lambda origin, ref=fans_in[i]: ref.at[origin],
                fan_sems[i],
            )
            for i in range(2)
        ]

        def fan_lines(which, block, line):
            chunk = 16
            return pl.ds(pl.multiple_of(block * tall[which] + line * chunk, chunk), chunk)

        def fan_send():
            for which in range(2):
                for step in range(1, dps):
                    to = lax.rem(me_d + step, dps)

                    def body(line, carry, which=which, to=to):
                        part = sums[which][fan_lines(which, to, line), :]
                        fans_out[which][to, fan_lines(which, 0, line), :] = part.astype(
                            fans_out[which].dtype
                        )
                        return carry

                    lax.fori_loop(0, tall[which] // 16, body, 0)
                    fans[which].going(step).start()

        def fan_total():
            for which in range(2):
                for step in range(1, dps):
                    fans[which].arriving(step).wait_recv()

                def body(line, carry, which=which):
                    total = sums[which][fan_lines(which, me_d, line), :]
                    for step in range(1, dps):
                        origin = lax.rem(me_d - step + dps, dps)
                        part = fans_in[which][origin, fan_lines(which, 0, line), :]
                        total = total + part.astype(fp32)
                    outs[which][fan_lines(which, 0, line), :] = total
                    return carry

                lax.fori_loop(0, tall[which] // 16, body, 0)
                for step in range(1, dps):
                    fans[which].going(step).wait_send()

        def chunk_of(step):
            return lax.rem(me_s + step, seqs)

        for step in range(seqs):
            for copy in loading(chunk_of(step)):
                copy.start()
        for work in works:
            work.begin()
        barrier = pltpu.get_barrier_semaphore()
        targets = [{"seq": lax.rem(me_s + step, seqs)} for step in range(1, seqs)]
        targets += [{"dp": lax.rem(me_d + step, dps)} for step in range(1, dps)]
        if pairs == 2:
            targets += [
                {"seq": lax.rem(me_s + step, seqs), "dp": flip(me_d, 1)} for step in range(1, seqs)
            ]
        for target in targets:
            pl.semaphore_signal(
                barrier, inc=1, device_id=target, device_id_type=pl.DeviceIdType.MESH
            )
        pl.semaphore_wait(barrier, len(targets))

        def behind(way):
            return me_d > 0 if way == 0 else me_d < dps - 1

        def target_of(way, hop):
            sign = 1 if way == 0 else -1
            return jnp.clip(me_d + sign * hop, 0, dps - 1)

        def has_target(way, hop):
            return me_d < dps - hop if way == 0 else me_d >= hop

        def line_copy(way, part, hop, chunk):
            return remote(
                outgoing.at[way, hop % 2, chunk, :, halves[part]],
                incoming.at[way, hop - 1, chunk, :, halves[part]],
                line_send.at[2 * part + way, hop - 1, chunk],
                line_recv.at[2 * part + way, hop - 1, chunk],
                {"dp": target_of(way, 1)},
            )

        def combine(store, terms):
            def body(step, carry):
                lines = pl.ds(pl.multiple_of(step * 16, 16), 16)
                total = terms[0](lines)
                for term in terms[1:]:
                    total = total + term(lines)
                store(lines, total)
                return carry

            lax.fori_loop(0, rows // 16, body, 0)

        def own_term(part, chunk, block):
            return lambda lines: held[chunk, block, lines, halves[part]]

        def far_term(part, way, hop, chunk):
            return lambda lines: incoming[way, hop - 1, chunk, lines, halves[part]].astype(fp32)

        def each_line(test, action):
            for part in range(2):
                for way in range(2):
                    condition = test(way)
                    if part == 1:
                        condition = condition & is_full
                    pl.when(condition)(lambda way=way, part=part: action(way, part))

        def line_round(hop, first):
            def body(step, carry):
                chunk = chunk_of(step)
                if first:
                    for copy in loading(chunk):
                        copy.wait()
                if hop + 2 < dps:
                    each_line(
                        lambda way: has_target(way, hop + 2),
                        lambda way, part: line_copy(way, part, hop + 2, chunk).wait_send(),
                    )

                def send(way, part, far):
                    def keep(lines, total):
                        outgoing[way, hop % 2, chunk, lines, halves[part]] = total.astype(half)

                    terms = [own_term(part, chunk, target_of(way, hop))]
                    if far:
                        line_copy(way, part, hop + 1, chunk).wait_recv()
                        terms.append(far_term(part, way, hop + 1, chunk))
                    combine(keep, terms)
                    line_copy(way, part, hop, chunk).start()

                if hop == dps - 1:
                    each_line(
                        lambda way: has_target(way, hop), lambda way, part: send(way, part, False)
                    )
                else:
                    each_line(
                        lambda way: has_target(way, hop) & behind(way),
                        lambda way, part: send(way, part, True),
                    )
                    each_line(
                        lambda way: has_target(way, hop) & jnp.logical_not(behind(way)),
                        lambda way, part: send(way, part, False),
                    )
                return carry

            lax.fori_loop(0, seqs, body, 0)

        def line_total(step, carry):
            chunk = chunk_of(step)
            if dps == 1:
                for copy in loading(chunk):
                    copy.wait()
            for part in range(2):
                for ups, downs in ((True, True), (True, False), (False, True), (False, False)):
                    condition = behind(0) if ups else jnp.logical_not(behind(0))
                    condition &= behind(1) if downs else jnp.logical_not(behind(1))
                    if part == 1:
                        condition &= is_full

                    @pl.when(condition)
                    def _():
                        def keep(lines, total):
                            totals[chunk, lines, halves[part]] = total.astype(half)

                        terms = [own_term(part, chunk, me_d)]
                        for way in [way for way, far in ((0, ups), (1, downs)) if far and dps > 1]:
                            line_copy(way, part, 1, chunk).wait_recv()
                            terms.append(far_term(part, way, 1, chunk))
                        combine(keep, terms)

            @pl.when(step > 0)
            def _():
                move.start(step)

            @pl.when(step == 0)
            def _():
                move.start_own()

            return carry

        depth = len(plane)
        first_total = max(dps - 2, 0)
        for turn in range(max(depth, dps - 1)):
            if turn < dps - 1:
                line_round(dps - 1 - turn, turn == 0)
            if turn == 0:
                for work in works[1:]:
                    for stage in range(depth):
                        work.stage(stage)
                    work.finish()
                fan_send()
                mlp_moves[0].start_own()
                for mlp_move in mlp_moves:
                    for step in range(0 if mlp_move.across else 1, seqs):
                        mlp_move.start(step)
            if turn == first_total:
                lax.fori_loop(0, seqs, line_total, 0)
            if turn < depth:
                works[0].stage(turn)
        works[0].finish()
        fan_total()

        def last_round(step, carry):
            for each in [move, *mlp_moves]:
                each.wait_arrived(step)
                each.wait_sent(step)
            return carry

        lax.fori_loop(1, seqs, last_round, 0)
        move.wait_own()
        mlp_moves[0].wait_own()
        if pairs == 2:
            mlp_moves[1].wait_arrived(0)
            mlp_moves[1].wait_sent(0)

        def close_round(step, carry):
            for hop in range(1, min(dps, 3)):
                each_line(
                    lambda way: has_target(way, hop),
                    lambda way, part: line_copy(way, part, hop, step).wait_send(),
                )
            return carry

        lax.fori_loop(0, seqs, close_round, 0)
        for work in works:
            work.close()

    vmem, anywhere = pl.BlockSpec(memory_space=pltpu.VMEM), pl.BlockSpec(memory_space=pl.ANY)
    results = pl.pallas_call(
        kernel,
        out_shape=[
            shape(in_part.shape[1:], fp32),
            *(shape(backs[name], half) for name in names),
            *[shape((rows, seqs * pairs * cols), half)] * MLPS,
            shape((tall[1], mats.shape[2]), fp32),
            shape((tall[0], small.shape[2]), fp32),
        ],
        in_specs=[anywhere, anywhere, anywhere, vmem, anywhere, anywhere],
        out_specs=[vmem, *[anywhere] * (len(names) + MLPS), vmem, vmem],
        scratch_shapes=[
            *(pltpu.VMEM(value.shape[1:], fp32) for value, _ in shared),
            *(
                pltpu.VMEM((dps, lines, value.shape[2]), wire)
                for _ in range(2)
                for (value, wire), lines in zip(shared, tall)
            ),
            *(Fan.semaphores(dps) * 2),
            *itertools.chain.from_iterable(
                Scattering.scratch(bits, value, wire) for bits, value, wire in jobs
            ),
            pltpu.VMEM((seqs, dps, rows, chans.lanes), fp32),
            pltpu.VMEM((2, 2, seqs, rows, chans.lanes), half),
            pltpu.VMEM((2, links, seqs, rows, chans.lanes), half),
            pltpu.VMEM((seqs, rows, chans.lanes), half),
            pltpu.SemaphoreType.DMA((3, seqs)),
            pltpu.SemaphoreType.DMA((4, links, seqs)),
            pltpu.SemaphoreType.DMA((4, links, seqs)),
            *itertools.chain.from_iterable(
                Exchange.semaphores(pieces, seqs) for pieces in piece_counts
            ),
        ],
        compiler_params=pltpu.CompilerParams(
            collective_id=number, has_side_effects=True, vmem_limit_bytes=63 * 2**20
        ),
        name="closing",
    )(in_part, grad_in, grad_out, mlp, mats, small)
    backs = dict(zip(names, results[1:]))
    return results[0], backs, *results[1 + len(names) :]


SUBLANES = 8


def scan_kernel(forward, decay_ref, other_ref, out_ref):
    steps, width = decay_ref.shape
    tiles = steps // SUBLANES
    row = lax.broadcasted_iota(jnp.int32, (SUBLANES, width), 0)

    def tile(step, carry):
        at = step if forward else tiles - 1 - step
        lines = pl.ds(pl.multiple_of(at * SUBLANES, SUBLANES), SUBLANES)
        decay, other = decay_ref[lines, :], other_ref[lines, :]
        product, total = decay, other if forward else decay * other
        for reach in (1, 2, 4):
            shift = reach if forward else SUBLANES - reach
            inside = row >= reach if forward else row < SUBLANES - reach
            total = jnp.where(inside, product * pltpu.roll(total, shift, 0) + total, total)
            product = jnp.where(inside, product * pltpu.roll(product, shift, 0), product)
        total = product * carry + total
        if forward:
            out_ref[lines, :] = total
            last = total[SUBLANES - 1 :]
        else:
            after = jnp.where(row == SUBLANES - 1, carry, pltpu.roll(total, SUBLANES - 1, 0))
            out_ref[lines, :] = other + after
            last = total[:1]
        return jnp.broadcast_to(last, (SUBLANES, width))

    lax.fori_loop(0, tiles, tile, jnp.zeros((SUBLANES, width), fp32), unroll=4)


def time_scan(forward, decays, other):
    vmem = pl.BlockSpec(memory_space=pltpu.VMEM)
    return pl.pallas_call(
        functools.partial(scan_kernel, forward),
        out_shape=jax.ShapeDtypeStruct(decays.shape, fp32),
        in_specs=[vmem, vmem],
        out_specs=vmem,
        name="forward_scan" if forward else "backward_scan",
    )(decays, other)


def swap(value, axis, mask):
    return lax.ppermute(value, axis, [(i, i ^ mask) for i in range(lax.axis_size(axis))])


def far_masks(axis):
    mask, masks = pair_count(), []
    while mask < lax.axis_size(axis):
        masks.append(mask)
        mask *= 2
    return masks


def share_gather(value, axis):
    me = lax.axis_index(axis)
    for mask in far_masks(axis):
        other = swap(value, axis, mask)
        low = (me // mask) % 2 == 0
        value = jnp.concatenate(
            [jnp.where(low, value, other), jnp.where(low, other, value)], axis=1
        )
    return value


def share_scatter(value, axis):
    pairs = pair_count()
    sources, count, rows, width = value.shape
    groups = [list(range(low, count, pairs)) for low in range(pairs)]
    value = value.reshape(sources, count // pairs, pairs, rows, width)
    return lax.psum_scatter(value, axis, scatter_dimension=1, axis_index_groups=groups)


def rms_norm(values, gain_vec):
    return (
        values * lax.rsqrt(jnp.mean(values * values, axis=-1, keepdims=True) + norm_eps) * gain_vec
    )


def gate_terms(gate_rec, gate_inp, conv_val, rec_vals):
    recur_gate = jax.nn.sigmoid(gate_rec)
    admit_gate = jax.nn.sigmoid(gate_inp)
    log_decay = -gate_power * recur_gate * jax.nn.softplus(-rec_vals)
    decays = jnp.exp(log_decay)
    scaler = jnp.sqrt(jnp.maximum(-jnp.expm1(2.0 * log_decay), floor_square))
    return (decays, scaler * admit_gate * conv_val)


def contract_rows(left, right):
    return lax.dot_general(left, right, (((0,), (0,)), ((), ())), preferred_element_type=fp32)


def times_trans(left, right):
    return lax.dot_general(left, right, (((1,), (1,)), ((), ())), preferred_element_type=fp32)


def part_of_sum(left, right):
    return times_trans(left, right).astype(half)


def times(left, right):
    return jnp.dot(left, right, preferred_element_type=fp32)


def gelu_product(first, second):
    return jax.nn.gelu(first, approximate=True) * second


def on_device(
    tokens,
    valid_mask,
    teacher,
    norm_one,
    proj_gelu,
    proj_rec,
    conv_taps,
    conv_bias,
    gate_rec_w,
    gate_rec_b,
    gate_inp_w,
    gate_inp_b,
    rec_param,
    proj_out,
    norm_two,
    mlp_gate,
    mlp_up,
    mlp_down,
):
    seqs, dps = lax.axis_size("seq"), lax.axis_size("dp")
    everyone = seqs * dps
    me_seq = lax.axis_index("seq")
    local_len, model = tokens.shape[-2:]
    rec_width = proj_rec.shape[1]
    hidden_width = mlp_gate.shape[1]
    rows_w = proj_rec.shape[0]
    rows_c = gate_rec_w.shape[0]
    steps = seqs * local_len

    plane, cube, pairs = plane_bits(), cube_bits(), pair_count()

    chans = Channels(rec_width, seqs)
    width_r, span, span_blocks = chans.width, chans.span, chans.blocks
    base = chans.base(me_seq)
    cols = hidden_width // (pairs * seqs)

    mask_val = valid_mask.reshape(local_len).astype(fp32)
    own_count = jnp.sum(mask_val)
    count_high = jnp.floor(own_count / 128.0)
    count_pair = jnp.stack([count_high, own_count - 128.0 * count_high]).astype(half)

    def row_of(value):
        return jnp.pad(value, ((0, 0), (0, 2 * BW - value.shape[1])))

    block_rows = -(-rows_c // 16) * 16
    package = jnp.concatenate(
        [
            jnp.pad(
                jnp.concatenate([gate_rec_w, gate_inp_w], axis=1),
                ((0, block_rows - rows_c), (0, 0)),
            ),
            row_of(conv_taps),
            row_of(jnp.stack([conv_bias, gate_rec_b, gate_inp_b, rec_param])),
            row_of(jnp.stack([norm_one, norm_two])),
            row_of(count_pair[None, :]),
            jnp.zeros((5, 2 * BW), half),
        ],
        axis=0,
    )
    w_in, w_out, mlp_own, shared, tokens_all = opening(
        chans,
        {"rec": proj_rec, "gelu": proj_gelu, "out": proj_out.T},
        [mlp_gate, mlp_up, mlp_down.T],
        package,
        tokens.reshape(local_len, model),
        1,
    )
    shared = shared.reshape(everyone, *package.shape)
    w_in, w_out = w_in.reshape(model, span + width_r), w_out.reshape(model, width_r)
    w_mlp = share_gather(mlp_own, "dp").reshape(model, 3 * cols)
    w_two, w_down = w_mlp[:, : 2 * cols], w_mlp[:, 2 * cols :]
    blocks_all = shared[:, :rows_c].reshape(rec_width, 2 * BW)
    vectors = shared[:, block_rows:].astype(fp32)
    channel_vecs = vectors[:, : CONV + 4, :rows_c].transpose(1, 0, 2).reshape(CONV + 4, rec_width)
    gains = vectors[:, CONV + 4 : CONV + 6, :rows_w].transpose(1, 0, 2).reshape(2, model)
    counts = jnp.sum(vectors[:, CONV + 6, :2], axis=0)
    valid_total = 128.0 * counts[0] + counts[1]

    span_vecs = lax.dynamic_slice(channel_vecs, (0, base), (CONV + 4, span))
    tap_vals, bias_vals = span_vecs[:CONV], span_vecs[CONV]
    rec_bias, inp_bias, rec_vals = (
        chans.owned(span_vecs[CONV + 1 + i], me_seq) for i in range(3)
    )
    mine = chans.mine(me_seq)
    span_mats = lax.dynamic_slice(blocks_all, (base, 0), (span, 2 * BW))

    def block_diagonal(value):
        rows = []
        for place in range(span_blocks):
            block = value[place * BW : (place + 1) * BW]
            rows.append(jnp.pad(block, ((0, 0), (place * BW, (span_blocks - 1 - place) * BW))))
        return chans.owned(jnp.concatenate(rows, axis=0), me_seq)

    w_gates = jnp.concatenate(
        [block_diagonal(span_mats[:, :BW]), block_diagonal(span_mats[:, BW:])], axis=1
    )
    gain_one, gain_two = gains[0], gains[1]

    flat_in = tokens.reshape(local_len, model).astype(fp32)
    tokens_all = tokens_all.reshape(steps, model).astype(fp32)
    normed_all = rms_norm(tokens_all, gain_one).astype(half)
    pre = times(normed_all, w_in)
    rec_pre, gelu_pre = chans.rec_of(pre)
    padded = jnp.concatenate([jnp.zeros((CONV - 1, span), fp32), rec_pre], axis=0)
    conv_sum = bias_vals + jnp.zeros_like(rec_pre)
    for offset in range(CONV):
        conv_sum = conv_sum + tap_vals[offset] * padded[CONV - 1 - offset : CONV - 1 - offset + steps]
    conv_low = conv_sum.astype(half)
    conv_val = chans.owned(conv_low, me_seq).astype(fp32)
    gates = times(conv_low, w_gates)
    gate_rec = gates[:, :width_r] + rec_bias
    gate_inp = gates[:, width_r:] + inp_bias
    decays, drives = gate_terms(gate_rec, gate_inp, conv_val, rec_vals)
    states = time_scan(True, decays, drives)
    mixed_low = jnp.where(mine, gelu_product(gelu_pre, states), 0.0).astype(half)
    mixed_part = part_of_sum(mixed_low, w_out).reshape(seqs, local_len, model)
    middle = flat_in + scatter_sum(mixed_part, plane, 3)

    normed_two_low = rms_norm(middle, gain_two).astype(half)
    group = pairs * seqs
    tall = group * local_len
    normed_two_all = gather(normed_two_low, cube, 4).reshape(tall, model)
    pre_two = times(normed_two_all, w_two)
    gate_pre, up_pre = pre_two[:, :cols], pre_two[:, cols:]
    hidden_low = gelu_product(gate_pre, up_pre).astype(half)
    down_part = part_of_sum(hidden_low, w_down).reshape(group, local_len, model)
    result = middle + scatter_sum(down_part, cube, 5)
    differ = result - teacher.reshape(local_len, model).astype(fp32)
    own_loss = 0.5 * jnp.sum(mask_val[:, None] * differ * differ)
    token_total = local_len * everyone
    grad_result = mask_val[:, None] * (token_total / valid_total) * differ
    output = result.reshape(tokens.shape).astype(half)

    down_all = gather(grad_result.astype(half), cube, 6).reshape(tall, model)
    grad_down = contract_rows(down_all, hidden_low)
    grad_hidden = times(down_all, w_down)
    _, pull_mlp = jax.vjp(gelu_product, gate_pre, up_pre)
    two_low = jnp.concatenate(pull_mlp(grad_hidden), axis=1).astype(half)
    grad_two = contract_rows(normed_two_all, two_low)
    two_part = part_of_sum(two_low, w_two).reshape(group, local_len, model)

    grad_normed_two = scatter_sum(two_part, cube, 7)
    grad_normed_two, grad_two, grad_down = lax.optimization_barrier(
        (grad_normed_two, grad_two, grad_down)
    )
    grad_mlp = jnp.concatenate([grad_two, grad_down], axis=1).astype(half)
    sent_mlp = share_scatter(grad_mlp.reshape(seqs, dps, rows_w, 3 * cols), "dp")

    _, pull_norm_two = jax.vjp(rms_norm, middle, gain_two)
    grad_middle_norm, grad_norm_two = pull_norm_two(grad_normed_two)
    grad_middle = grad_result + grad_middle_norm

    middle_low = gather(grad_middle.astype(half), plane, 8).reshape(steps, model)
    grad_out = contract_rows(middle_low, mixed_low)
    grad_mixed = jnp.where(mine, times(middle_low, w_out), 0.0)
    _, pull_mix = jax.vjp(gelu_product, gelu_pre, states)
    grad_gelu_pre, grad_states = pull_mix(grad_mixed)
    adjoint = time_scan(False, decays, grad_states)
    prior_state = jnp.concatenate([jnp.zeros_like(states[:1]), states[:-1]], axis=0)
    _, pull_gates = jax.vjp(gate_terms, gate_rec, gate_inp, conv_val, rec_vals)
    grad_rec_gate, grad_inp_gate, grad_conv_direct, grad_rec_param = pull_gates(
        (adjoint * prior_state, adjoint)
    )
    gates_low = jnp.concatenate([grad_rec_gate, grad_inp_gate], axis=1).astype(half)
    grad_gate_bias = jnp.sum(gates_low.astype(fp32), axis=0)
    grad_gates = contract_rows(conv_low, gates_low)
    grad_conv = times_trans(gates_low, w_gates) + chans.widened(grad_conv_direct, me_seq)
    grad_conv_bias = jnp.sum(grad_conv, axis=0)
    ahead = jnp.concatenate([grad_conv, jnp.zeros((CONV - 1, span), fp32)], axis=0)
    tap_grads = []
    rec_back = jnp.zeros_like(grad_conv)
    for offset in range(CONV):
        window = padded[CONV - 1 - offset : CONV - 1 - offset + steps]
        tap_grads.append(jnp.sum(grad_conv * window, axis=0))
        rec_back = rec_back + tap_vals[offset] * ahead[offset : offset + steps]
    rec_low = rec_back.astype(half)
    in_low = jnp.concatenate(
        [rec_low[:, :BW], grad_gelu_pre.astype(half), rec_low[:, BW:]], axis=1
    )
    grad_in = contract_rows(normed_all, in_low)
    in_part = part_of_sum(in_low, w_in).reshape(seqs, local_len, model)
    grad_norm_one = jnp.sum(w_in.astype(fp32) * grad_in, axis=1) / gain_one

    def spread(value):
        return lax.dynamic_update_slice(
            jnp.zeros((value.shape[0], rec_width), fp32), value, (0, base)
        )

    def diagonal_blocks(value):
        wide = chans.widened(value, me_seq)
        block = lax.broadcasted_iota(jnp.int32, (span, BW), 0) // BW
        picked = wide[:, :BW]
        for i in range(1, span_blocks):
            picked = jnp.where(block == i, wide[:, i * BW : (i + 1) * BW], picked)
        return picked

    mats = jnp.concatenate(
        [diagonal_blocks(grad_gates[:, :width_r]), diagonal_blocks(grad_gates[:, width_r:])], axis=1
    )
    mats = lax.dynamic_update_slice(jnp.zeros((rec_width, 2 * BW), fp32), mats, (base, 0))
    mats = jnp.pad(
        mats.reshape(everyone, rows_c, 2 * BW), ((0, 0), (0, block_rows - rows_c), (0, 0))
    )

    def widen(value):
        return chans.widened(value[None, :], me_seq)

    lines = jnp.concatenate(
        [
            jnp.stack(tap_grads),
            grad_conv_bias[None, :],
            widen(grad_gate_bias[:width_r]),
            widen(grad_gate_bias[width_r:]),
            widen(grad_rec_param),
        ],
        axis=0,
    )
    lines = spread(lines).reshape(CONV + 4, everyone, rows_c).transpose(1, 0, 2)
    gain_lines = jnp.stack([grad_norm_one, grad_norm_two]).reshape(2, everyone, rows_w)
    gain_lines = gain_lines.transpose(1, 0, 2)

    def lane_pad(value):
        return jnp.pad(value, ((0, 0), (0, 0), (0, LANES - value.shape[2])))

    small = jnp.concatenate(
        [
            lane_pad(lines),
            lane_pad(gain_lines),
            jnp.full((everyone, 1, LANES), own_loss),
            jnp.zeros((everyone, 5, LANES), fp32),
        ],
        axis=1,
    )
    grad_normed, backs, out_gate, out_up, out_down, mats, small = closing(
        chans,
        in_part,
        grad_in.reshape(seqs, dps, rows_w, span + width_r),
        grad_out.reshape(seqs, dps, rows_w, width_r),
        sent_mlp,
        mats.astype(half).reshape(seqs, -1, 2 * BW),
        small.reshape(seqs, -1, LANES),
        2,
    )
    mean_loss = small[CONV + 6, 0] / (valid_total * model)

    _, pull_norm_one = jax.vjp(lambda values: rms_norm(values, gain_one), flat_in)
    grad_tokens = (grad_middle + pull_norm_one(grad_normed)[0]).reshape(tokens.shape).astype(half)

    block_of = lax.broadcasted_iota(jnp.int32, (1, rec_width), 1) // BW

    def layer_sum(at, blocks):
        has = functools.reduce(jnp.logical_or, [block_of == block for block in sorted(blocks)])
        return jnp.where(has, backs["rec"][at].astype(fp32), 0.0)

    out_gate, out_up = out_gate.astype(fp32), out_up.astype(fp32)
    out_down = out_down.T.astype(fp32)
    out_proj_out = backs["out"].T.astype(fp32)
    out_proj_gelu = backs["gelu"].astype(fp32)
    layers = [layer_sum(at, blocks) for at, blocks in enumerate(chans.taken)]
    out_proj_rec = functools.reduce(jnp.add, layers)

    return (
        output,
        mean_loss,
        grad_tokens,
        small[CONV + 4, :rows_w],
        out_proj_gelu,
        out_proj_rec,
        small[:CONV, :rows_c],
        small[CONV, :rows_c],
        mats[:rows_c, :BW],
        small[CONV + 1, :rows_c],
        mats[:rows_c, BW:],
        small[CONV + 2, :rows_c],
        small[CONV + 3, :rows_c],
        out_proj_out,
        small[CONV + 5, :rows_w],
        out_gate,
        out_up,
        out_down,
    )


def solution(mesh):
    both = ("seq", "dp")
    rows, cols, flat = P(both, None), P(None, both), P(both)
    acts = P("dp", "seq", None)
    in_specs = (
        acts,
        P("dp", "seq"),
        acts,
        flat,
        rows,
        rows,
        cols,
        flat,
        rows,
        flat,
        rows,
        flat,
        flat,
        cols,
        flat,
        rows,
        rows,
        cols,
    )
    out_specs = (
        acts,
        P(),
        acts,
        flat,
        rows,
        rows,
        cols,
        flat,
        rows,
        flat,
        rows,
        flat,
        flat,
        cols,
        flat,
        rows,
        rows,
        cols,
    )
    return jax.shard_map(
        on_device, mesh=mesh, in_specs=in_specs, out_specs=out_specs, check_vma=False
    )
```

```python
import functools
import itertools

import jax
import jax.numpy as jnp
from jax import lax
from jax.experimental import pallas as pl
from jax.experimental.pallas import tpu as pltpu
from jax.sharding import PartitionSpec as P

NB = 10
BW = 256
CONV = 4
LANES = 128
MLPS = 3

norm_eps = 1e-06
gate_power = 8.0
floor_square = 0.0001

fp32 = jnp.float32
half = jnp.bfloat16


def flip(index, mask):
    return index + mask - 2 * mask * ((index // mask) % 2)


def bit_values(bits):
    return [(lax.axis_index(axis) // mask) % 2 for axis, mask, _ in bits]


def slot_number(bits, vals, flipped):
    total = 0
    for place, (_, _, weight) in enumerate(bits):
        total = total + weight * (1 - vals[place] if place in flipped else vals[place])
    return total


def partner(bit):
    axis, mask, _ = bit
    return {axis: flip(lax.axis_index(axis), mask)}


def greet(bits):
    barrier = pltpu.get_barrier_semaphore()
    for bit in bits:
        pl.semaphore_signal(
            barrier, inc=1, device_id=partner(bit), device_id_type=pl.DeviceIdType.MESH
        )
    pl.semaphore_wait(barrier, len(bits))


def masks_of(size):
    return [2**place for place in reversed(range(size.bit_length() - 1))]


def plane_bits():
    return tuple(("seq", mask, mask) for mask in masks_of(lax.axis_size("seq")))


def pair_count():
    return 2 if lax.axis_size("dp") > 1 and 2 * lax.axis_size("seq") <= 16 else 1


def cube_bits():
    pair = (("dp", 1, lax.axis_size("seq")),) if pair_count() == 2 else ()
    return (*pair, *plane_bits())


def world_bits():
    dps = lax.axis_size("dp")
    return tuple(("dp", mask, mask) for mask in masks_of(dps)) + tuple(
        ("seq", mask, mask * dps) for mask in masks_of(lax.axis_size("seq"))
    )


def subsets(items):
    for size in range(len(items) + 1):
        yield from itertools.combinations(items, size)


def splits(width, count):
    tiles = width // LANES
    if tiles * LANES != width or tiles < count:
        return [(0, width)]
    cuts = [tiles * i // count * LANES for i in range(count + 1)]
    return [(cuts[i], cuts[i + 1] - cuts[i]) for i in range(count)]


def rotations(bits, width, fixed=0):
    begin, slow, last = list(range(fixed)), list(range(fixed, len(bits) - 1)), [len(bits) - 1]
    pieces = splits(width, len(slow))
    return [
        (first, size, tuple(begin + slow[turn:] + slow[:turn] + last))
        for turn, (first, size) in enumerate(pieces)
    ]


class Gathering:
    def __init__(self, bits, width, x_ref, o_ref, sems, fixed=0):
        self.bits, self.x_ref, self.o_ref = bits, x_ref, o_ref
        self.send_sems, self.recv_sems, self.local_sem = sems
        self.vals = bit_values(bits)
        self.parts = rotations(bits, width, fixed)
        self.numbers = {}
        for which in range(len(self.parts)):
            for stage in range(len(bits)):
                for held in subsets(range(stage)):
                    self.numbers[which, stage, held] = len(self.numbers)

    @staticmethod
    def semaphores(bits, width, fixed=0):
        copies = len(rotations(bits, width, fixed)) * (2 ** len(bits) - 1)
        return [
            pltpu.SemaphoreType.DMA((copies,)),
            pltpu.SemaphoreType.DMA((copies,)),
            pltpu.SemaphoreType.DMA,
        ]

    def own(self):
        slot = slot_number(self.bits, self.vals, ())
        return pltpu.make_async_copy(self.x_ref, self.o_ref.at[slot], self.local_sem)

    def transfer(self, which, stage, held):
        first, width, order = self.parts[which]
        cols = pl.ds(first, width)
        slot = slot_number(self.bits, self.vals, [order[place] for place in held])
        dst = self.o_ref.at[slot, :, cols]
        number = self.numbers[which, stage, held]
        in_place = held or self.x_ref is None
        return pltpu.make_async_remote_copy(
            src_ref=dst if in_place else self.x_ref.at[:, cols],
            dst_ref=dst,
            send_sem=self.send_sems.at[number],
            recv_sem=self.recv_sems.at[number],
            device_id=partner(self.bits[order[stage]]),
            device_id_type=pl.DeviceIdType.MESH,
        )

    def begin(self):
        if self.x_ref is not None:
            self.own().start()
        for stage in range(len(self.bits)):
            for which in range(len(self.parts)):
                self.transfer(which, stage, ()).start()

    def level(self, size):
        depth = len(self.bits)
        for held in itertools.combinations(range(depth), size):
            for which in range(len(self.parts)):
                self.transfer(which, held[-1], held[:-1]).wait_recv()
                for stage in range(held[-1] + 1, depth):
                    self.transfer(which, stage, held).start()

    def finish(self):
        for key in self.numbers:
            self.transfer(*key).wait_send()
        if self.x_ref is not None:
            self.own().wait()


class Fan:
    def __init__(self, source, target, sems):
        self.source, self.target = source, target
        self.send, self.recv = sems
        self.me, self.count = lax.axis_index("dp"), lax.axis_size("dp")

    @staticmethod
    def semaphores(count):
        return [pltpu.SemaphoreType.DMA((count,)), pltpu.SemaphoreType.DMA((count,))]

    def going(self, step):
        to = lax.rem(self.me + step, self.count)
        return remote(
            self.source(to), self.target(self.me), self.send.at[step], self.recv.at[step], {"dp": to}
        )

    def arriving(self, step):
        block = self.target(lax.rem(self.me - step + self.count, self.count))
        return remote(block, block, self.send.at[step], self.recv.at[step], {"dp": self.me})


class Scattering:
    def __init__(self, bits, x_ref, o_ref, scratch, fixed=0):
        self.bits, self.x_ref, self.o_ref = bits, x_ref, o_ref
        self.held, self.outgoing, self.incoming, self.load, self.send, self.recv = scratch
        self.rows, width = o_ref.shape
        self.chunk = 32 if self.rows % 32 == 0 else 16
        self.parts = [(at, size, order[::-1]) for at, size, order in rotations(bits, width, fixed)]
        self.vals = bit_values(bits)
        self.depth = len(bits)
        first_bit = self.parts[0][2][0]
        self.blocks = sorted(subsets(range(self.depth)), key=lambda s: (first_bit not in s, -len(s)))
        self.slots, self.numbers = {}, {}
        for stage in range(self.depth):
            for rest in subsets(range(stage + 1, self.depth)):
                self.slots[stage, rest] = len(self.slots)
        for which in range(len(self.parts)):
            for key in self.slots:
                self.numbers[(which, *key)] = len(self.numbers)
        self.loaded = set()

    @staticmethod
    def scratch(bits, value, wire, fixed=0):
        count, rows, width = value.shape
        copies = len(rotations(bits, width, fixed)) * (count - 1)
        return [
            pltpu.VMEM((count, rows, width), value.dtype),
            pltpu.VMEM((count - 1, rows, width), wire),
            pltpu.VMEM((count - 1, rows, width), wire),
            pltpu.SemaphoreType.DMA((count,)),
            pltpu.SemaphoreType.DMA((copies,)),
            pltpu.SemaphoreType.DMA((copies,)),
        ]

    def loading(self, members):
        key = sum(2**place for place in members)
        slot = slot_number(self.bits, self.vals, members)
        return pltpu.make_async_copy(self.x_ref.at[slot], self.held.at[key], self.load.at[key])

    def begin(self):
        for members in self.blocks:
            self.loading(members).start()

    def ready(self, members):
        key = sum(2**place for place in members)
        if key not in self.loaded:
            self.loaded.add(key)
            self.loading(members).wait()
        return key

    def transfer(self, which, stage, rest):
        first, width, order = self.parts[which]
        place = self.slots[stage, rest]
        number = self.numbers[which, stage, rest]
        return pltpu.make_async_remote_copy(
            src_ref=self.outgoing.at[place, :, pl.ds(first, width)],
            dst_ref=self.incoming.at[place, :, pl.ds(first, width)],
            send_sem=self.send.at[number],
            recv_sem=self.recv.at[number],
            device_id=partner(self.bits[order[stage]]),
            device_id_type=pl.DeviceIdType.MESH,
        )

    def add_up(self, which, key, arrived, store):
        first, width, _ = self.parts[which]
        cols = pl.ds(first, width)

        def body(step, carry):
            lines = pl.ds(pl.multiple_of(step * self.chunk, self.chunk), self.chunk)
            total = self.held[key, lines, cols].astype(fp32)
            for place in arrived:
                total = total + self.incoming[place, lines, cols].astype(fp32)
            store(lines, cols, total)
            return carry

        lax.fori_loop(0, self.rows // self.chunk, body, 0)

    def stage(self, stage):
        for rest in sorted(subsets(range(stage + 1, self.depth)), key=lambda s: (-len(s), s)):
            for which, (_, _, order) in enumerate(self.parts):
                going = (stage, *rest)
                key = self.ready([order[place] for place in going])
                for earlier in range(stage):
                    self.transfer(which, earlier, going).wait_recv()
                place = self.slots[stage, rest]

                def keep(lines, cols, total, place=place):
                    self.outgoing[place, lines, cols] = total.astype(self.outgoing.dtype)

                arrived = [self.slots[earlier, going] for earlier in range(stage)]
                self.add_up(which, key, arrived, keep)
                self.transfer(which, stage, rest).start()

    def finish(self):
        def keep(lines, cols, total):
            self.o_ref[lines, cols] = total

        key = self.ready(())
        for which in range(len(self.parts)):
            for stage in range(self.depth):
                self.transfer(which, stage, ()).wait_recv()
            self.add_up(which, key, [self.slots[stage, ()] for stage in range(self.depth)], keep)

    def close(self):
        for members in self.blocks:
            self.ready(members)
        for key in self.numbers:
            self.transfer(*key).wait_send()


def gather(value, bits, number, fixed=0):
    rows, width = value.shape

    def kernel(x_ref, o_ref, *sems):
        work = Gathering(bits, width, x_ref, o_ref, sems, fixed)
        greet(bits)
        work.begin()
        for size in range(1, len(bits) + 1):
            work.level(size)
        work.finish()

    return pl.pallas_call(
        kernel,
        out_shape=jax.ShapeDtypeStruct((2 ** len(bits), rows, width), value.dtype),
        in_specs=[pl.BlockSpec(memory_space=pltpu.VMEM)],
        out_specs=pl.BlockSpec(memory_space=pl.ANY),
        scratch_shapes=Gathering.semaphores(bits, width, fixed),
        compiler_params=pltpu.CompilerParams(collective_id=number, has_side_effects=True),
        name=f"gather_{number}",
    )(value)


def scatter_sum(value, bits, number, fixed=0):
    _, rows, width = value.shape

    def kernel(x_ref, o_ref, *scratch):
        work = Scattering(bits, x_ref, o_ref, scratch, fixed)
        work.begin()
        greet(bits)
        for stage in range(len(bits)):
            work.stage(stage)
        work.finish()
        work.close()

    return pl.pallas_call(
        kernel,
        out_shape=jax.ShapeDtypeStruct((rows, width), fp32),
        in_specs=[pl.BlockSpec(memory_space=pl.ANY)],
        out_specs=pl.BlockSpec(memory_space=pltpu.VMEM),
        scratch_shapes=Scattering.scratch(bits, value, half, fixed),
        compiler_params=pltpu.CompilerParams(
            collective_id=number, has_side_effects=True, vmem_limit_bytes=60 * 2**20
        ),
        name=f"scatter_{number}",
    )(value)


def remote(src, dst, send_sem, recv_sem, device):
    return pltpu.make_async_remote_copy(
        src_ref=src,
        dst_ref=dst,
        send_sem=send_sem,
        recv_sem=recv_sem,
        device_id=device,
        device_id_type=pl.DeviceIdType.MESH,
    )


class Exchange:
    def __init__(self, pieces, sems, across=False):
        self.pieces = [(*piece, None, None)[:4] for piece in pieces]
        self.send, self.recv, self.local = sems
        self.me, self.count = lax.axis_index("seq"), lax.axis_size("seq")
        self.other = {"dp": flip(lax.axis_index("dp"), 1)} if across else {}
        self.across = across

    @staticmethod
    def semaphores(pieces, count):
        return [
            pltpu.SemaphoreType.DMA((pieces, count)),
            pltpu.SemaphoreType.DMA((pieces, count)),
            pltpu.SemaphoreType.DMA((pieces,)),
        ]

    @staticmethod
    def where(needed, place, action):
        if needed is None:
            action()
        else:
            pl.when(needed(place))(action)

    def own(self, which):
        source, target = self.pieces[which][:2]
        return pltpu.make_async_copy(source(self.me), target(self.me), self.local.at[which])

    def each_own(self, action):
        for which, piece in enumerate(self.pieces):
            self.where(piece[3], self.me, lambda which=which: action(self.own(which)))

    def start_own(self):
        self.each_own(lambda copy: copy.start())

    def wait_own(self):
        self.each_own(lambda copy: copy.wait())

    def going(self, which, step):
        to = lax.rem(self.me + step, self.count)
        source, target = self.pieces[which][:2]
        return remote(
            source(to),
            target(self.me),
            self.send.at[which, step],
            self.recv.at[which, step],
            {"seq": to, **self.other},
        )

    def origin(self, step):
        return lax.rem(self.me - step + self.count, self.count)

    def each_going(self, step, action):
        to = lax.rem(self.me + step, self.count)
        for which, piece in enumerate(self.pieces):
            self.where(piece[3], to, lambda which=which: action(self.going(which, step)))

    def start(self, step):
        self.each_going(step, lambda copy: copy.start())

    def wait_sent(self, step):
        self.each_going(step, lambda copy: copy.wait_send())

    def wait_arrived(self, step):
        for which, (_, target, arrival, needed) in enumerate(self.pieces):
            block = (arrival or target)(self.origin(step))

            def wait(which=which, block=block):
                remote(
                    block,
                    block,
                    self.send.at[which, step],
                    self.recv.at[which, step],
                    {"seq": self.me},
                ).wait_recv()

            self.where(needed, self.me, wait)


class Channels:
    def __init__(self, width, places):
        tiles = width // LANES
        if places == 8 and tiles == 20:
            half_starts, half_counts = [0, 4, 2, 7], [2, 3, 2, 3]
            self.starts = half_starts + [start + 10 for start in half_starts]
            self.counts = half_counts * 2
        else:
            cuts = [tiles * i // places for i in range(places + 1)]
            self.starts = cuts[:places]
            self.counts = [cuts[i + 1] - cuts[i] for i in range(places)]
        self.places, self.total = places, width
        self.tiles = max(self.counts)
        self.width = self.tiles * LANES
        self.least = self.width - LANES
        per_block = BW // LANES
        lasts = [start + count - 1 for start, count in zip(self.starts, self.counts)]
        reach = [last // per_block - start // per_block + 1 for start, last in zip(self.starts, lasts)]
        self.blocks = max(reach)
        self.span = self.blocks * BW
        firsts = [min(start // per_block, NB - self.blocks) for start in self.starts]
        self.bases = [first * BW for first in firsts]
        self.full = [
            count == self.tiles or last // per_block > first
            for count, last, first in zip(self.counts, lasts, firsts)
        ]
        assert self.full == [count == self.tiles for count in self.counts]
        self.layer, taken = {}, []
        for part in range(2):
            for i in range(places):
                if part and not self.full[i]:
                    self.layer[i, part] = 0
                    continue
                held = {firsts[i]} if part == 0 else set(range(firsts[i] + 1, firsts[i] + self.blocks))
                free = [at for at, blocks in enumerate(taken) if not blocks & held]
                if not free:
                    free = [len(taken)]
                    taken.append(set())
                self.layer[i, part] = free[0]
                taken[free[0]] |= held
        self.taken = taken
        self.shifts = [start * LANES - base for start, base in zip(self.starts, self.bases)]
        assert all(shift + self.width <= self.span for shift in self.shifts)
        self.common = self.least + BW + self.least
        self.lanes = 2 * self.width + self.span

    def pick(self, table, place):
        out = table[0]
        for i in range(1, self.places):
            out = jnp.where(place == i, int(table[i]), out)
        return out

    def begin(self, place):
        return self.pick([start * LANES for start in self.starts], place)

    def base(self, place):
        return self.pick(self.bases, place)

    def layer_of(self, part, place):
        return self.pick([self.layer[i, part] for i in range(self.places)], place)

    def is_full(self, place):
        return self.pick([int(full) for full in self.full], place) == 1

    def owned(self, value, place):
        choices = sorted(set(self.shifts))
        shift = self.pick(self.shifts, place)
        out = value[..., choices[0] : choices[0] + self.width]
        for at in choices[1:]:
            out = jnp.where(shift == at, value[..., at : at + self.width], out)
        return out

    def widened(self, value, place):
        lead = [(0, 0)] * (value.ndim - 1)
        choices = sorted(set(self.shifts))
        shift = self.pick(self.shifts, place)
        out = jnp.pad(value, (*lead, (choices[0], self.span - self.width - choices[0])))
        for at in choices[1:]:
            padded = jnp.pad(value, (*lead, (at, self.span - self.width - at)))
            out = jnp.where(shift == at, padded, out)
        return out

    def mine(self, place):
        count = self.pick(self.counts, place)
        return lax.broadcasted_iota(jnp.int32, (1, self.width), 1) < count * LANES

    def place_in(self, at):
        if at < self.least:
            return "out", at
        if at >= self.lanes - LANES:
            return "out", at - (self.lanes - LANES) + self.least
        return "in", at - self.least

    def line_parts(self):
        common, inputs = self.common - self.least, self.span + self.width
        return [
            ("in", pl.ds(0, common), False),
            ("out", pl.ds(0, self.least), False),
            ("in", pl.ds(common, inputs - common), True),
            ("out", pl.ds(self.least, LANES), True),
        ]

    def rec_of(self, value):
        rec = jnp.concatenate([value[..., :BW], value[..., BW + self.width :]], axis=-1)
        return rec, value[..., BW : BW + self.width]

    def routes(self):
        least, common = self.least, self.common
        return [
            ("out", 0, least, 0, False),
            ("rec", 0, BW, least, False),
            ("gelu", 0, least, least + BW, False),
            ("gelu", least, LANES, common, True),
            ("rec", BW, self.span - BW, common + LANES, True),
            ("out", least, LANES, self.lanes - LANES, True),
        ]


def lanes(start, width):
    return pl.ds(pl.multiple_of(start, LANES) if width % LANES == 0 else start, width)


def opening(chans, arrays, mlps, package, tokens, number):
    seqs, dps, pairs = lax.axis_size("seq"), lax.axis_size("dp"), pair_count()
    plane = plane_bits()
    names = sorted(arrays)
    rows, lines = arrays["rec"].shape[0], package.shape[0]
    cols = mlps[0].shape[1] // (pairs * seqs)
    routes = chans.routes()
    parts = chans.line_parts()
    piece_counts = [len(routes), len(mlps), len(mlps)]
    x_sems = len(Exchange.semaphores(1, seqs))

    def kernel(*refs):
        array_refs, refs = dict(zip(names, refs)), refs[len(names) :]
        mlp_refs, refs = refs[: len(mlps)], refs[len(mlps) :]
        package_ref, tokens_ref, refs = refs[0], refs[1], refs[2:]
        fulls, refs = dict(zip(("in", "out"), refs)), refs[2:]
        mlp_all, shared_all, tokens_all, refs = *refs[:3], refs[3:]
        exchange_sems = [refs[x_sems * i : x_sems * (i + 1)] for i in range(3)]
        refs = refs[3 * x_sems :]
        line_send, line_recv, zeros, zero_sem, refs = *refs[:4], refs[4:]
        me_s, me_d = lax.axis_index("seq"), lax.axis_index("dp")
        is_full = chans.is_full(me_s)

        def route(name, skip, width, at, optional):
            def source(to):
                begin = chans.base(to) if name == "rec" else chans.begin(to)
                return array_refs[name].at[:, lanes(begin + skip, width)]

            which, inside = chans.place_in(at)
            target = lambda origin: fulls[which].at[origin, me_d, :, pl.ds(inside, width)]
            return source, target, target, chans.is_full if optional else None

        move = Exchange([route(*entry) for entry in routes], exchange_sems[0])
        low = lax.rem(me_d, pairs)

        def mlp_piece(which, target_low, here, there):
            return (
                lambda to: mlp_refs[which].at[:, lanes((to * pairs + target_low) * cols, cols)],
                lambda origin: mlp_all.at[origin, here, :, pl.ds(which * cols, cols)],
                lambda origin: mlp_all.at[origin, there, :, pl.ds(which * cols, cols)],
            )

        mlp_moves = [
            Exchange([mlp_piece(which, low, low, low) for which in range(len(mlps))], exchange_sems[1])
        ]
        if pairs == 2:
            mlp_moves.append(
                Exchange(
                    [mlp_piece(which, 1 - low, low, 1 - low) for which in range(len(mlps))],
                    exchange_sems[2],
                    across=True,
                )
            )
        shared = Gathering(plane, package.shape[1], None, shared_all, refs[:3])
        toks = Gathering(plane, tokens.shape[1], tokens_ref, tokens_all, refs[3:6])

        def package_slot(origin):
            return shared_all.at[me_s, pl.ds(pl.multiple_of(origin * lines, 16), lines), :]

        fan = Fan(lambda to: package_ref, package_slot, refs[6:8])
        package_own = pltpu.make_async_copy(package_ref, package_slot(me_d), refs[8])

        def greeted():
            barrier = pltpu.get_barrier_semaphore()
            targets = [{"seq": lax.rem(me_s + step, seqs)} for step in range(1, seqs)]
            targets += [{"dp": lax.rem(me_d + step, dps)} for step in range(1, dps)]
            if pairs == 2:
                targets += [
                    {"seq": lax.rem(me_s + step, seqs), "dp": flip(me_d, 1)}
                    for step in range(1, seqs)
                ]
            for target in targets:
                pl.semaphore_signal(
                    barrier, inc=1, device_id=target, device_id_type=pl.DeviceIdType.MESH
                )
            pl.semaphore_wait(barrier, len(targets))

        greeted()
        package_own.start()
        for step in range(1, dps):
            fan.going(step).start()
        move.start_own()
        for step in range(1, seqs):
            move.start(step)
        optional_parts = [(which, cut) for which, cut, optional in parts if optional]
        blanks = [
            pltpu.make_async_copy(
                zeros.at[:, :, :, pl.ds(0, cut.size)], fulls[which].at[:, :, :, cut], zero_sem.at[i]
            )
            for i, (which, cut) in enumerate(optional_parts)
        ]

        @pl.when(jnp.logical_not(is_full))
        def _():
            zeros[...] = jnp.zeros_like(zeros)
            for blank in blanks:
                blank.start()

        def line_copy(way, part, hop, step, number):
            sign = 1 if way == 0 else -1
            origin = jnp.clip(me_d - sign * hop, 0, dps - 1)
            which, cut, _ = parts[part]
            block = fulls[which].at[move.origin(step), origin, :, cut]
            return remote(
                block,
                block,
                line_send.at[2 * part + way, number, step],
                line_recv.at[2 * part + way, number, step],
                {"dp": jnp.clip(me_d + sign, 0, dps - 1)},
            )

        def has_next(way):
            return me_d < dps - 1 if way == 0 else me_d > 0

        def has_origin(way, hop):
            return me_d >= hop if way == 0 else me_d < dps - hop

        def each_line(test, action):
            for part, (_, _, optional) in enumerate(parts):
                for way in range(2):
                    condition = test(way)
                    if optional:
                        condition = condition & is_full
                    pl.when(condition)(lambda way=way, part=part: action(way, part))

        def pass_on(hop, step):
            each_line(
                lambda way: has_next(way) & has_origin(way, hop),
                lambda way, part: line_copy(way, part, hop, step, hop).start(),
            )

        move.wait_own()
        pass_on(0, 0)

        def first_round(step, carry):
            move.wait_arrived(step)
            pass_on(0, step)
            return carry

        lax.fori_loop(1, seqs, first_round, 0)
        package_own.wait()
        for step in range(1, dps):
            fan.arriving(step).wait_recv()
        shared.begin()
        levels = range(1, len(plane) + 1)
        for size in levels:
            shared.level(size)
        mlp_moves[0].start_own()
        for mlp_move in mlp_moves:
            for step in range(0 if mlp_move.across else 1, seqs):
                mlp_move.start(step)
        toks.begin()
        for hop in range(1, dps):

            def round_of(step, carry, hop=hop):
                each_line(
                    lambda way: has_origin(way, hop),
                    lambda way, part: line_copy(way, part, hop, step, hop - 1).wait_recv(),
                )
                if hop < dps - 1:
                    pass_on(hop, step)
                return carry

            lax.fori_loop(0, seqs, round_of, 0)
            if hop == min(2, dps - 1):
                for size in levels:
                    toks.level(size)

        def last_round(step, carry):
            move.wait_sent(step)
            for mlp_move in mlp_moves:
                mlp_move.wait_sent(step)
                mlp_move.wait_arrived(step)
            return carry

        lax.fori_loop(1, seqs, last_round, 0)
        mlp_moves[0].wait_own()
        if pairs == 2:
            mlp_moves[1].wait_sent(0)
            mlp_moves[1].wait_arrived(0)

        def close_round(step, carry):
            for hop in range(dps - 1):
                each_line(
                    lambda way: has_next(way) & has_origin(way, hop),
                    lambda way, part: line_copy(way, part, hop, step, hop).wait_send(),
                )
            return carry

        lax.fori_loop(0, seqs, close_round, 0)
        for step in range(1, dps):
            fan.going(step).wait_send()

        @pl.when(jnp.logical_not(is_full))
        def _():
            for blank in blanks:
                blank.wait()

        shared.finish()
        toks.finish()

    vmem, anywhere = pl.BlockSpec(memory_space=pltpu.VMEM), pl.BlockSpec(memory_space=pl.ANY)
    return pl.pallas_call(
        kernel,
        out_shape=[
            jax.ShapeDtypeStruct((seqs, dps, rows, chans.span + chans.width), half),
            jax.ShapeDtypeStruct((seqs, dps, rows, chans.width), half),
            jax.ShapeDtypeStruct((seqs, pairs, rows, len(mlps) * cols), half),
            jax.ShapeDtypeStruct((seqs, dps * lines, package.shape[1]), half),
            jax.ShapeDtypeStruct((seqs, *tokens.shape), half),
        ],
        in_specs=[anywhere] * (len(names) + len(mlps)) + [vmem] * 2,
        out_specs=[anywhere] * 5,
        scratch_shapes=[
            *itertools.chain.from_iterable(
                Exchange.semaphores(pieces, seqs) for pieces in piece_counts
            ),
            pltpu.SemaphoreType.DMA((2 * len(parts), max(dps - 1, 1), seqs)),
            pltpu.SemaphoreType.DMA((2 * len(parts), max(dps - 1, 1), seqs)),
            pltpu.VMEM((seqs, dps, rows, chans.span + LANES - BW), half),
            pltpu.SemaphoreType.DMA((len(parts),)),
            *Gathering.semaphores(plane, package.shape[1]),
            *Gathering.semaphores(plane, tokens.shape[1]),
            *Fan.semaphores(dps),
            pltpu.SemaphoreType.DMA,
        ],
        compiler_params=pltpu.CompilerParams(
            collective_id=number, has_side_effects=True, vmem_limit_bytes=63 * 2**20
        ),
        name="opening",
    )(*(arrays[name] for name in names), *mlps, package, tokens)


def closing(chans, in_part, grad_in, grad_out, mlp, mats, small, number):
    seqs, dps, pairs = lax.axis_size("seq"), lax.axis_size("dp"), pair_count()
    plane = plane_bits()
    rows = grad_in.shape[2]
    links = max(dps - 1, 1)
    cols = mlp.shape[3] // MLPS
    routes = chans.routes()
    names = sorted({route[0] for route in routes})
    wide = chans.total
    backs = {"rec": (len(chans.taken), rows, wide), "gelu": (rows, wide), "out": (rows, wide)}
    halves = [pl.ds(0, chans.common), pl.ds(chans.common, chans.lanes - chans.common)]
    piece_counts = [len(routes), MLPS, MLPS]
    x_sems = len(Exchange.semaphores(1, seqs))
    shape = jax.ShapeDtypeStruct
    shared = [(small, fp32), (mats, half)]
    jobs = [(plane, in_part, half), *((plane, value, wire) for value, wire in shared)]
    tall = [value.shape[1] // dps for value, _ in shared]
    s_count = len(Scattering.scratch(plane, in_part, half))

    def kernel(*refs):
        part_ref, in_ref, out_ref, mlp_ref, mats_ref, small_ref, refs = *refs[:6], refs[6:]
        part_out, refs = refs[0], refs[1:]
        back_refs, refs = dict(zip(names, refs)), refs[len(names) :]
        mlp_outs, refs = refs[:MLPS], refs[MLPS:]
        mats_out, small_out, refs = refs[0], refs[1], refs[2:]
        sums, outs, fans_out, fans_in = refs[:2], [small_out, mats_out], refs[2:4], refs[4:6]
        fan_sems, refs = [refs[6:8], refs[8:10]], refs[10:]
        works = []
        for (bits, _, _), x_ref, o_ref in zip(
            jobs, (part_ref, small_ref, mats_ref), (part_out, *sums)
        ):
            works.append(Scattering(bits, x_ref, o_ref, refs[:s_count]))
            refs = refs[s_count:]
        held, outgoing, incoming, totals, load, line_send, line_recv, refs = *refs[:7], refs[7:]
        exchange_sems = [refs[x_sems * i : x_sems * (i + 1)] for i in range(3)]
        me_s, me_d = lax.axis_index("seq"), lax.axis_index("dp")
        is_full = chans.is_full(me_s)

        def route(name, skip, width, at, optional):
            def target(origin):
                if name == "rec":
                    layer = chans.layer_of(int(skip > 0), origin)
                    return back_refs[name].at[layer, :, lanes(chans.base(origin) + skip, width)]
                return back_refs[name].at[:, lanes(chans.begin(origin) + skip, width)]

            return lambda to: totals.at[to, :, pl.ds(at, width)], target, None, optional

        low = lax.rem(me_d, pairs)

        class Owners(Exchange):
            def each_own(self, action):
                for which, piece in enumerate(self.pieces):
                    test = is_full if piece[3] else None
                    self.where(test, None, lambda which=which: action(self.own(which)))

            @staticmethod
            def where(test, place, action):
                if test is None:
                    action()
                else:
                    pl.when(test)(action)

            def each_going(self, step, action):
                for which, piece in enumerate(self.pieces):
                    test = is_full if piece[3] else None
                    self.where(test, None, lambda which=which: action(self.going(which, step)))

            def wait_arrived(self, step):
                origin = self.origin(step)
                for which, (_, target, _, optional) in enumerate(self.pieces):
                    block = target(origin)

                    def wait(which=which, block=block):
                        remote(
                            block,
                            block,
                            self.send.at[which, step],
                            self.recv.at[which, step],
                            {"seq": self.me},
                        ).wait_recv()

                    self.where(chans.is_full(origin) if optional else None, None, wait)

        move = Owners([route(*entry) for entry in routes], exchange_sems[0])

        def mlp_piece(which, source_low, here, there):
            def columns(origin, part):
                return mlp_outs[which].at[:, lanes((origin * pairs + part) * cols, cols)]

            return (
                lambda to: mlp_ref.at[to, source_low, :, pl.ds(which * cols, cols)],
                lambda origin: columns(origin, here),
                lambda origin: columns(origin, there),
            )

        mlp_moves = [
            Exchange([mlp_piece(which, low, low, low) for which in range(MLPS)], exchange_sems[1])
        ]
        if pairs == 2:
            mlp_moves.append(
                Exchange(
                    [mlp_piece(which, 1 - low, low, 1 - low) for which in range(MLPS)],
                    exchange_sems[2],
                    across=True,
                )
            )

        input_lanes = pl.ds(chans.least, chans.lanes - LANES - chans.least)
        out_lanes = [
            (pl.ds(0, chans.least), pl.ds(0, chans.least)),
            (pl.ds(chans.least, LANES), pl.ds(chans.lanes - LANES, LANES)),
        ]

        def loading(chunk):
            copies = [(in_ref.at[chunk], held.at[chunk, :, :, input_lanes])]
            copies += [
                (out_ref.at[chunk, :, :, source], held.at[chunk, :, :, target])
                for source, target in out_lanes
            ]
            return [
                pltpu.make_async_copy(source, target, load.at[which, chunk])
                for which, (source, target) in enumerate(copies)
            ]

        fans = [
            Fan(
                lambda to, ref=fans_out[i]: ref.at[to],
                lambda origin, ref=fans_in[i]: ref.at[origin],
                fan_sems[i],
            )
            for i in range(2)
        ]

        def fan_lines(which, block, line):
            chunk = 16
            return pl.ds(pl.multiple_of(block * tall[which] + line * chunk, chunk), chunk)

        def fan_send():
            for which in range(2):
                for step in range(1, dps):
                    to = lax.rem(me_d + step, dps)

                    def body(line, carry, which=which, to=to):
                        part = sums[which][fan_lines(which, to, line), :]
                        fans_out[which][to, fan_lines(which, 0, line), :] = part.astype(
                            fans_out[which].dtype
                        )
                        return carry

                    lax.fori_loop(0, tall[which] // 16, body, 0)
                    fans[which].going(step).start()

        def fan_total():
            for which in range(2):
                for step in range(1, dps):
                    fans[which].arriving(step).wait_recv()

                def body(line, carry, which=which):
                    total = sums[which][fan_lines(which, me_d, line), :]
                    for step in range(1, dps):
                        origin = lax.rem(me_d - step + dps, dps)
                        part = fans_in[which][origin, fan_lines(which, 0, line), :]
                        total = total + part.astype(fp32)
                    outs[which][fan_lines(which, 0, line), :] = total
                    return carry

                lax.fori_loop(0, tall[which] // 16, body, 0)
                for step in range(1, dps):
                    fans[which].going(step).wait_send()

        def chunk_of(step):
            return lax.rem(me_s + step, seqs)

        for step in range(seqs):
            for copy in loading(chunk_of(step)):
                copy.start()
        for work in works:
            work.begin()
        barrier = pltpu.get_barrier_semaphore()
        targets = [{"seq": lax.rem(me_s + step, seqs)} for step in range(1, seqs)]
        targets += [{"dp": lax.rem(me_d + step, dps)} for step in range(1, dps)]
        if pairs == 2:
            targets += [
                {"seq": lax.rem(me_s + step, seqs), "dp": flip(me_d, 1)} for step in range(1, seqs)
            ]
        for target in targets:
            pl.semaphore_signal(
                barrier, inc=1, device_id=target, device_id_type=pl.DeviceIdType.MESH
            )
        pl.semaphore_wait(barrier, len(targets))

        def behind(way):
            return me_d > 0 if way == 0 else me_d < dps - 1

        def target_of(way, hop):
            sign = 1 if way == 0 else -1
            return jnp.clip(me_d + sign * hop, 0, dps - 1)

        def has_target(way, hop):
            return me_d < dps - hop if way == 0 else me_d >= hop

        def line_copy(way, part, hop, chunk):
            return remote(
                outgoing.at[way, hop % 2, chunk, :, halves[part]],
                incoming.at[way, hop - 1, chunk, :, halves[part]],
                line_send.at[2 * part + way, hop - 1, chunk],
                line_recv.at[2 * part + way, hop - 1, chunk],
                {"dp": target_of(way, 1)},
            )

        def combine(store, terms):
            def body(step, carry):
                lines = pl.ds(pl.multiple_of(step * 16, 16), 16)
                total = terms[0](lines)
                for term in terms[1:]:
                    total = total + term(lines)
                store(lines, total)
                return carry

            lax.fori_loop(0, rows // 16, body, 0)

        def own_term(part, chunk, block):
            return lambda lines: held[chunk, block, lines, halves[part]]

        def far_term(part, way, hop, chunk):
            return lambda lines: incoming[way, hop - 1, chunk, lines, halves[part]].astype(fp32)

        def each_line(test, action):
            for part in range(2):
                for way in range(2):
                    condition = test(way)
                    if part == 1:
                        condition = condition & is_full
                    pl.when(condition)(lambda way=way, part=part: action(way, part))

        def line_round(hop, first):
            def body(step, carry):
                chunk = chunk_of(step)
                if first:
                    for copy in loading(chunk):
                        copy.wait()
                if hop + 2 < dps:
                    each_line(
                        lambda way: has_target(way, hop + 2),
                        lambda way, part: line_copy(way, part, hop + 2, chunk).wait_send(),
                    )

                def send(way, part, far):
                    def keep(lines, total):
                        outgoing[way, hop % 2, chunk, lines, halves[part]] = total.astype(half)

                    terms = [own_term(part, chunk, target_of(way, hop))]
                    if far:
                        line_copy(way, part, hop + 1, chunk).wait_recv()
                        terms.append(far_term(part, way, hop + 1, chunk))
                    combine(keep, terms)
                    line_copy(way, part, hop, chunk).start()

                if hop == dps - 1:
                    each_line(
                        lambda way: has_target(way, hop), lambda way, part: send(way, part, False)
                    )
                else:
                    each_line(
                        lambda way: has_target(way, hop) & behind(way),
                        lambda way, part: send(way, part, True),
                    )
                    each_line(
                        lambda way: has_target(way, hop) & jnp.logical_not(behind(way)),
                        lambda way, part: send(way, part, False),
                    )
                return carry

            lax.fori_loop(0, seqs, body, 0)

        def line_total(step, carry):
            chunk = chunk_of(step)
            if dps == 1:
                for copy in loading(chunk):
                    copy.wait()
            for part in range(2):
                for ups, downs in ((True, True), (True, False), (False, True), (False, False)):
                    condition = behind(0) if ups else jnp.logical_not(behind(0))
                    condition &= behind(1) if downs else jnp.logical_not(behind(1))
                    if part == 1:
                        condition &= is_full

                    @pl.when(condition)
                    def _():
                        def keep(lines, total):
                            totals[chunk, lines, halves[part]] = total.astype(half)

                        terms = [own_term(part, chunk, me_d)]
                        for way in [way for way, far in ((0, ups), (1, downs)) if far and dps > 1]:
                            line_copy(way, part, 1, chunk).wait_recv()
                            terms.append(far_term(part, way, 1, chunk))
                        combine(keep, terms)

            @pl.when(step > 0)
            def _():
                move.start(step)

            @pl.when(step == 0)
            def _():
                move.start_own()

            return carry

        depth = len(plane)
        first_total = max(dps - 2, 0)
        for turn in range(max(depth, dps - 1)):
            if turn < dps - 1:
                line_round(dps - 1 - turn, turn == 0)
            if turn == 0:
                for work in works[1:]:
                    for stage in range(depth):
                        work.stage(stage)
                    work.finish()
                fan_send()
                mlp_moves[0].start_own()
                for mlp_move in mlp_moves:
                    for step in range(0 if mlp_move.across else 1, seqs):
                        mlp_move.start(step)
            if turn == first_total:
                lax.fori_loop(0, seqs, line_total, 0)
            if turn < depth:
                works[0].stage(turn)
        works[0].finish()
        fan_total()

        def last_round(step, carry):
            for each in [move, *mlp_moves]:
                each.wait_arrived(step)
                each.wait_sent(step)
            return carry

        lax.fori_loop(1, seqs, last_round, 0)
        move.wait_own()
        mlp_moves[0].wait_own()
        if pairs == 2:
            mlp_moves[1].wait_arrived(0)
            mlp_moves[1].wait_sent(0)

        def close_round(step, carry):
            for hop in range(1, min(dps, 3)):
                each_line(
                    lambda way: has_target(way, hop),
                    lambda way, part: line_copy(way, part, hop, step).wait_send(),
                )
            return carry

        lax.fori_loop(0, seqs, close_round, 0)
        for work in works:
            work.close()

    vmem, anywhere = pl.BlockSpec(memory_space=pltpu.VMEM), pl.BlockSpec(memory_space=pl.ANY)
    results = pl.pallas_call(
        kernel,
        out_shape=[
            shape(in_part.shape[1:], fp32),
            *(shape(backs[name], half) for name in names),
            *[shape((rows, seqs * pairs * cols), half)] * MLPS,
            shape((tall[1], mats.shape[2]), fp32),
            shape((tall[0], small.shape[2]), fp32),
        ],
        in_specs=[anywhere, anywhere, anywhere, vmem, anywhere, anywhere],
        out_specs=[vmem, *[anywhere] * (len(names) + MLPS), vmem, vmem],
        scratch_shapes=[
            *(pltpu.VMEM(value.shape[1:], fp32) for value, _ in shared),
            *(
                pltpu.VMEM((dps, lines, value.shape[2]), wire)
                for _ in range(2)
                for (value, wire), lines in zip(shared, tall)
            ),
            *(Fan.semaphores(dps) * 2),
            *itertools.chain.from_iterable(
                Scattering.scratch(bits, value, wire) for bits, value, wire in jobs
            ),
            pltpu.VMEM((seqs, dps, rows, chans.lanes), fp32),
            pltpu.VMEM((2, 2, seqs, rows, chans.lanes), half),
            pltpu.VMEM((2, links, seqs, rows, chans.lanes), half),
            pltpu.VMEM((seqs, rows, chans.lanes), half),
            pltpu.SemaphoreType.DMA((3, seqs)),
            pltpu.SemaphoreType.DMA((4, links, seqs)),
            pltpu.SemaphoreType.DMA((4, links, seqs)),
            *itertools.chain.from_iterable(
                Exchange.semaphores(pieces, seqs) for pieces in piece_counts
            ),
        ],
        compiler_params=pltpu.CompilerParams(
            collective_id=number, has_side_effects=True, vmem_limit_bytes=63 * 2**20
        ),
        name="closing",
    )(in_part, grad_in, grad_out, mlp, mats, small)
    backs = dict(zip(names, results[1:]))
    return results[0], backs, *results[1 + len(names) :]


SUBLANES = 8


def scan_kernel(forward, decay_ref, other_ref, out_ref):
    steps, width = decay_ref.shape
    tiles = steps // SUBLANES
    row = lax.broadcasted_iota(jnp.int32, (SUBLANES, width), 0)

    def tile(step, carry):
        at = step if forward else tiles - 1 - step
        lines = pl.ds(pl.multiple_of(at * SUBLANES, SUBLANES), SUBLANES)
        decay, other = decay_ref[lines, :], other_ref[lines, :]
        product, total = decay, other if forward else decay * other
        for reach in (1, 2, 4):
            shift = reach if forward else SUBLANES - reach
            inside = row >= reach if forward else row < SUBLANES - reach
            total = jnp.where(inside, product * pltpu.roll(total, shift, 0) + total, total)
            product = jnp.where(inside, product * pltpu.roll(product, shift, 0), product)
        total = product * carry + total
        if forward:
            out_ref[lines, :] = total
            last = total[SUBLANES - 1 :]
        else:
            after = jnp.where(row == SUBLANES - 1, carry, pltpu.roll(total, SUBLANES - 1, 0))
            out_ref[lines, :] = other + after
            last = total[:1]
        return jnp.broadcast_to(last, (SUBLANES, width))

    lax.fori_loop(0, tiles, tile, jnp.zeros((SUBLANES, width), fp32), unroll=4)


def time_scan(forward, decays, other):
    vmem = pl.BlockSpec(memory_space=pltpu.VMEM)
    return pl.pallas_call(
        functools.partial(scan_kernel, forward),
        out_shape=jax.ShapeDtypeStruct(decays.shape, fp32),
        in_specs=[vmem, vmem],
        out_specs=vmem,
        name="forward_scan" if forward else "backward_scan",
    )(decays, other)


def swap(value, axis, mask):
    return lax.ppermute(value, axis, [(i, i ^ mask) for i in range(lax.axis_size(axis))])


def far_masks(axis):
    mask, masks = pair_count(), []
    while mask < lax.axis_size(axis):
        masks.append(mask)
        mask *= 2
    return masks


def share_gather(value, axis):
    me = lax.axis_index(axis)
    for mask in far_masks(axis):
        sources, size, rows, width = value.shape
        high = (me // mask) % 2
        whole = jnp.zeros((sources, 2 * size, rows, width), value.dtype)
        whole = lax.dynamic_update_slice(whole, value, (0, high * size, 0, 0))
        value = lax.dynamic_update_slice(
            whole, swap(value, axis, mask), (0, (1 - high) * size, 0, 0)
        )
    return value


def share_scatter(value, axis):
    pairs = pair_count()
    sources, count, rows, width = value.shape
    groups = [list(range(low, count, pairs)) for low in range(pairs)]
    value = value.reshape(sources, count // pairs, pairs, rows, width)
    return lax.psum_scatter(value, axis, scatter_dimension=1, axis_index_groups=groups)


def rms_norm(values, gain_vec):
    return (
        values * lax.rsqrt(jnp.mean(values * values, axis=-1, keepdims=True) + norm_eps) * gain_vec
    )


def gate_terms(gate_rec, gate_inp, conv_val, rec_vals):
    recur_gate = jax.nn.sigmoid(gate_rec)
    admit_gate = jax.nn.sigmoid(gate_inp)
    log_decay = -gate_power * recur_gate * jax.nn.softplus(-rec_vals)
    decays = jnp.exp(log_decay)
    scaler = jnp.sqrt(jnp.maximum(-jnp.expm1(2.0 * log_decay), floor_square))
    return (decays, scaler * admit_gate * conv_val)


def contract_rows(left, right):
    return lax.dot_general(left, right, (((0,), (0,)), ((), ())), preferred_element_type=fp32)


def times_trans(left, right):
    return lax.dot_general(left, right, (((1,), (1,)), ((), ())), preferred_element_type=fp32)


def part_of_sum(left, right):
    return times_trans(left, right).astype(half)


def times(left, right):
    return jnp.dot(left, right, preferred_element_type=fp32)


def gelu_product(first, second):
    return jax.nn.gelu(first, approximate=True) * second


def on_device(
    tokens,
    valid_mask,
    teacher,
    norm_one,
    proj_gelu,
    proj_rec,
    conv_taps,
    conv_bias,
    gate_rec_w,
    gate_rec_b,
    gate_inp_w,
    gate_inp_b,
    rec_param,
    proj_out,
    norm_two,
    mlp_gate,
    mlp_up,
    mlp_down,
):
    seqs, dps = lax.axis_size("seq"), lax.axis_size("dp")
    everyone = seqs * dps
    me_seq = lax.axis_index("seq")
    local_len, model = tokens.shape[-2:]
    rec_width = proj_rec.shape[1]
    hidden_width = mlp_gate.shape[1]
    rows_w = proj_rec.shape[0]
    rows_c = gate_rec_w.shape[0]
    steps = seqs * local_len

    plane, cube, pairs = plane_bits(), cube_bits(), pair_count()

    chans = Channels(rec_width, seqs)
    width_r, span, span_blocks = chans.width, chans.span, chans.blocks
    base = chans.base(me_seq)
    cols = hidden_width // (pairs * seqs)

    mask_val = valid_mask.reshape(local_len).astype(fp32)
    own_count = jnp.sum(mask_val)
    count_high = jnp.floor(own_count / 128.0)
    count_pair = jnp.stack([count_high, own_count - 128.0 * count_high]).astype(half)

    def row_of(value):
        return jnp.pad(value, ((0, 0), (0, 2 * BW - value.shape[1])))

    block_rows = -(-rows_c // 16) * 16
    package = jnp.concatenate(
        [
            jnp.pad(
                jnp.concatenate([gate_rec_w, gate_inp_w], axis=1),
                ((0, block_rows - rows_c), (0, 0)),
            ),
            row_of(conv_taps),
            row_of(jnp.stack([conv_bias, gate_rec_b, gate_inp_b, rec_param])),
            row_of(jnp.stack([norm_one, norm_two])),
            row_of(count_pair[None, :]),
            jnp.zeros((5, 2 * BW), half),
        ],
        axis=0,
    )
    w_in, w_out, mlp_own, shared, tokens_all = opening(
        chans,
        {"rec": proj_rec, "gelu": proj_gelu, "out": proj_out.T},
        [mlp_gate, mlp_up, mlp_down.T],
        package,
        tokens.reshape(local_len, model),
        1,
    )
    shared = shared.reshape(everyone, *package.shape)
    w_in, w_out = w_in.reshape(model, span + width_r), w_out.reshape(model, width_r)
    w_mlp = share_gather(mlp_own, "dp").reshape(model, 3 * cols)
    w_two, w_down = w_mlp[:, : 2 * cols], w_mlp[:, 2 * cols :]
    vectors = shared[:, block_rows:].astype(fp32)
    channel_vecs = vectors[:, : CONV + 4, :rows_c].transpose(1, 0, 2).reshape(CONV + 4, rec_width)
    gains = vectors[:, CONV + 4 : CONV + 6, :rows_w].transpose(1, 0, 2).reshape(2, model)
    counts = jnp.sum(vectors[:, CONV + 6, :2], axis=0)
    valid_total = 128.0 * counts[0] + counts[1]

    span_vecs = lax.dynamic_slice(channel_vecs, (0, base), (CONV + 4, span))
    tap_vals, bias_vals = span_vecs[:CONV], span_vecs[CONV]
    rec_bias, inp_bias, rec_vals = (
        chans.owned(span_vecs[CONV + 1 + i], me_seq) for i in range(3)
    )
    mine = chans.mine(me_seq)
    touched = min(everyone, -(-(span - 1) // rows_c) + 1)
    from_device = jnp.minimum(base // rows_c, everyone - touched)
    near = lax.dynamic_slice(shared, (from_device, 0, 0), (touched, rows_c, 2 * BW))
    span_mats = lax.dynamic_slice(
        near.reshape(touched * rows_c, 2 * BW), (base - from_device * rows_c, 0), (span, 2 * BW)
    )

    def block_diagonal(value):
        rows = []
        for place in range(span_blocks):
            block = value[place * BW : (place + 1) * BW]
            rows.append(jnp.pad(block, ((0, 0), (place * BW, (span_blocks - 1 - place) * BW))))
        return chans.owned(jnp.concatenate(rows, axis=0), me_seq)

    w_gates = jnp.concatenate(
        [block_diagonal(span_mats[:, :BW]), block_diagonal(span_mats[:, BW:])], axis=1
    )
    gain_one, gain_two = gains[0], gains[1]

    flat_in = tokens.reshape(local_len, model).astype(fp32)
    tokens_all = tokens_all.reshape(steps, model).astype(fp32)
    normed_all = lax.optimization_barrier(rms_norm(tokens_all, gain_one).astype(half))
    pre = times(normed_all, w_in)
    rec_pre, gelu_pre = chans.rec_of(pre)
    padded = jnp.concatenate([jnp.zeros((CONV - 1, span), fp32), rec_pre], axis=0)
    conv_sum = bias_vals + jnp.zeros_like(rec_pre)
    for offset in range(CONV):
        conv_sum = conv_sum + tap_vals[offset] * padded[CONV - 1 - offset : CONV - 1 - offset + steps]
    conv_low = conv_sum.astype(half)
    conv_val = chans.owned(conv_low, me_seq).astype(fp32)
    gates = times(conv_low, w_gates)
    gate_rec = gates[:, :width_r] + rec_bias
    gate_inp = gates[:, width_r:] + inp_bias
    decays, drives = gate_terms(gate_rec, gate_inp, conv_val, rec_vals)
    states = time_scan(True, decays, drives)
    mixed_low = jnp.where(mine, gelu_product(gelu_pre, states), 0.0).astype(half)
    mixed_part = part_of_sum(mixed_low, w_out).reshape(seqs, local_len, model)
    middle = flat_in + scatter_sum(mixed_part, plane, 3)

    normed_two_low = rms_norm(middle, gain_two).astype(half)
    group = pairs * seqs
    tall = group * local_len
    normed_two_all = gather(normed_two_low, cube, 4).reshape(tall, model)
    pre_two = times(normed_two_all, w_two)
    gate_pre, up_pre = pre_two[:, :cols], pre_two[:, cols:]
    hidden_low = gelu_product(gate_pre, up_pre).astype(half)
    down_part = part_of_sum(hidden_low, w_down).reshape(group, local_len, model)
    result = middle + scatter_sum(down_part, cube, 5)
    differ = result - teacher.reshape(local_len, model).astype(fp32)
    own_loss = 0.5 * jnp.sum(mask_val[:, None] * differ * differ)
    token_total = local_len * everyone
    grad_result = mask_val[:, None] * (token_total / valid_total) * differ
    output = result.reshape(tokens.shape).astype(half)

    down_all = gather(grad_result.astype(half), cube, 6).reshape(tall, model)
    grad_down = contract_rows(down_all, hidden_low)
    grad_hidden = times(down_all, w_down)
    _, pull_mlp = jax.vjp(gelu_product, gate_pre, up_pre)
    two_low = jnp.concatenate(pull_mlp(grad_hidden), axis=1).astype(half)
    grad_two = contract_rows(normed_two_all, two_low)
    two_part = part_of_sum(two_low, w_two).reshape(group, local_len, model)

    grad_normed_two = scatter_sum(two_part, cube, 7)
    grad_normed_two, grad_two, grad_down = lax.optimization_barrier(
        (grad_normed_two, grad_two, grad_down)
    )
    grad_mlp = jnp.concatenate([grad_two, grad_down], axis=1).astype(half)
    sent_mlp = share_scatter(grad_mlp.reshape(seqs, dps, rows_w, 3 * cols), "dp")

    _, pull_norm_two = jax.vjp(rms_norm, middle, gain_two)
    grad_middle_norm, grad_norm_two = pull_norm_two(grad_normed_two)
    grad_middle = grad_result + grad_middle_norm

    middle_low = gather(grad_middle.astype(half), plane, 8).reshape(steps, model)
    grad_out = contract_rows(middle_low, mixed_low)
    grad_mixed = jnp.where(mine, times(middle_low, w_out), 0.0)
    _, pull_mix = jax.vjp(gelu_product, gelu_pre, states)
    grad_gelu_pre, grad_states = pull_mix(grad_mixed)
    adjoint = time_scan(False, decays, grad_states)
    prior_state = jnp.concatenate([jnp.zeros_like(states[:1]), states[:-1]], axis=0)
    _, pull_gates = jax.vjp(gate_terms, gate_rec, gate_inp, conv_val, rec_vals)
    grad_rec_gate, grad_inp_gate, grad_conv_direct, grad_rec_param = pull_gates(
        (adjoint * prior_state, adjoint)
    )
    gates_low = jnp.concatenate([grad_rec_gate, grad_inp_gate], axis=1).astype(half)
    grad_gate_bias = jnp.sum(gates_low.astype(fp32), axis=0)
    grad_gates = contract_rows(conv_low, gates_low)
    grad_conv = times_trans(gates_low, w_gates) + chans.widened(grad_conv_direct, me_seq)
    grad_conv_bias = jnp.sum(grad_conv, axis=0)
    ahead = jnp.concatenate([grad_conv, jnp.zeros((CONV - 1, span), fp32)], axis=0)
    tap_grads = []
    rec_back = jnp.zeros_like(grad_conv)
    for offset in range(CONV):
        window = padded[CONV - 1 - offset : CONV - 1 - offset + steps]
        tap_grads.append(jnp.sum(grad_conv * window, axis=0))
        rec_back = rec_back + tap_vals[offset] * ahead[offset : offset + steps]
    rec_low = rec_back.astype(half)
    in_low = jnp.concatenate(
        [rec_low[:, :BW], grad_gelu_pre.astype(half), rec_low[:, BW:]], axis=1
    )
    grad_in = contract_rows(normed_all, in_low)
    in_part = part_of_sum(in_low, w_in).reshape(seqs, local_len, model)
    grad_norm_one = jnp.sum(w_in.astype(fp32) * grad_in, axis=1) / gain_one

    def spread(value):
        return lax.dynamic_update_slice(
            jnp.zeros((value.shape[0], rec_width), fp32), value, (0, base)
        )

    def diagonal_blocks(value):
        wide = chans.widened(value, me_seq)
        block = lax.broadcasted_iota(jnp.int32, (span, BW), 0) // BW
        picked = wide[:, :BW]
        for i in range(1, span_blocks):
            picked = jnp.where(block == i, wide[:, i * BW : (i + 1) * BW], picked)
        return picked

    mats = jnp.concatenate(
        [diagonal_blocks(grad_gates[:, :width_r]), diagonal_blocks(grad_gates[:, width_r:])], axis=1
    )
    mats = lax.dynamic_update_slice(jnp.zeros((rec_width, 2 * BW), fp32), mats, (base, 0))
    mats = jnp.pad(
        mats.reshape(everyone, rows_c, 2 * BW), ((0, 0), (0, block_rows - rows_c), (0, 0))
    )

    def widen(value):
        return chans.widened(value[None, :], me_seq)

    lines = jnp.concatenate(
        [
            jnp.stack(tap_grads),
            grad_conv_bias[None, :],
            widen(grad_gate_bias[:width_r]),
            widen(grad_gate_bias[width_r:]),
            widen(grad_rec_param),
        ],
        axis=0,
    )
    lines = spread(lines).reshape(CONV + 4, everyone, rows_c).transpose(1, 0, 2)
    gain_lines = jnp.stack([grad_norm_one, grad_norm_two]).reshape(2, everyone, rows_w)
    gain_lines = gain_lines.transpose(1, 0, 2)

    def lane_pad(value):
        return jnp.pad(value, ((0, 0), (0, 0), (0, LANES - value.shape[2])))

    small = jnp.concatenate(
        [
            lane_pad(lines),
            lane_pad(gain_lines),
            jnp.full((everyone, 1, LANES), own_loss),
            jnp.zeros((everyone, 5, LANES), fp32),
        ],
        axis=1,
    )
    grad_normed, backs, out_gate, out_up, out_down, mats, small = closing(
        chans,
        in_part,
        grad_in.reshape(seqs, dps, rows_w, span + width_r),
        grad_out.reshape(seqs, dps, rows_w, width_r),
        sent_mlp,
        mats.astype(half).reshape(seqs, -1, 2 * BW),
        small.reshape(seqs, -1, LANES),
        2,
    )
    mean_loss = small[CONV + 6, 0] / (valid_total * model)

    _, pull_norm_one = jax.vjp(lambda values: rms_norm(values, gain_one), flat_in)
    grad_tokens = (grad_middle + pull_norm_one(grad_normed)[0]).reshape(tokens.shape).astype(half)

    block_of = lax.broadcasted_iota(jnp.int32, (1, rec_width), 1) // BW

    def layer_sum(at, blocks):
        has = functools.reduce(jnp.logical_or, [block_of == block for block in sorted(blocks)])
        return jnp.where(has, backs["rec"][at].astype(fp32), 0.0)

    out_gate, out_up = out_gate.astype(fp32), out_up.astype(fp32)
    out_down = out_down.T.astype(fp32)
    out_proj_out = backs["out"].T.astype(fp32)
    out_proj_gelu = backs["gelu"].astype(fp32)
    layers = [layer_sum(at, blocks) for at, blocks in enumerate(chans.taken)]
    out_proj_rec = functools.reduce(jnp.add, layers)

    return (
        output,
        mean_loss,
        grad_tokens,
        small[CONV + 4, :rows_w],
        out_proj_gelu,
        out_proj_rec,
        small[:CONV, :rows_c],
        small[CONV, :rows_c],
        mats[:rows_c, :BW],
        small[CONV + 1, :rows_c],
        mats[:rows_c, BW:],
        small[CONV + 2, :rows_c],
        small[CONV + 3, :rows_c],
        out_proj_out,
        small[CONV + 5, :rows_w],
        out_gate,
        out_up,
        out_down,
    )


def solution(mesh):
    both = ("seq", "dp")
    rows, cols, flat = P(both, None), P(None, both), P(both)
    acts = P("dp", "seq", None)
    in_specs = (
        acts,
        P("dp", "seq"),
        acts,
        flat,
        rows,
        rows,
        cols,
        flat,
        rows,
        flat,
        rows,
        flat,
        flat,
        cols,
        flat,
        rows,
        rows,
        cols,
    )
    out_specs = (
        acts,
        P(),
        acts,
        flat,
        rows,
        rows,
        cols,
        flat,
        rows,
        flat,
        rows,
        flat,
        flat,
        cols,
        flat,
        rows,
        rows,
        cols,
    )
    return jax.shard_map(
        on_device, mesh=mesh, in_specs=in_specs, out_specs=out_specs, check_vma=False
    )
```

```python
import functools
import itertools

import jax
import jax.numpy as jnp
from jax import lax
from jax.experimental import pallas as pl
from jax.experimental.pallas import tpu as pltpu
from jax.sharding import PartitionSpec as P

NB = 10
BW = 256
CONV = 4
LANES = 128
MLPS = 3

norm_eps = 1e-06
gate_power = 8.0
floor_square = 0.0001

fp32 = jnp.float32
half = jnp.bfloat16


def flip(index, mask):
    return index + mask - 2 * mask * ((index // mask) % 2)


def bit_values(bits):
    return [(lax.axis_index(axis) // mask) % 2 for axis, mask, _ in bits]


def slot_number(bits, vals, flipped):
    total = 0
    for place, (_, _, weight) in enumerate(bits):
        total = total + weight * (1 - vals[place] if place in flipped else vals[place])
    return total


def partner(bit):
    axis, mask, _ = bit
    return {axis: flip(lax.axis_index(axis), mask)}


def greet(bits):
    barrier = pltpu.get_barrier_semaphore()
    for bit in bits:
        pl.semaphore_signal(
            barrier, inc=1, device_id=partner(bit), device_id_type=pl.DeviceIdType.MESH
        )
    pl.semaphore_wait(barrier, len(bits))


def masks_of(size):
    return [2**place for place in reversed(range(size.bit_length() - 1))]


def plane_bits():
    return tuple(("seq", mask, mask) for mask in masks_of(lax.axis_size("seq")))


def pair_count():
    return 2 if lax.axis_size("dp") > 1 and 2 * lax.axis_size("seq") <= 16 else 1


def cube_bits():
    pair = (("dp", 1, lax.axis_size("seq")),) if pair_count() == 2 else ()
    return (*pair, *plane_bits())


def world_bits():
    dps = lax.axis_size("dp")
    return tuple(("dp", mask, mask) for mask in masks_of(dps)) + tuple(
        ("seq", mask, mask * dps) for mask in masks_of(lax.axis_size("seq"))
    )


def subsets(items):
    for size in range(len(items) + 1):
        yield from itertools.combinations(items, size)


def splits(width, count):
    tiles = width // LANES
    if tiles * LANES != width or tiles < count:
        return [(0, width)]
    cuts = [tiles * i // count * LANES for i in range(count + 1)]
    return [(cuts[i], cuts[i + 1] - cuts[i]) for i in range(count)]


def rotations(bits, width, fixed=0):
    begin, slow, last = list(range(fixed)), list(range(fixed, len(bits) - 1)), [len(bits) - 1]
    pieces = splits(width, len(slow))
    return [
        (first, size, tuple(begin + slow[turn:] + slow[:turn] + last))
        for turn, (first, size) in enumerate(pieces)
    ]


class Gathering:
    def __init__(self, bits, width, x_ref, o_ref, sems, fixed=0):
        self.bits, self.x_ref, self.o_ref = bits, x_ref, o_ref
        self.send_sems, self.recv_sems, self.local_sem = sems
        self.vals = bit_values(bits)
        self.parts = rotations(bits, width, fixed)
        self.numbers = {}
        for which in range(len(self.parts)):
            for stage in range(len(bits)):
                for held in subsets(range(stage)):
                    self.numbers[which, stage, held] = len(self.numbers)

    @staticmethod
    def semaphores(bits, width, fixed=0):
        copies = len(rotations(bits, width, fixed)) * (2 ** len(bits) - 1)
        return [
            pltpu.SemaphoreType.DMA((copies,)),
            pltpu.SemaphoreType.DMA((copies,)),
            pltpu.SemaphoreType.DMA,
        ]

    def own(self):
        slot = slot_number(self.bits, self.vals, ())
        return pltpu.make_async_copy(self.x_ref, self.o_ref.at[slot], self.local_sem)

    def transfer(self, which, stage, held):
        first, width, order = self.parts[which]
        cols = pl.ds(first, width)
        slot = slot_number(self.bits, self.vals, [order[place] for place in held])
        dst = self.o_ref.at[slot, :, cols]
        number = self.numbers[which, stage, held]
        in_place = held or self.x_ref is None
        return pltpu.make_async_remote_copy(
            src_ref=dst if in_place else self.x_ref.at[:, cols],
            dst_ref=dst,
            send_sem=self.send_sems.at[number],
            recv_sem=self.recv_sems.at[number],
            device_id=partner(self.bits[order[stage]]),
            device_id_type=pl.DeviceIdType.MESH,
        )

    def begin(self):
        if self.x_ref is not None:
            self.own().start()
        for stage in range(len(self.bits)):
            for which in range(len(self.parts)):
                self.transfer(which, stage, ()).start()

    def level(self, size):
        depth = len(self.bits)
        for held in itertools.combinations(range(depth), size):
            for which in range(len(self.parts)):
                self.transfer(which, held[-1], held[:-1]).wait_recv()
                for stage in range(held[-1] + 1, depth):
                    self.transfer(which, stage, held).start()

    def finish(self):
        for key in self.numbers:
            self.transfer(*key).wait_send()
        if self.x_ref is not None:
            self.own().wait()


class Fan:
    def __init__(self, source, target, sems):
        self.source, self.target = source, target
        self.send, self.recv = sems
        self.me, self.count = lax.axis_index("dp"), lax.axis_size("dp")

    @staticmethod
    def semaphores(count):
        return [pltpu.SemaphoreType.DMA((count,)), pltpu.SemaphoreType.DMA((count,))]

    def going(self, step):
        to = lax.rem(self.me + step, self.count)
        return remote(
            self.source(to), self.target(self.me), self.send.at[step], self.recv.at[step], {"dp": to}
        )

    def arriving(self, step):
        block = self.target(lax.rem(self.me - step + self.count, self.count))
        return remote(block, block, self.send.at[step], self.recv.at[step], {"dp": self.me})


class Scattering:
    def __init__(self, bits, x_ref, o_ref, scratch, fixed=0):
        self.bits, self.x_ref, self.o_ref = bits, x_ref, o_ref
        self.held, self.outgoing, self.incoming, self.load, self.send, self.recv = scratch
        self.rows, width = o_ref.shape
        self.chunk = 32 if self.rows % 32 == 0 else 16
        self.parts = [(at, size, order[::-1]) for at, size, order in rotations(bits, width, fixed)]
        self.vals = bit_values(bits)
        self.depth = len(bits)
        first_bit = self.parts[0][2][0]
        self.blocks = sorted(subsets(range(self.depth)), key=lambda s: (first_bit not in s, -len(s)))
        self.slots, self.numbers = {}, {}
        for stage in range(self.depth):
            for rest in subsets(range(stage + 1, self.depth)):
                self.slots[stage, rest] = len(self.slots)
        for which in range(len(self.parts)):
            for key in self.slots:
                self.numbers[(which, *key)] = len(self.numbers)
        self.loaded = set()

    @staticmethod
    def scratch(bits, value, wire, fixed=0):
        count, rows, width = value.shape
        copies = len(rotations(bits, width, fixed)) * (count - 1)
        return [
            pltpu.VMEM((count, rows, width), value.dtype),
            pltpu.VMEM((count - 1, rows, width), wire),
            pltpu.VMEM((count - 1, rows, width), wire),
            pltpu.SemaphoreType.DMA((count,)),
            pltpu.SemaphoreType.DMA((copies,)),
            pltpu.SemaphoreType.DMA((copies,)),
        ]

    def loading(self, members):
        key = sum(2**place for place in members)
        slot = slot_number(self.bits, self.vals, members)
        return pltpu.make_async_copy(self.x_ref.at[slot], self.held.at[key], self.load.at[key])

    def begin(self):
        for members in self.blocks:
            self.loading(members).start()

    def ready(self, members):
        key = sum(2**place for place in members)
        if key not in self.loaded:
            self.loaded.add(key)
            self.loading(members).wait()
        return key

    def transfer(self, which, stage, rest):
        first, width, order = self.parts[which]
        place = self.slots[stage, rest]
        number = self.numbers[which, stage, rest]
        return pltpu.make_async_remote_copy(
            src_ref=self.outgoing.at[place, :, pl.ds(first, width)],
            dst_ref=self.incoming.at[place, :, pl.ds(first, width)],
            send_sem=self.send.at[number],
            recv_sem=self.recv.at[number],
            device_id=partner(self.bits[order[stage]]),
            device_id_type=pl.DeviceIdType.MESH,
        )

    def add_up(self, which, key, arrived, store):
        first, width, _ = self.parts[which]
        cols = pl.ds(first, width)

        def body(step, carry):
            lines = pl.ds(pl.multiple_of(step * self.chunk, self.chunk), self.chunk)
            total = self.held[key, lines, cols].astype(fp32)
            for place in arrived:
                total = total + self.incoming[place, lines, cols].astype(fp32)
            store(lines, cols, total)
            return carry

        lax.fori_loop(0, self.rows // self.chunk, body, 0)

    def stage(self, stage):
        for rest in sorted(subsets(range(stage + 1, self.depth)), key=lambda s: (-len(s), s)):
            for which, (_, _, order) in enumerate(self.parts):
                going = (stage, *rest)
                key = self.ready([order[place] for place in going])
                for earlier in range(stage):
                    self.transfer(which, earlier, going).wait_recv()
                place = self.slots[stage, rest]

                def keep(lines, cols, total, place=place):
                    self.outgoing[place, lines, cols] = total.astype(self.outgoing.dtype)

                arrived = [self.slots[earlier, going] for earlier in range(stage)]
                self.add_up(which, key, arrived, keep)
                self.transfer(which, stage, rest).start()

    def finish(self):
        def keep(lines, cols, total):
            self.o_ref[lines, cols] = total

        key = self.ready(())
        for which in range(len(self.parts)):
            for stage in range(self.depth):
                self.transfer(which, stage, ()).wait_recv()
            self.add_up(which, key, [self.slots[stage, ()] for stage in range(self.depth)], keep)

    def close(self):
        for members in self.blocks:
            self.ready(members)
        for key in self.numbers:
            self.transfer(*key).wait_send()


def gather(value, bits, number, fixed=0):
    rows, width = value.shape

    def kernel(x_ref, o_ref, *sems):
        work = Gathering(bits, width, x_ref, o_ref, sems, fixed)
        greet(bits)
        work.begin()
        for size in range(1, len(bits) + 1):
            work.level(size)
        work.finish()

    return pl.pallas_call(
        kernel,
        out_shape=jax.ShapeDtypeStruct((2 ** len(bits), rows, width), value.dtype),
        in_specs=[pl.BlockSpec(memory_space=pltpu.VMEM)],
        out_specs=pl.BlockSpec(memory_space=pl.ANY),
        scratch_shapes=Gathering.semaphores(bits, width, fixed),
        compiler_params=pltpu.CompilerParams(collective_id=number, has_side_effects=True),
        name=f"gather_{number}",
    )(value)


def scatter_sum(value, bits, number, fixed=0):
    _, rows, width = value.shape

    def kernel(x_ref, o_ref, *scratch):
        work = Scattering(bits, x_ref, o_ref, scratch, fixed)
        work.begin()
        greet(bits)
        for stage in range(len(bits)):
            work.stage(stage)
        work.finish()
        work.close()

    return pl.pallas_call(
        kernel,
        out_shape=jax.ShapeDtypeStruct((rows, width), fp32),
        in_specs=[pl.BlockSpec(memory_space=pl.ANY)],
        out_specs=pl.BlockSpec(memory_space=pltpu.VMEM),
        scratch_shapes=Scattering.scratch(bits, value, half, fixed),
        compiler_params=pltpu.CompilerParams(
            collective_id=number, has_side_effects=True, vmem_limit_bytes=60 * 2**20
        ),
        name=f"scatter_{number}",
    )(value)


def remote(src, dst, send_sem, recv_sem, device):
    return pltpu.make_async_remote_copy(
        src_ref=src,
        dst_ref=dst,
        send_sem=send_sem,
        recv_sem=recv_sem,
        device_id=device,
        device_id_type=pl.DeviceIdType.MESH,
    )


class Exchange:
    def __init__(self, pieces, sems, across=False):
        self.pieces = [(*piece, None, None)[:4] for piece in pieces]
        self.send, self.recv, self.local = sems
        self.me, self.count = lax.axis_index("seq"), lax.axis_size("seq")
        self.other = {"dp": flip(lax.axis_index("dp"), 1)} if across else {}
        self.across = across

    @staticmethod
    def semaphores(pieces, count):
        return [
            pltpu.SemaphoreType.DMA((pieces, count)),
            pltpu.SemaphoreType.DMA((pieces, count)),
            pltpu.SemaphoreType.DMA((pieces,)),
        ]

    @staticmethod
    def where(needed, place, action):
        if needed is None:
            action()
        else:
            pl.when(needed(place))(action)

    def own(self, which):
        source, target = self.pieces[which][:2]
        return pltpu.make_async_copy(source(self.me), target(self.me), self.local.at[which])

    def each_own(self, action):
        for which, piece in enumerate(self.pieces):
            self.where(piece[3], self.me, lambda which=which: action(self.own(which)))

    def start_own(self):
        self.each_own(lambda copy: copy.start())

    def wait_own(self):
        self.each_own(lambda copy: copy.wait())

    def going(self, which, step):
        to = lax.rem(self.me + step, self.count)
        source, target = self.pieces[which][:2]
        return remote(
            source(to),
            target(self.me),
            self.send.at[which, step],
            self.recv.at[which, step],
            {"seq": to, **self.other},
        )

    def origin(self, step):
        return lax.rem(self.me - step + self.count, self.count)

    def each_going(self, step, action):
        to = lax.rem(self.me + step, self.count)
        for which, piece in enumerate(self.pieces):
            self.where(piece[3], to, lambda which=which: action(self.going(which, step)))

    def start(self, step):
        self.each_going(step, lambda copy: copy.start())

    def wait_sent(self, step):
        self.each_going(step, lambda copy: copy.wait_send())

    def wait_arrived(self, step):
        for which, (_, target, arrival, needed) in enumerate(self.pieces):
            block = (arrival or target)(self.origin(step))

            def wait(which=which, block=block):
                remote(
                    block,
                    block,
                    self.send.at[which, step],
                    self.recv.at[which, step],
                    {"seq": self.me},
                ).wait_recv()

            self.where(needed, self.me, wait)


class Channels:
    def __init__(self, width, places):
        tiles = width // LANES
        if places == 8 and tiles == 20:
            half_starts, half_counts = [0, 4, 2, 7], [2, 3, 2, 3]
            self.starts = half_starts + [start + 10 for start in half_starts]
            self.counts = half_counts * 2
        else:
            cuts = [tiles * i // places for i in range(places + 1)]
            self.starts = cuts[:places]
            self.counts = [cuts[i + 1] - cuts[i] for i in range(places)]
        self.places, self.total = places, width
        self.tiles = max(self.counts)
        self.width = self.tiles * LANES
        self.least = self.width - LANES
        per_block = BW // LANES
        lasts = [start + count - 1 for start, count in zip(self.starts, self.counts)]
        reach = [last // per_block - start // per_block + 1 for start, last in zip(self.starts, lasts)]
        self.blocks = max(reach)
        self.span = self.blocks * BW
        firsts = [min(start // per_block, NB - self.blocks) for start in self.starts]
        self.bases = [first * BW for first in firsts]
        self.full = [
            count == self.tiles or last // per_block > first
            for count, last, first in zip(self.counts, lasts, firsts)
        ]
        assert self.full == [count == self.tiles for count in self.counts]
        self.layer, taken = {}, []
        for part in range(2):
            for i in range(places):
                if part and not self.full[i]:
                    self.layer[i, part] = 0
                    continue
                held = {firsts[i]} if part == 0 else set(range(firsts[i] + 1, firsts[i] + self.blocks))
                free = [at for at, blocks in enumerate(taken) if not blocks & held]
                if not free:
                    free = [len(taken)]
                    taken.append(set())
                self.layer[i, part] = free[0]
                taken[free[0]] |= held
        self.taken = taken
        self.shifts = [start * LANES - base for start, base in zip(self.starts, self.bases)]
        assert all(shift + self.width <= self.span for shift in self.shifts)
        self.common = self.least + BW + self.least
        self.lanes = 2 * self.width + self.span

    def pick(self, table, place):
        out = table[0]
        for i in range(1, self.places):
            out = jnp.where(place == i, int(table[i]), out)
        return out

    def begin(self, place):
        return self.pick([start * LANES for start in self.starts], place)

    def base(self, place):
        return self.pick(self.bases, place)

    def layer_of(self, part, place):
        return self.pick([self.layer[i, part] for i in range(self.places)], place)

    def is_full(self, place):
        return self.pick([int(full) for full in self.full], place) == 1

    def owned(self, value, place):
        choices = sorted(set(self.shifts))
        shift = self.pick(self.shifts, place)
        out = value[..., choices[0] : choices[0] + self.width]
        for at in choices[1:]:
            out = jnp.where(shift == at, value[..., at : at + self.width], out)
        return out

    def widened(self, value, place):
        lead = [(0, 0)] * (value.ndim - 1)
        choices = sorted(set(self.shifts))
        shift = self.pick(self.shifts, place)
        out = jnp.pad(value, (*lead, (choices[0], self.span - self.width - choices[0])))
        for at in choices[1:]:
            padded = jnp.pad(value, (*lead, (at, self.span - self.width - at)))
            out = jnp.where(shift == at, padded, out)
        return out

    def mine(self, place):
        count = self.pick(self.counts, place)
        return lax.broadcasted_iota(jnp.int32, (1, self.width), 1) < count * LANES

    def place_in(self, at):
        if at < self.least:
            return "out", at
        if at >= self.lanes - LANES:
            return "out", at - (self.lanes - LANES) + self.least
        return "in", at - self.least

    def line_parts(self):
        common, inputs = self.common - self.least, self.span + self.width
        return [
            ("in", pl.ds(0, common), False),
            ("out", pl.ds(0, self.least), False),
            ("in", pl.ds(common, inputs - common), True),
            ("out", pl.ds(self.least, LANES), True),
        ]

    def rec_of(self, value):
        rec = jnp.concatenate([value[..., :BW], value[..., BW + self.width :]], axis=-1)
        return rec, value[..., BW : BW + self.width]

    def routes(self):
        least, common = self.least, self.common
        return [
            ("out", 0, least, 0, False),
            ("rec", 0, BW, least, False),
            ("gelu", 0, least, least + BW, False),
            ("gelu", least, LANES, common, True),
            ("rec", BW, self.span - BW, common + LANES, True),
            ("out", least, LANES, self.lanes - LANES, True),
        ]


def lanes(start, width):
    return pl.ds(pl.multiple_of(start, LANES) if width % LANES == 0 else start, width)


def opening(chans, arrays, mlps, package, tokens, number):
    seqs, dps, pairs = lax.axis_size("seq"), lax.axis_size("dp"), pair_count()
    plane = plane_bits()
    names = sorted(arrays)
    rows, lines = arrays["rec"].shape[0], package.shape[0]
    cols = mlps[0].shape[1] // (pairs * seqs)
    routes = chans.routes()
    parts = chans.line_parts()
    piece_counts = [len(routes), len(mlps), len(mlps)]
    x_sems = len(Exchange.semaphores(1, seqs))

    def kernel(*refs):
        array_refs, refs = dict(zip(names, refs)), refs[len(names) :]
        mlp_refs, refs = refs[: len(mlps)], refs[len(mlps) :]
        package_ref, tokens_ref, refs = refs[0], refs[1], refs[2:]
        fulls, refs = dict(zip(("in", "out"), refs)), refs[2:]
        mlp_all, shared_all, tokens_all, refs = *refs[:3], refs[3:]
        exchange_sems = [refs[x_sems * i : x_sems * (i + 1)] for i in range(3)]
        refs = refs[3 * x_sems :]
        line_send, line_recv, zeros, zero_sem, refs = *refs[:4], refs[4:]
        me_s, me_d = lax.axis_index("seq"), lax.axis_index("dp")
        is_full = chans.is_full(me_s)

        def route(name, skip, width, at, optional):
            def source(to):
                begin = chans.base(to) if name == "rec" else chans.begin(to)
                return array_refs[name].at[:, lanes(begin + skip, width)]

            which, inside = chans.place_in(at)
            target = lambda origin: fulls[which].at[origin, me_d, :, pl.ds(inside, width)]
            return source, target, target, chans.is_full if optional else None

        move = Exchange([route(*entry) for entry in routes], exchange_sems[0])
        low = lax.rem(me_d, pairs)

        def mlp_piece(which, target_low, here, there):
            return (
                lambda to: mlp_refs[which].at[:, lanes((to * pairs + target_low) * cols, cols)],
                lambda origin: mlp_all.at[origin, here, :, pl.ds(which * cols, cols)],
                lambda origin: mlp_all.at[origin, there, :, pl.ds(which * cols, cols)],
            )

        mlp_moves = [
            Exchange([mlp_piece(which, low, low, low) for which in range(len(mlps))], exchange_sems[1])
        ]
        if pairs == 2:
            mlp_moves.append(
                Exchange(
                    [mlp_piece(which, 1 - low, low, 1 - low) for which in range(len(mlps))],
                    exchange_sems[2],
                    across=True,
                )
            )
        shared = Gathering(plane, package.shape[1], None, shared_all, refs[:3])
        toks = Gathering(plane, tokens.shape[1], tokens_ref, tokens_all, refs[3:6])

        def package_slot(origin):
            return shared_all.at[me_s, pl.ds(pl.multiple_of(origin * lines, 16), lines), :]

        fan = Fan(lambda to: package_ref, package_slot, refs[6:8])
        package_own = pltpu.make_async_copy(package_ref, package_slot(me_d), refs[8])

        def greeted():
            barrier = pltpu.get_barrier_semaphore()
            targets = [{"seq": lax.rem(me_s + step, seqs)} for step in range(1, seqs)]
            targets += [{"dp": lax.rem(me_d + step, dps)} for step in range(1, dps)]
            if pairs == 2:
                targets += [
                    {"seq": lax.rem(me_s + step, seqs), "dp": flip(me_d, 1)}
                    for step in range(1, seqs)
                ]
            for target in targets:
                pl.semaphore_signal(
                    barrier, inc=1, device_id=target, device_id_type=pl.DeviceIdType.MESH
                )
            pl.semaphore_wait(barrier, len(targets))

        greeted()
        package_own.start()
        for step in range(1, dps):
            fan.going(step).start()
        move.start_own()
        for step in range(1, seqs):
            move.start(step)
        optional_parts = [(which, cut) for which, cut, optional in parts if optional]
        blanks = [
            pltpu.make_async_copy(
                zeros.at[:, :, :, pl.ds(0, cut.size)], fulls[which].at[:, :, :, cut], zero_sem.at[i]
            )
            for i, (which, cut) in enumerate(optional_parts)
        ]

        @pl.when(jnp.logical_not(is_full))
        def _():
            zeros[...] = jnp.zeros_like(zeros)
            for blank in blanks:
                blank.start()

        def line_copy(way, part, hop, step, number):
            sign = 1 if way == 0 else -1
            origin = jnp.clip(me_d - sign * hop, 0, dps - 1)
            which, cut, _ = parts[part]
            block = fulls[which].at[move.origin(step), origin, :, cut]
            return remote(
                block,
                block,
                line_send.at[2 * part + way, number, step],
                line_recv.at[2 * part + way, number, step],
                {"dp": jnp.clip(me_d + sign, 0, dps - 1)},
            )

        def has_next(way):
            return me_d < dps - 1 if way == 0 else me_d > 0

        def has_origin(way, hop):
            return me_d >= hop if way == 0 else me_d < dps - hop

        def each_line(test, action):
            for part, (_, _, optional) in enumerate(parts):
                for way in range(2):
                    condition = test(way)
                    if optional:
                        condition = condition & is_full
                    pl.when(condition)(lambda way=way, part=part: action(way, part))

        def pass_on(hop, step):
            each_line(
                lambda way: has_next(way) & has_origin(way, hop),
                lambda way, part: line_copy(way, part, hop, step, hop).start(),
            )

        move.wait_own()
        pass_on(0, 0)

        def first_round(step, carry):
            move.wait_arrived(step)
            pass_on(0, step)
            return carry

        lax.fori_loop(1, seqs, first_round, 0)
        package_own.wait()
        for step in range(1, dps):
            fan.arriving(step).wait_recv()
        shared.begin()
        levels = range(1, len(plane) + 1)
        for size in levels:
            shared.level(size)
        mlp_moves[0].start_own()
        for step in range(1, seqs):
            mlp_moves[0].start(step)
        toks.begin()
        if dps == 1:
            assert pairs == 1
        for hop in range(1, dps):

            def round_of(step, carry, hop=hop):
                each_line(
                    lambda way: has_origin(way, hop),
                    lambda way, part: line_copy(way, part, hop, step, hop - 1).wait_recv(),
                )
                if hop < dps - 1:
                    pass_on(hop, step)
                return carry

            lax.fori_loop(0, seqs, round_of, 0)
            if hop == 1 and pairs == 2:
                for step in range(seqs):
                    mlp_moves[1].start(step)
            if hop == min(2, dps - 1):
                for size in levels:
                    toks.level(size)

        def last_round(step, carry):
            move.wait_sent(step)
            for mlp_move in mlp_moves:
                mlp_move.wait_sent(step)
                mlp_move.wait_arrived(step)
            return carry

        lax.fori_loop(1, seqs, last_round, 0)
        mlp_moves[0].wait_own()
        if pairs == 2:
            mlp_moves[1].wait_sent(0)
            mlp_moves[1].wait_arrived(0)

        def close_round(step, carry):
            for hop in range(dps - 1):
                each_line(
                    lambda way: has_next(way) & has_origin(way, hop),
                    lambda way, part: line_copy(way, part, hop, step, hop).wait_send(),
                )
            return carry

        lax.fori_loop(0, seqs, close_round, 0)
        for step in range(1, dps):
            fan.going(step).wait_send()

        @pl.when(jnp.logical_not(is_full))
        def _():
            for blank in blanks:
                blank.wait()

        shared.finish()
        toks.finish()

    vmem, anywhere = pl.BlockSpec(memory_space=pltpu.VMEM), pl.BlockSpec(memory_space=pl.ANY)
    return pl.pallas_call(
        kernel,
        out_shape=[
            jax.ShapeDtypeStruct((seqs, dps, rows, chans.span + chans.width), half),
            jax.ShapeDtypeStruct((seqs, dps, rows, chans.width), half),
            jax.ShapeDtypeStruct((seqs, pairs, rows, len(mlps) * cols), half),
            jax.ShapeDtypeStruct((seqs, dps * lines, package.shape[1]), half),
            jax.ShapeDtypeStruct((seqs, *tokens.shape), half),
        ],
        in_specs=[anywhere] * (len(names) + len(mlps)) + [vmem] * 2,
        out_specs=[anywhere] * 5,
        scratch_shapes=[
            *itertools.chain.from_iterable(
                Exchange.semaphores(pieces, seqs) for pieces in piece_counts
            ),
            pltpu.SemaphoreType.DMA((2 * len(parts), max(dps - 1, 1), seqs)),
            pltpu.SemaphoreType.DMA((2 * len(parts), max(dps - 1, 1), seqs)),
            pltpu.VMEM((seqs, dps, rows, chans.span + LANES - BW), half),
            pltpu.SemaphoreType.DMA((len(parts),)),
            *Gathering.semaphores(plane, package.shape[1]),
            *Gathering.semaphores(plane, tokens.shape[1]),
            *Fan.semaphores(dps),
            pltpu.SemaphoreType.DMA,
        ],
        compiler_params=pltpu.CompilerParams(
            collective_id=number, has_side_effects=True, vmem_limit_bytes=63 * 2**20
        ),
        name="opening",
    )(*(arrays[name] for name in names), *mlps, package, tokens)


def closing(chans, in_part, grad_in, grad_out, mlp, mats, small, number):
    seqs, dps, pairs = lax.axis_size("seq"), lax.axis_size("dp"), pair_count()
    plane = plane_bits()
    rows = grad_in.shape[2]
    links = max(dps - 1, 1)
    cols = mlp.shape[3] // MLPS
    routes = chans.routes()
    names = sorted({route[0] for route in routes})
    wide = chans.total
    backs = {"rec": (len(chans.taken), rows, wide), "gelu": (rows, wide), "out": (rows, wide)}
    halves = [pl.ds(0, chans.common), pl.ds(chans.common, chans.lanes - chans.common)]
    piece_counts = [len(routes), MLPS, MLPS]
    x_sems = len(Exchange.semaphores(1, seqs))
    shape = jax.ShapeDtypeStruct
    shared = [(small, fp32), (mats, half)]
    jobs = [(plane, in_part, half), *((plane, value, wire) for value, wire in shared)]
    tall = [value.shape[1] // dps for value, _ in shared]
    s_count = len(Scattering.scratch(plane, in_part, half))

    def kernel(*refs):
        part_ref, in_ref, out_ref, mlp_ref, mats_ref, small_ref, refs = *refs[:6], refs[6:]
        part_out, refs = refs[0], refs[1:]
        back_refs, refs = dict(zip(names, refs)), refs[len(names) :]
        mlp_outs, refs = refs[:MLPS], refs[MLPS:]
        mats_out, small_out, refs = refs[0], refs[1], refs[2:]
        sums, outs, fans_out, fans_in = refs[:2], [small_out, mats_out], refs[2:4], refs[4:6]
        fan_sems, refs = [refs[6:8], refs[8:10]], refs[10:]
        works = []
        for (bits, _, _), x_ref, o_ref in zip(
            jobs, (part_ref, small_ref, mats_ref), (part_out, *sums)
        ):
            works.append(Scattering(bits, x_ref, o_ref, refs[:s_count]))
            refs = refs[s_count:]
        held, outgoing, incoming, totals, load, line_send, line_recv, refs = *refs[:7], refs[7:]
        exchange_sems = [refs[x_sems * i : x_sems * (i + 1)] for i in range(3)]
        me_s, me_d = lax.axis_index("seq"), lax.axis_index("dp")
        is_full = chans.is_full(me_s)

        def route(name, skip, width, at, optional):
            def target(origin):
                if name == "rec":
                    layer = chans.layer_of(int(skip > 0), origin)
                    return back_refs[name].at[layer, :, lanes(chans.base(origin) + skip, width)]
                return back_refs[name].at[:, lanes(chans.begin(origin) + skip, width)]

            return lambda to: totals.at[to, :, pl.ds(at, width)], target, None, optional

        low = lax.rem(me_d, pairs)

        class Owners(Exchange):
            def each_own(self, action):
                for which, piece in enumerate(self.pieces):
                    test = is_full if piece[3] else None
                    self.where(test, None, lambda which=which: action(self.own(which)))

            @staticmethod
            def where(test, place, action):
                if test is None:
                    action()
                else:
                    pl.when(test)(action)

            def each_going(self, step, action):
                for which, piece in enumerate(self.pieces):
                    test = is_full if piece[3] else None
                    self.where(test, None, lambda which=which: action(self.going(which, step)))

            def wait_arrived(self, step):
                origin = self.origin(step)
                for which, (_, target, _, optional) in enumerate(self.pieces):
                    block = target(origin)

                    def wait(which=which, block=block):
                        remote(
                            block,
                            block,
                            self.send.at[which, step],
                            self.recv.at[which, step],
                            {"seq": self.me},
                        ).wait_recv()

                    self.where(chans.is_full(origin) if optional else None, None, wait)

        move = Owners([route(*entry) for entry in routes], exchange_sems[0])

        def mlp_piece(which, source_low, here, there):
            def columns(origin, part):
                return mlp_outs[which].at[:, lanes((origin * pairs + part) * cols, cols)]

            return (
                lambda to: mlp_ref.at[to, source_low, :, pl.ds(which * cols, cols)],
                lambda origin: columns(origin, here),
                lambda origin: columns(origin, there),
            )

        mlp_moves = [
            Exchange([mlp_piece(which, low, low, low) for which in range(MLPS)], exchange_sems[1])
        ]
        if pairs == 2:
            mlp_moves.append(
                Exchange(
                    [mlp_piece(which, 1 - low, low, 1 - low) for which in range(MLPS)],
                    exchange_sems[2],
                    across=True,
                )
            )

        input_lanes = pl.ds(chans.least, chans.lanes - LANES - chans.least)
        out_lanes = [
            (pl.ds(0, chans.least), pl.ds(0, chans.least)),
            (pl.ds(chans.least, LANES), pl.ds(chans.lanes - LANES, LANES)),
        ]

        def loading(chunk):
            copies = [(in_ref.at[chunk], held.at[chunk, :, :, input_lanes])]
            copies += [
                (out_ref.at[chunk, :, :, source], held.at[chunk, :, :, target])
                for source, target in out_lanes
            ]
            return [
                pltpu.make_async_copy(source, target, load.at[which, chunk])
                for which, (source, target) in enumerate(copies)
            ]

        fans = [
            Fan(
                lambda to, ref=fans_out[i]: ref.at[to],
                lambda origin, ref=fans_in[i]: ref.at[origin],
                fan_sems[i],
            )
            for i in range(2)
        ]

        def fan_lines(which, block, line):
            chunk = 16
            return pl.ds(pl.multiple_of(block * tall[which] + line * chunk, chunk), chunk)

        def fan_send():
            for which in range(2):
                for step in range(1, dps):
                    to = lax.rem(me_d + step, dps)

                    def body(line, carry, which=which, to=to):
                        part = sums[which][fan_lines(which, to, line), :]
                        fans_out[which][to, fan_lines(which, 0, line), :] = part.astype(
                            fans_out[which].dtype
                        )
                        return carry

                    lax.fori_loop(0, tall[which] // 16, body, 0)
                    fans[which].going(step).start()

        def fan_total():
            for which in range(2):
                for step in range(1, dps):
                    fans[which].arriving(step).wait_recv()

                def body(line, carry, which=which):
                    total = sums[which][fan_lines(which, me_d, line), :]
                    for step in range(1, dps):
                        origin = lax.rem(me_d - step + dps, dps)
                        part = fans_in[which][origin, fan_lines(which, 0, line), :]
                        total = total + part.astype(fp32)
                    outs[which][fan_lines(which, 0, line), :] = total
                    return carry

                lax.fori_loop(0, tall[which] // 16, body, 0)
                for step in range(1, dps):
                    fans[which].going(step).wait_send()

        def chunk_of(step):
            return lax.rem(me_s + step, seqs)

        for step in range(seqs):
            for copy in loading(chunk_of(step)):
                copy.start()
        for work in works:
            work.begin()
        barrier = pltpu.get_barrier_semaphore()
        targets = [{"seq": lax.rem(me_s + step, seqs)} for step in range(1, seqs)]
        targets += [{"dp": lax.rem(me_d + step, dps)} for step in range(1, dps)]
        if pairs == 2:
            targets += [
                {"seq": lax.rem(me_s + step, seqs), "dp": flip(me_d, 1)} for step in range(1, seqs)
            ]
        for target in targets:
            pl.semaphore_signal(
                barrier, inc=1, device_id=target, device_id_type=pl.DeviceIdType.MESH
            )
        pl.semaphore_wait(barrier, len(targets))

        def behind(way):
            return me_d > 0 if way == 0 else me_d < dps - 1

        def target_of(way, hop):
            sign = 1 if way == 0 else -1
            return jnp.clip(me_d + sign * hop, 0, dps - 1)

        def has_target(way, hop):
            return me_d < dps - hop if way == 0 else me_d >= hop

        def line_copy(way, part, hop, chunk):
            return remote(
                outgoing.at[way, hop % 2, chunk, :, halves[part]],
                incoming.at[way, hop - 1, chunk, :, halves[part]],
                line_send.at[2 * part + way, hop - 1, chunk],
                line_recv.at[2 * part + way, hop - 1, chunk],
                {"dp": target_of(way, 1)},
            )

        def combine(store, terms):
            def body(step, carry):
                lines = pl.ds(pl.multiple_of(step * 16, 16), 16)
                total = terms[0](lines)
                for term in terms[1:]:
                    total = total + term(lines)
                store(lines, total)
                return carry

            lax.fori_loop(0, rows // 16, body, 0)

        def own_term(part, chunk, block):
            return lambda lines: held[chunk, block, lines, halves[part]]

        def far_term(part, way, hop, chunk):
            return lambda lines: incoming[way, hop - 1, chunk, lines, halves[part]].astype(fp32)

        def each_line(test, action):
            for part in range(2):
                for way in range(2):
                    condition = test(way)
                    if part == 1:
                        condition = condition & is_full
                    pl.when(condition)(lambda way=way, part=part: action(way, part))

        def line_round(hop, first):
            def body(step, carry):
                chunk = chunk_of(step)
                if first:
                    for copy in loading(chunk):
                        copy.wait()
                if hop + 2 < dps:
                    each_line(
                        lambda way: has_target(way, hop + 2),
                        lambda way, part: line_copy(way, part, hop + 2, chunk).wait_send(),
                    )

                def send(way, part, far):
                    def keep(lines, total):
                        outgoing[way, hop % 2, chunk, lines, halves[part]] = total.astype(half)

                    terms = [own_term(part, chunk, target_of(way, hop))]
                    if far:
                        line_copy(way, part, hop + 1, chunk).wait_recv()
                        terms.append(far_term(part, way, hop + 1, chunk))
                    combine(keep, terms)
                    line_copy(way, part, hop, chunk).start()

                if hop == dps - 1:
                    each_line(
                        lambda way: has_target(way, hop), lambda way, part: send(way, part, False)
                    )
                else:
                    each_line(
                        lambda way: has_target(way, hop) & behind(way),
                        lambda way, part: send(way, part, True),
                    )
                    each_line(
                        lambda way: has_target(way, hop) & jnp.logical_not(behind(way)),
                        lambda way, part: send(way, part, False),
                    )
                return carry

            lax.fori_loop(0, seqs, body, 0)

        def line_total(step, carry):
            chunk = chunk_of(step)
            if dps == 1:
                for copy in loading(chunk):
                    copy.wait()
            for part in range(2):
                for ups, downs in ((True, True), (True, False), (False, True), (False, False)):
                    condition = behind(0) if ups else jnp.logical_not(behind(0))
                    condition &= behind(1) if downs else jnp.logical_not(behind(1))
                    if part == 1:
                        condition &= is_full

                    @pl.when(condition)
                    def _():
                        def keep(lines, total):
                            totals[chunk, lines, halves[part]] = total.astype(half)

                        terms = [own_term(part, chunk, me_d)]
                        for way in [way for way, far in ((0, ups), (1, downs)) if far and dps > 1]:
                            line_copy(way, part, 1, chunk).wait_recv()
                            terms.append(far_term(part, way, 1, chunk))
                        combine(keep, terms)

            @pl.when(step > 0)
            def _():
                move.start(step)

            @pl.when(step == 0)
            def _():
                move.start_own()

            return carry

        depth = len(plane)
        first_total = max(dps - 2, 0)
        for turn in range(max(depth, dps - 1)):
            if turn < dps - 1:
                line_round(dps - 1 - turn, turn == 0)
            if turn == 0:
                for work in works[1:]:
                    for stage in range(depth):
                        work.stage(stage)
                    work.finish()
                fan_send()
                mlp_moves[0].start_own()
                for mlp_move in mlp_moves:
                    for step in range(0 if mlp_move.across else 1, seqs):
                        mlp_move.start(step)
            if turn == first_total:
                lax.fori_loop(0, seqs, line_total, 0)
            if turn < depth:
                works[0].stage(turn)
        works[0].finish()
        fan_total()

        def last_round(step, carry):
            for each in [move, *mlp_moves]:
                each.wait_arrived(step)
                each.wait_sent(step)
            return carry

        lax.fori_loop(1, seqs, last_round, 0)
        move.wait_own()
        mlp_moves[0].wait_own()
        if pairs == 2:
            mlp_moves[1].wait_arrived(0)
            mlp_moves[1].wait_sent(0)

        def close_round(step, carry):
            for hop in range(1, min(dps, 3)):
                each_line(
                    lambda way: has_target(way, hop),
                    lambda way, part: line_copy(way, part, hop, step).wait_send(),
                )
            return carry

        lax.fori_loop(0, seqs, close_round, 0)
        for work in works:
            work.close()

    vmem, anywhere = pl.BlockSpec(memory_space=pltpu.VMEM), pl.BlockSpec(memory_space=pl.ANY)
    results = pl.pallas_call(
        kernel,
        out_shape=[
            shape(in_part.shape[1:], fp32),
            *(shape(backs[name], half) for name in names),
            *[shape((rows, seqs * pairs * cols), half)] * MLPS,
            shape((tall[1], mats.shape[2]), fp32),
            shape((tall[0], small.shape[2]), fp32),
        ],
        in_specs=[anywhere, anywhere, anywhere, vmem, anywhere, anywhere],
        out_specs=[vmem, *[anywhere] * (len(names) + MLPS), vmem, vmem],
        scratch_shapes=[
            *(pltpu.VMEM(value.shape[1:], fp32) for value, _ in shared),
            *(
                pltpu.VMEM((dps, lines, value.shape[2]), wire)
                for _ in range(2)
                for (value, wire), lines in zip(shared, tall)
            ),
            *(Fan.semaphores(dps) * 2),
            *itertools.chain.from_iterable(
                Scattering.scratch(bits, value, wire) for bits, value, wire in jobs
            ),
            pltpu.VMEM((seqs, dps, rows, chans.lanes), fp32),
            pltpu.VMEM((2, 2, seqs, rows, chans.lanes), half),
            pltpu.VMEM((2, links, seqs, rows, chans.lanes), half),
            pltpu.VMEM((seqs, rows, chans.lanes), half),
            pltpu.SemaphoreType.DMA((3, seqs)),
            pltpu.SemaphoreType.DMA((4, links, seqs)),
            pltpu.SemaphoreType.DMA((4, links, seqs)),
            *itertools.chain.from_iterable(
                Exchange.semaphores(pieces, seqs) for pieces in piece_counts
            ),
        ],
        compiler_params=pltpu.CompilerParams(
            collective_id=number, has_side_effects=True, vmem_limit_bytes=63 * 2**20
        ),
        name="closing",
    )(in_part, grad_in, grad_out, mlp, mats, small)
    backs = dict(zip(names, results[1:]))
    return results[0], backs, *results[1 + len(names) :]


SUBLANES = 8


def scan_kernel(forward, decay_ref, other_ref, out_ref):
    steps, width = decay_ref.shape
    tiles = steps // SUBLANES
    row = lax.broadcasted_iota(jnp.int32, (SUBLANES, width), 0)

    def tile(step, carry):
        at = step if forward else tiles - 1 - step
        lines = pl.ds(pl.multiple_of(at * SUBLANES, SUBLANES), SUBLANES)
        decay, other = decay_ref[lines, :], other_ref[lines, :]
        product, total = decay, other if forward else decay * other
        for reach in (1, 2, 4):
            shift = reach if forward else SUBLANES - reach
            inside = row >= reach if forward else row < SUBLANES - reach
            total = jnp.where(inside, product * pltpu.roll(total, shift, 0) + total, total)
            product = jnp.where(inside, product * pltpu.roll(product, shift, 0), product)
        total = product * carry + total
        if forward:
            out_ref[lines, :] = total
            last = total[SUBLANES - 1 :]
        else:
            after = jnp.where(row == SUBLANES - 1, carry, pltpu.roll(total, SUBLANES - 1, 0))
            out_ref[lines, :] = other + after
            last = total[:1]
        return jnp.broadcast_to(last, (SUBLANES, width))

    lax.fori_loop(0, tiles, tile, jnp.zeros((SUBLANES, width), fp32), unroll=4)


def time_scan(forward, decays, other):
    vmem = pl.BlockSpec(memory_space=pltpu.VMEM)
    return pl.pallas_call(
        functools.partial(scan_kernel, forward),
        out_shape=jax.ShapeDtypeStruct(decays.shape, fp32),
        in_specs=[vmem, vmem],
        out_specs=vmem,
        name="forward_scan" if forward else "backward_scan",
    )(decays, other)


def swap(value, axis, mask):
    return lax.ppermute(value, axis, [(i, i ^ mask) for i in range(lax.axis_size(axis))])


def far_masks(axis):
    mask, masks = pair_count(), []
    while mask < lax.axis_size(axis):
        masks.append(mask)
        mask *= 2
    return masks


def share_gather(value, axis):
    me = lax.axis_index(axis)
    for mask in far_masks(axis):
        sources, size, rows, width = value.shape
        high = (me // mask) % 2
        whole = jnp.zeros((sources, 2 * size, rows, width), value.dtype)
        whole = lax.dynamic_update_slice(whole, value, (0, high * size, 0, 0))
        value = lax.dynamic_update_slice(
            whole, swap(value, axis, mask), (0, (1 - high) * size, 0, 0)
        )
    return value


def share_scatter(value, axis):
    pairs = pair_count()
    sources, count, rows, width = value.shape
    groups = [list(range(low, count, pairs)) for low in range(pairs)]
    value = value.reshape(sources, count // pairs, pairs, rows, width)
    return lax.psum_scatter(value, axis, scatter_dimension=1, axis_index_groups=groups)


def rms_norm(values, gain_vec):
    return (
        values * lax.rsqrt(jnp.mean(values * values, axis=-1, keepdims=True) + norm_eps) * gain_vec
    )


def gate_terms(gate_rec, gate_inp, conv_val, rec_vals):
    recur_gate = jax.nn.sigmoid(gate_rec)
    admit_gate = jax.nn.sigmoid(gate_inp)
    log_decay = -gate_power * recur_gate * jax.nn.softplus(-rec_vals)
    decays = jnp.exp(log_decay)
    scaler = jnp.sqrt(jnp.maximum(-jnp.expm1(2.0 * log_decay), floor_square))
    return (decays, scaler * admit_gate * conv_val)


def contract_rows(left, right):
    return lax.dot_general(left, right, (((0,), (0,)), ((), ())), preferred_element_type=fp32)


def times_trans(left, right):
    return lax.dot_general(left, right, (((1,), (1,)), ((), ())), preferred_element_type=fp32)


def part_of_sum(left, right):
    return times_trans(left, right).astype(half)


def times(left, right):
    return jnp.dot(left, right, preferred_element_type=fp32)


def gelu_product(first, second):
    return jax.nn.gelu(first, approximate=True) * second


def on_device(
    tokens,
    valid_mask,
    teacher,
    norm_one,
    proj_gelu,
    proj_rec,
    conv_taps,
    conv_bias,
    gate_rec_w,
    gate_rec_b,
    gate_inp_w,
    gate_inp_b,
    rec_param,
    proj_out,
    norm_two,
    mlp_gate,
    mlp_up,
    mlp_down,
):
    seqs, dps = lax.axis_size("seq"), lax.axis_size("dp")
    everyone = seqs * dps
    me_seq = lax.axis_index("seq")
    local_len, model = tokens.shape[-2:]
    rec_width = proj_rec.shape[1]
    hidden_width = mlp_gate.shape[1]
    rows_w = proj_rec.shape[0]
    rows_c = gate_rec_w.shape[0]
    steps = seqs * local_len

    plane, cube, pairs = plane_bits(), cube_bits(), pair_count()

    chans = Channels(rec_width, seqs)
    width_r, span, span_blocks = chans.width, chans.span, chans.blocks
    base = chans.base(me_seq)
    cols = hidden_width // (pairs * seqs)

    mask_val = valid_mask.reshape(local_len).astype(fp32)
    own_count = jnp.sum(mask_val)
    count_high = jnp.floor(own_count / 128.0)
    count_pair = jnp.stack([count_high, own_count - 128.0 * count_high]).astype(half)

    def row_of(value):
        return jnp.pad(value, ((0, 0), (0, 2 * BW - value.shape[1])))

    block_rows = -(-rows_c // 16) * 16
    package = jnp.concatenate(
        [
            jnp.pad(
                jnp.concatenate([gate_rec_w, gate_inp_w], axis=1),
                ((0, block_rows - rows_c), (0, 0)),
            ),
            row_of(conv_taps),
            row_of(jnp.stack([conv_bias, gate_rec_b, gate_inp_b, rec_param])),
            row_of(jnp.stack([norm_one, norm_two])),
            row_of(count_pair[None, :]),
            jnp.zeros((5, 2 * BW), half),
        ],
        axis=0,
    )
    w_in, w_out, mlp_own, shared, tokens_all = opening(
        chans,
        {"rec": proj_rec, "gelu": proj_gelu, "out": proj_out.T},
        [mlp_gate, mlp_up, mlp_down.T],
        package,
        tokens.reshape(local_len, model),
        1,
    )
    shared = shared.reshape(everyone, *package.shape)
    w_in, w_out = w_in.reshape(model, span + width_r), w_out.reshape(model, width_r)
    w_mlp = share_gather(mlp_own, "dp").reshape(model, 3 * cols)
    w_two, w_down = w_mlp[:, : 2 * cols], w_mlp[:, 2 * cols :]
    vectors = shared[:, block_rows:].astype(fp32)
    channel_vecs = vectors[:, : CONV + 4, :rows_c].transpose(1, 0, 2).reshape(CONV + 4, rec_width)
    gains = vectors[:, CONV + 4 : CONV + 6, :rows_w].transpose(1, 0, 2).reshape(2, model)
    counts = jnp.sum(vectors[:, CONV + 6, :2], axis=0)
    valid_total = 128.0 * counts[0] + counts[1]

    span_vecs = lax.dynamic_slice(channel_vecs, (0, base), (CONV + 4, span))
    tap_vals, bias_vals = span_vecs[:CONV], span_vecs[CONV]
    rec_bias, inp_bias, rec_vals = (
        chans.owned(span_vecs[CONV + 1 + i], me_seq) for i in range(3)
    )
    mine = chans.mine(me_seq)
    touched = min(everyone, -(-(span - 1) // rows_c) + 1)
    from_device = jnp.minimum(base // rows_c, everyone - touched)
    near = lax.dynamic_slice(shared, (from_device, 0, 0), (touched, rows_c, 2 * BW))
    span_mats = lax.dynamic_slice(
        near.reshape(touched * rows_c, 2 * BW), (base - from_device * rows_c, 0), (span, 2 * BW)
    )

    def block_diagonal(value):
        rows = []
        for place in range(span_blocks):
            block = value[place * BW : (place + 1) * BW]
            rows.append(jnp.pad(block, ((0, 0), (place * BW, (span_blocks - 1 - place) * BW))))
        return chans.owned(jnp.concatenate(rows, axis=0), me_seq)

    w_gates = jnp.concatenate(
        [block_diagonal(span_mats[:, :BW]), block_diagonal(span_mats[:, BW:])], axis=1
    )
    gain_one, gain_two = gains[0], gains[1]

    flat_in = tokens.reshape(local_len, model).astype(fp32)
    tokens_all = tokens_all.reshape(steps, model).astype(fp32)
    normed_all = lax.optimization_barrier(rms_norm(tokens_all, gain_one).astype(half))
    pre = times(normed_all, w_in)
    rec_pre, gelu_pre = chans.rec_of(pre)
    padded = jnp.concatenate([jnp.zeros((CONV - 1, span), fp32), rec_pre], axis=0)
    conv_sum = bias_vals + jnp.zeros_like(rec_pre)
    for offset in range(CONV):
        conv_sum = conv_sum + tap_vals[offset] * padded[CONV - 1 - offset : CONV - 1 - offset + steps]
    conv_low = conv_sum.astype(half)
    conv_val = chans.owned(conv_low, me_seq).astype(fp32)
    gates = times(conv_low, w_gates)
    gate_rec = gates[:, :width_r] + rec_bias
    gate_inp = gates[:, width_r:] + inp_bias
    decays, drives = gate_terms(gate_rec, gate_inp, conv_val, rec_vals)
    states = time_scan(True, decays, drives)
    mixed_low = jnp.where(mine, gelu_product(gelu_pre, states), 0.0).astype(half)
    mixed_part = part_of_sum(mixed_low, w_out).reshape(seqs, local_len, model)
    middle = flat_in + scatter_sum(mixed_part, plane, 3)

    normed_two_low = rms_norm(middle, gain_two).astype(half)
    group = pairs * seqs
    tall = group * local_len
    normed_two_all = gather(normed_two_low, cube, 4).reshape(tall, model)
    pre_two = times(normed_two_all, w_two)
    gate_pre, up_pre = pre_two[:, :cols], pre_two[:, cols:]
    hidden_low = gelu_product(gate_pre, up_pre).astype(half)
    down_part = part_of_sum(hidden_low, w_down).reshape(group, local_len, model)
    result = middle + scatter_sum(down_part, cube, 5)
    differ = result - teacher.reshape(local_len, model).astype(fp32)
    own_loss = 0.5 * jnp.sum(mask_val[:, None] * differ * differ)
    token_total = local_len * everyone
    grad_result = mask_val[:, None] * (token_total / valid_total) * differ
    output = result.reshape(tokens.shape).astype(half)

    down_all = gather(grad_result.astype(half), cube, 6).reshape(tall, model)
    grad_down = contract_rows(down_all, hidden_low)
    grad_hidden = times(down_all, w_down)
    _, pull_mlp = jax.vjp(gelu_product, gate_pre, up_pre)
    two_low = jnp.concatenate(pull_mlp(grad_hidden), axis=1).astype(half)
    grad_two = contract_rows(normed_two_all, two_low)
    two_part = part_of_sum(two_low, w_two).reshape(group, local_len, model)

    grad_normed_two = scatter_sum(two_part, cube, 7)
    grad_normed_two, grad_two, grad_down = lax.optimization_barrier(
        (grad_normed_two, grad_two, grad_down)
    )
    grad_mlp = jnp.concatenate([grad_two, grad_down], axis=1).astype(half)
    sent_mlp = share_scatter(grad_mlp.reshape(seqs, dps, rows_w, 3 * cols), "dp")

    _, pull_norm_two = jax.vjp(rms_norm, middle, gain_two)
    grad_middle_norm, grad_norm_two = pull_norm_two(grad_normed_two)
    grad_middle = grad_result + grad_middle_norm

    middle_low = gather(grad_middle.astype(half), plane, 8).reshape(steps, model)
    grad_out = contract_rows(middle_low, mixed_low)
    grad_mixed = jnp.where(mine, times(middle_low, w_out), 0.0)
    _, pull_mix = jax.vjp(gelu_product, gelu_pre, states)
    grad_gelu_pre, grad_states = pull_mix(grad_mixed)
    adjoint = time_scan(False, decays, grad_states)
    prior_state = jnp.concatenate([jnp.zeros_like(states[:1]), states[:-1]], axis=0)
    _, pull_gates = jax.vjp(gate_terms, gate_rec, gate_inp, conv_val, rec_vals)
    grad_rec_gate, grad_inp_gate, grad_conv_direct, grad_rec_param = pull_gates(
        (adjoint * prior_state, adjoint)
    )
    gates_low = jnp.concatenate([grad_rec_gate, grad_inp_gate], axis=1).astype(half)
    grad_gate_bias = jnp.sum(gates_low.astype(fp32), axis=0)
    grad_gates = contract_rows(conv_low, gates_low)
    grad_conv = times_trans(gates_low, w_gates) + chans.widened(grad_conv_direct, me_seq)
    grad_conv_bias = jnp.sum(grad_conv, axis=0)
    ahead = jnp.concatenate([grad_conv, jnp.zeros((CONV - 1, span), fp32)], axis=0)
    tap_grads = []
    rec_back = jnp.zeros_like(grad_conv)
    for offset in range(CONV):
        window = padded[CONV - 1 - offset : CONV - 1 - offset + steps]
        tap_grads.append(jnp.sum(grad_conv * window, axis=0))
        rec_back = rec_back + tap_vals[offset] * ahead[offset : offset + steps]
    rec_low = rec_back.astype(half)
    in_low = jnp.concatenate(
        [rec_low[:, :BW], grad_gelu_pre.astype(half), rec_low[:, BW:]], axis=1
    )
    grad_in = contract_rows(normed_all, in_low)
    in_part = part_of_sum(in_low, w_in).reshape(seqs, local_len, model)
    grad_norm_one = jnp.sum(w_in.astype(fp32) * grad_in, axis=1) / gain_one

    def spread(value):
        return lax.dynamic_update_slice(
            jnp.zeros((value.shape[0], rec_width), fp32), value, (0, base)
        )

    def diagonal_blocks(value):
        wide = chans.widened(value, me_seq)
        block = lax.broadcasted_iota(jnp.int32, (span, BW), 0) // BW
        picked = wide[:, :BW]
        for i in range(1, span_blocks):
            picked = jnp.where(block == i, wide[:, i * BW : (i + 1) * BW], picked)
        return picked

    mats = jnp.concatenate(
        [diagonal_blocks(grad_gates[:, :width_r]), diagonal_blocks(grad_gates[:, width_r:])], axis=1
    )
    mats = lax.dynamic_update_slice(jnp.zeros((rec_width, 2 * BW), fp32), mats, (base, 0))
    mats = jnp.pad(
        mats.reshape(everyone, rows_c, 2 * BW), ((0, 0), (0, block_rows - rows_c), (0, 0))
    )

    def widen(value):
        return chans.widened(value[None, :], me_seq)

    lines = jnp.concatenate(
        [
            jnp.stack(tap_grads),
            grad_conv_bias[None, :],
            widen(grad_gate_bias[:width_r]),
            widen(grad_gate_bias[width_r:]),
            widen(grad_rec_param),
        ],
        axis=0,
    )
    lines = spread(lines).reshape(CONV + 4, everyone, rows_c).transpose(1, 0, 2)
    gain_lines = jnp.stack([grad_norm_one, grad_norm_two]).reshape(2, everyone, rows_w)
    gain_lines = gain_lines.transpose(1, 0, 2)

    def lane_pad(value):
        return jnp.pad(value, ((0, 0), (0, 0), (0, LANES - value.shape[2])))

    small = jnp.concatenate(
        [
            lane_pad(lines),
            lane_pad(gain_lines),
            jnp.full((everyone, 1, LANES), own_loss),
            jnp.zeros((everyone, 5, LANES), fp32),
        ],
        axis=1,
    )
    grad_normed, backs, out_gate, out_up, out_down, mats, small = closing(
        chans,
        in_part,
        grad_in.reshape(seqs, dps, rows_w, span + width_r),
        grad_out.reshape(seqs, dps, rows_w, width_r),
        sent_mlp,
        mats.astype(half).reshape(seqs, -1, 2 * BW),
        small.reshape(seqs, -1, LANES),
        2,
    )
    mean_loss = small[CONV + 6, 0] / (valid_total * model)

    _, pull_norm_one = jax.vjp(lambda values: rms_norm(values, gain_one), flat_in)
    grad_tokens = (grad_middle + pull_norm_one(grad_normed)[0]).reshape(tokens.shape).astype(half)

    block_of = lax.broadcasted_iota(jnp.int32, (1, rec_width), 1) // BW

    def layer_sum(at, blocks):
        has = functools.reduce(jnp.logical_or, [block_of == block for block in sorted(blocks)])
        return jnp.where(has, backs["rec"][at].astype(fp32), 0.0)

    out_gate, out_up = out_gate.astype(fp32), out_up.astype(fp32)
    out_down = out_down.T.astype(fp32)
    out_proj_out = backs["out"].T.astype(fp32)
    out_proj_gelu = backs["gelu"].astype(fp32)
    layers = [layer_sum(at, blocks) for at, blocks in enumerate(chans.taken)]
    out_proj_rec = functools.reduce(jnp.add, layers)

    return (
        output,
        mean_loss,
        grad_tokens,
        small[CONV + 4, :rows_w],
        out_proj_gelu,
        out_proj_rec,
        small[:CONV, :rows_c],
        small[CONV, :rows_c],
        mats[:rows_c, :BW],
        small[CONV + 1, :rows_c],
        mats[:rows_c, BW:],
        small[CONV + 2, :rows_c],
        small[CONV + 3, :rows_c],
        out_proj_out,
        small[CONV + 5, :rows_w],
        out_gate,
        out_up,
        out_down,
    )


def solution(mesh):
    both = ("seq", "dp")
    rows, cols, flat = P(both, None), P(None, both), P(both)
    acts = P("dp", "seq", None)
    in_specs = (
        acts,
        P("dp", "seq"),
        acts,
        flat,
        rows,
        rows,
        cols,
        flat,
        rows,
        flat,
        rows,
        flat,
        flat,
        cols,
        flat,
        rows,
        rows,
        cols,
    )
    out_specs = (
        acts,
        P(),
        acts,
        flat,
        rows,
        rows,
        cols,
        flat,
        rows,
        flat,
        rows,
        flat,
        flat,
        cols,
        flat,
        rows,
        rows,
        cols,
    )
    return jax.shard_map(
        on_device, mesh=mesh, in_specs=in_specs, out_specs=out_specs, check_vma=False
    )
```
